32 devices in a mesh: expert: 8 (over y, x, core), context: 2 (over z_hi), dp: 2 (over z_lo).
Axes of the slice: x: 2, y: 2, z: 4 (z_hi: 2, z_lo: 2; z = z_hi * 2 + z_lo), core: 2. Of those that a mesh axis runs over, the one named last changes fastest.
Arguments:
- tokens: bfloat16 [2, 3072, 1536], P('dp', ('expert', 'context')), may hold values from -6 to 6
- gain_attn: float32 [1536], replicated, may hold values from 0.5 to 1.5
- w_query: bfloat16 [1536, 1536], replicated, may hold values from -0.29882812 to 0.29882812
- w_key: bfloat16 [1536, 256], replicated, may hold values from -0.15625 to 0.15625
- w_value: bfloat16 [1536, 256], replicated, may hold values from -0.15625 to 0.15625
- w_out: bfloat16 [1536, 1536], replicated, may hold values from -0.71875 to 0.71875
- gain_moe: float32 [1536], replicated, may hold values from 0.5 to 1.5
- w_router: bfloat16 [1536, 8], replicated, may hold values from -0.076660156 to 0.076660156
- w_gate: bfloat16 [8, 1536, 768], P('expert'), may hold values from -0.15625 to 0.15625
- w_up: bfloat16 [8, 1536, 768], P('expert'), may hold values from -0.15625 to 0.15625
- w_down: bfloat16 [8, 768, 1536], P('expert'), may hold values from -0.4296875 to 0.4296875
- routes: int32 [2, 3072, 4], P('dp', ('expert', 'context')), may hold values from 0 to 7, all different within a row; in each aligned block of 192 rows (0 to 191, 192 to 383, ..., all dimensions but the last counted through in order) at most 192 rows name the same one
- positions: int32 [2, 3072], P('dp', ('expert', 'context')), may hold values from 0 to 3071, as said below
- cotangent: bfloat16 [2, 3072, 1536], P('dp', ('expert', 'context')), may hold values from -6 to 6
Outputs:
- output: bfloat16 [2, 3072, 1536], P('dp', ('expert', 'context'))
- input_grad: bfloat16 [2, 3072, 1536], P('dp', ('expert', 'context'))
- gain_attn_grad: float32 [1536], P(('expert', 'context', 'dp'))
- w_query_grad: float32 [1536, 1536], P(('expert', 'context', 'dp'))
- w_key_grad: float32 [1536, 256], P(('expert', 'context', 'dp'))
- w_value_grad: float32 [1536, 256], P(('expert', 'context', 'dp'))
- w_out_grad: float32 [1536, 1536], P(None, ('expert', 'context', 'dp'))
- gain_moe_grad: float32 [1536], P(('expert', 'context', 'dp'))
- w_router_grad: float32 [1536, 8], P(('expert', 'context', 'dp'))
- w_gate_grad: float32 [8, 1536, 768], P('expert', ('context', 'dp'))
- w_up_grad: float32 [8, 1536, 768], P('expert', ('context', 'dp'))
- w_down_grad: float32 [8, 768, 1536], P('expert', None, ('context', 'dp'))
The draws below stay inside these ranges and needn't reach their ends.
Inputs may be any that keep to these rules, and one draw needn't show every extreme that they name: Along expert then context, device j of a sequence holds 192 rows: 96 consecutive positions of block b, then 192/2 consecutive positions of block 2 K - 1 - b, with K = 16 and b a permutation of the devices; every position occurs once. `routes`: each row names 4 different experts; within the rows of one device no expert is named by more than 192 rows, a bound that some block reaches.
All inputs are finite; a program needn't handle non-finite values.
Results may differ from the reference program's by a relative error of at most 0.017.
Values may be sent and summed in bfloat16 or wider, within the bound.
No kernel may reach another device: no remote copies, remote signals or barrier semaphores. Data moves between devices by JAX's collectives and lax.ppermute only.
A program may use at most 192 MiB of HBM per device.

```python
import math
import jax
import jax.numpy as jnp
import numpy as np
from jax import lax

D = 1536
H = 12
KV = 2
HD = 128
FF = 768
TOP = 4
TOK_DEV = 192
EXPERTS = 8
SEQ = 3072
SEQS = 2
TOKENS = 6144
CAP = 192


def draw_positions(key, part):
    blocks = SEQ // TOK_DEV
    half_rows = TOK_DEV // 2
    seq_keys = jax.random.split(jax.random.fold_in(key, 7), SEQS)

    def one_sequence(seq_key):
        block_order = jax.random.permutation(seq_key, blocks).astype(jnp.int32)
        within = jnp.arange(TOK_DEV, dtype=jnp.int32)
        front_rows = block_order[:, None] * half_rows + within[None, :]
        back_rows = (2 * blocks - 1 - block_order[:, None]) * half_rows + within[None, :] - half_rows
        return jnp.where(within[None, :] < half_rows, front_rows, back_rows).reshape(SEQ)
    return jax.vmap(one_sequence)(seq_keys).astype(jnp.int32)


def shard_levels(key, extent, pieces, smallest, largest):
    factor_of, own = 1.0, jax.random.fold_in(key, 6)
    for position, blocks in pieces:
        steps = jnp.exp(jax.random.uniform(jax.random.fold_in(own, position), (blocks,), jnp.float32, smallest / len(pieces), largest / len(pieces)))
        factor_of = factor_of * jnp.repeat(steps, extent[position] // blocks).reshape([-1 if axis == position else 1 for axis in range(len(extent))])
    return factor_of


def assign_block(rng, own, number, rows, number_of, top, limit, lean):
    sequence = jax.random.permutation(rng, number_of)
    crowded, usual = shares(number_of, rows * top, limit, lean, True), shares(number_of, rows * top, limit, lean, False)
    places = jnp.arange(number_of)

    def named(tallies, turn):
        used = int((tallies > 0).sum())
        fixed = max(1, used // 4)
        moved = fixed + (places - fixed + turn * (used - fixed)) % max(1, number_of - fixed)
        return jnp.zeros((number_of,), jnp.int32).at[sequence[jnp.where(places < fixed, places, moved)]].set(jnp.asarray(tallies, jnp.int32))

    tallies = jnp.where(number % 4 == 0, named(crowded, number // 4), named(usual, number - number // 4 - 1))
    mixed = jax.random.permutation(jax.random.fold_in(own, 3), number_of)
    giver, sink = mixed[0:number_of // 2 * 2:2], mixed[1:number_of // 2 * 2:2]
    slack = jnp.minimum(tallies[giver] - 1, limit - tallies[sink]) // 2
    slack = jnp.where((giver == sequence[0]) | (sink == sequence[0]) | (tallies[sink] == 0), 0, jnp.maximum(slack, 0))
    moved = jax.random.randint(jax.random.fold_in(own, 4), (number_of // 2,), 0, 1 << 20) % (slack + 1)
    tallies = tallies.at[giver].add(-moved).at[sink].add(moved)
    items = jnp.searchsorted(jnp.cumsum(tallies), jnp.arange(rows * top), side="right").astype(jnp.int32)
    listing = items.reshape(top, rows).T
    listing = listing[jax.random.permutation(jax.random.fold_in(own, 1), rows)]
    turn = jax.random.randint(jax.random.fold_in(own, 2), (rows, 1), 0, top)
    return jnp.take_along_axis(listing, (jnp.arange(top)[None, :] + turn) % top, axis=1)


def shares(amount, total, limit, lean, full):
    loads = [(1 << 20) // math.isqrt(rank ** lean) + 1 for rank in range(1, amount + 1)]
    largest = limit if full else min(limit, max(-(-total // amount), total * loads[0] // sum(loads)))
    least = 1 if total - largest >= amount - 1 else 0
    holding, surplus = [largest] + [least] * (amount - 1), total - largest - least * (amount - 1)
    while surplus > 0:
        free = [i for i in range(1, amount) if holding[i] < largest] or [i for i in range(1, amount) if holding[i] < limit]
        mass, left = sum([loads[i] for i in free]), surplus
        for i in free:
            more = min(limit - holding[i], max(1, left * loads[i] // mass), surplus)
            holding[i] = holding[i] + more
            surplus = surplus - more
    return np.array(holding)


def normal_values(key, extent, width, limit, pieces=(), kind=jnp.bfloat16):
    entries = jax.random.normal(key, extent, jnp.float32) * width
    if len(pieces) > 0:
        entries = shard_levels(key, extent, pieces, -0.22, 0.18) * entries
    return jnp.clip(entries, min=-limit, max=limit).astype(kind)


def setup_inputs(seed: int = 0) -> dict:
    keys = jax.random.split(jax.random.key(seed), 15)
    tokens = normal_values(keys[0], (SEQS, SEQ, D), 1.0, 6.0, ((0, 2), (1, 16)))
    gain_attn = jnp.clip(1.0 + 0.1 * jax.random.normal(keys[1], (D,), jnp.float32), 0.5, 1.5)
    w_query = normal_values(keys[2], (D, H * HD), 0.051, 0.29882812)
    w_key = normal_values(keys[3], (D, KV * HD), D ** -0.5, 0.15625)
    w_value = normal_values(keys[4], (D, KV * HD), D ** -0.5, 0.15625)
    w_out = normal_values(keys[5], (H * HD, D), 0.12, 0.71875)
    gain_moe = jnp.clip(1.0 + 0.1 * jax.random.normal(keys[6], (D,), jnp.float32), 0.5, 1.5)
    w_router = normal_values(keys[7], (D, EXPERTS), 0.0128, 0.076660156)
    w_gate = normal_values(keys[8], (EXPERTS, D, FF), D ** -0.5, 0.15625, ((0, 8),))
    w_up = normal_values(keys[9], (EXPERTS, D, FF), D ** -0.5, 0.15625, ((0, 8),))
    w_down = normal_values(keys[10], (EXPERTS, FF, D), 0.072, 0.4296875, ((0, 8),))
    routes_keys = jax.random.split(jax.random.fold_in(keys[11], 1), SEQS * SEQ // TOK_DEV)
    routes_turns = jax.random.permutation(jax.random.fold_in(keys[11], 3), SEQS * SEQ // TOK_DEV)
    routes = jax.vmap(lambda own, number: assign_block(jax.random.fold_in(keys[11], 2), own, number, TOK_DEV, EXPERTS, TOP, CAP, 1))(routes_keys, routes_turns).reshape((SEQS, SEQ, TOP))
    positions = draw_positions(jax.random.fold_in(keys[14], 71), 0)
    cotangent = normal_values(keys[13], (SEQS, SEQ, D), 1.0, 6.0, ((0, 2), (1, 16)))
    return {"tokens": tokens, "gain_attn": gain_attn, "w_query": w_query, "w_key": w_key, "w_value": w_value, "w_out": w_out, "gain_moe": gain_moe, "w_router": w_router, "w_gate": w_gate, "w_up": w_up, "w_down": w_down, "routes": routes, "positions": positions, "cotangent": cotangent}


eps = 1e-06
rope_base = 1000000.0
negative = -1e+30
highest = lax.Precision.HIGHEST

@jax.custom_vjp
def low(v):
    return lax.optimization_barrier(v.astype(jnp.bfloat16)).astype(jnp.float32)

@jax.custom_vjp
def low_back(v):
    return v

def low_keep(v):
    return (low(v), None)

def low_pass(kept, grad):
    return (grad,)

def back_keep(v):
    return (v, None)

def back_low(kept, grad):
    return (low(grad),)
low.defvjp(low_keep, low_pass)
low_back.defvjp(back_keep, back_low)

def normalize(values, gain):
    scale_row = lax.rsqrt(lax.optimization_barrier(jnp.mean(values * values, axis=-1, keepdims=True)) + eps)
    return values * scale_row * gain

def rope_tables(places, dtype):
    freqs = 1.0 / rope_base ** (jnp.arange(0, HD, 2).astype(dtype) / HD)
    angles = places.astype(dtype)[:, None] * freqs[None, :]
    return (jnp.cos(angles), jnp.sin(angles))

def rotate(values, cosine, sine_table):
    half_width = values.shape[-1] // 2
    front_half = values[..., :half_width]
    back_half = values[..., half_width:]
    cos_rows = cosine[:, None, :]
    sin_rows = sine_table[:, None, :]
    return jnp.concatenate([front_half * cos_rows - back_half * sin_rows, back_half * cos_rows + front_half * sin_rows], axis=-1)

def attend_sequence(inputs):
    queries, key_rows, value_rows, places = inputs
    block_size = math.gcd(SEQ, 512)
    groups = H // KV
    query_blocks = queries.reshape(SEQ // block_size, block_size, KV, groups, HD)
    place_blocks = places.reshape(SEQ // block_size, block_size)

    def one_block(block_pair):
        query_block, place_block = block_pair
        scores = jnp.einsum('bkgd,skd->kgbs', query_block, key_rows, precision=highest) / math.sqrt(HD)
        scores = low_back(scores)
        visible = place_block[:, None] >= places[None, :]
        scores = jnp.where(visible, scores, negative)
        weights = jax.nn.softmax(scores, axis=-1)
        mixed_rows = jnp.einsum('kgbs,skd->bkgd', weights, value_rows, precision=highest)
        return mixed_rows.reshape(block_size, H * HD)
    outputs = lax.map(jax.checkpoint(one_block), (query_blocks, place_blocks))
    return outputs.reshape(SEQ, H * HD)

def reference(tokens, gain_attn, w_query, w_key, w_value, w_out, gain_moe, w_router, w_gate, w_up, w_down, routes, positions, cotangent):
    route_flat = routes.reshape(TOKENS, TOP)
    place_flat = positions.reshape(TOKENS)

    def forward(x_in, gain_one, wq_in, wk_in, wv_in, wo_in, gain_two, wr_in, wg_in, wu_in, wd_in):
        dtype = x_in.dtype
        cosine, sine_table = rope_tables(place_flat, dtype)
        flat_tokens = x_in.reshape(TOKENS, D)
        xn_one = low(normalize(flat_tokens, gain_one))
        query_raw = low_back(jnp.dot(xn_one, wq_in, precision=highest)).reshape(TOKENS, H, HD)
        key_raw = low_back(jnp.dot(xn_one, wk_in, precision=highest)).reshape(TOKENS, KV, HD)
        value_rows = low_back(low(jnp.dot(xn_one, wv_in, precision=highest))).reshape(TOKENS, KV, HD)
        query_rot = low(rotate(query_raw, cosine, sine_table))
        key_rot = low(rotate(key_raw, cosine, sine_table))
        attended = lax.map(attend_sequence, (query_rot.reshape(SEQS, SEQ, H, HD), key_rot.reshape(SEQS, SEQ, KV, HD), value_rows.reshape(SEQS, SEQ, KV, HD), positions))
        attended = low_back(low(attended.reshape(TOKENS, H * HD)))
        branch = low_back(jnp.dot(attended, wo_in, precision=highest))
        hidden_state = flat_tokens + branch
        xn_two = low(normalize(hidden_state, gain_two))
        logits = low_back(jnp.dot(xn_two, wr_in, precision=highest))
        pick_float = (route_flat[:, :, None] == jnp.arange(EXPERTS, dtype=jnp.int32)[None, None, :]).astype(dtype)
        selected = lax.optimization_barrier(jnp.sum(pick_float * logits[:, None, :], axis=-1))
        gate_share = jax.nn.softmax(selected, axis=-1)
        route_share = lax.optimization_barrier(jnp.sum(gate_share[:, :, None] * pick_float, axis=1))

        def expert_step(running, inputs):
            gate_w, up_w, down_w, share_col = inputs
            rows_in = low_back(xn_two)
            gate_pre = low_back(jnp.dot(rows_in, gate_w, precision=highest))
            up_pre = low_back(jnp.dot(rows_in, up_w, precision=highest))
            hidden = low(jax.nn.silu(gate_pre) * up_pre)
            result = low_back(low(jnp.dot(hidden, down_w, precision=highest)))
            return (running + share_col[:, None] * result, None)
        mixture, _ = lax.scan(jax.checkpoint(expert_step), jnp.zeros((TOKENS, D), dtype), (wg_in, wu_in, wd_in, route_share.T))
        output = hidden_state + mixture
        return output.reshape(SEQS, SEQ, D)
    primals = (tokens.astype(jnp.float32), gain_attn.astype(jnp.float32), w_query.astype(jnp.float32), w_key.astype(jnp.float32), w_value.astype(jnp.float32), w_out.astype(jnp.float32), gain_moe.astype(jnp.float32), w_router.astype(jnp.float32), w_gate.astype(jnp.float32), w_up.astype(jnp.float32), w_down.astype(jnp.float32))
    output, pullback = jax.vjp(forward, *primals)
    grads = pullback(cotangent.astype(output.dtype))
    return (output.astype(jnp.bfloat16), grads[0].astype(jnp.bfloat16), grads[1], grads[2], grads[3], grads[4], grads[5], grads[6], grads[7], grads[8], grads[9], grads[10])
```

```python
import functools
import math

import jax
import jax.numpy as jnp
from jax import lax
from jax.experimental import pallas as pl
from jax.experimental.pallas import tpu as pltpu
from jax.sharding import PartitionSpec as P

H = 12
KV = 2
HD = 128
TOP = 4

eps = 1e-06
rope_base = 1000000.0
negative = -1e30
LANES = 128
PAD_ROWS = 16
VMEM_LIMIT = 60 * 1024 * 1024
bf16 = jnp.bfloat16
f32 = jnp.float32
LOG2E = 1.4426950408889634


def dot(a, b):
    return lax.dot_general(a, b, (((1,), (0,)), ((), ())), preferred_element_type=f32)


def dot_nt(a, b):
    return lax.dot_general(a, b, (((1,), (1,)), ((), ())), preferred_element_type=f32)


def dot_tn(a, b):
    return lax.dot_general(a, b, (((0,), (0,)), ((), ())), preferred_element_type=f32)


def params(semantics=1):
    return pltpu.CompilerParams(
        dimension_semantics=("arbitrary",) * semantics, vmem_limit_bytes=VMEM_LIMIT
    )


def cost(flops, moved, exps=0):
    return pl.CostEstimate(flops=int(flops), bytes_accessed=int(moved), transcendentals=int(exps))


def turn(values, cos, sin):
    return values * cos + pltpu.roll(values, HD // 2, 1) * sin


def norm_scale(values):
    return lax.rsqrt(jnp.mean(values * values, axis=-1, keepdims=True) + eps)


def rope_tables(places):
    freqs = 1.0 / rope_base ** (jnp.arange(0, HD, 2).astype(f32) / HD)
    angles = places.astype(f32)[:, None] * freqs[None, :]
    cosine, sine_table = jnp.cos(angles), jnp.sin(angles)
    return (
        jnp.concatenate([cosine, cosine], axis=1),
        jnp.concatenate([-sine_table, sine_table], axis=1),
    )


def fixed(shape):
    zeros = (0,) * len(shape)
    return pl.BlockSpec(shape, lambda *_: zeros, pipeline_mode=pl.Buffered(1))


def front_kernel(
    meta_ref, x_ref, gain_ref, wk_ref, wv_ref, cos_ref, sin_ref, xn_ref, packed_ref
):
    core = meta_ref[0]
    rows = x_ref.shape[0]
    values = x_ref[...].astype(f32)
    normed = (values * norm_scale(values) * gain_ref[...]).astype(bf16)
    xn_ref[...] = normed
    keys = dot(normed, wk_ref[...])
    vals = dot(normed, wv_ref[...]).astype(bf16)
    edge = lax.broadcasted_iota(jnp.int32, (PAD_ROWS, 2 * HD), 0) < PAD_ROWS // 2
    tail = jnp.where(edge, meta_ref[1].astype(f32), meta_ref[2].astype(f32)).astype(bf16)
    for head in range(KV):
        slot = jnp.where(core == head, 0, 1)
        span = slice(head * HD, (head + 1) * HD)
        turned = turn(keys[:, span], cos_ref[...], sin_ref[...]).astype(bf16)
        packed_ref[slot, :rows, :HD] = turned
        packed_ref[slot, :rows, HD:] = vals[:, span]
        packed_ref[slot, rows:, :] = tail


def front(meta, x, gain, wk, wv, cos, sin):
    rows, width = x.shape
    return pl.pallas_call(
        front_kernel,
        grid_spec=pltpu.PrefetchScalarGridSpec(
            num_scalar_prefetch=1,
            grid=(1,),
            in_specs=[fixed(a.shape) for a in (x, gain, wk, wv, cos, sin)],
            out_specs=[fixed((rows, width)), fixed((2, rows + PAD_ROWS, 2 * HD))],
        ),
        out_shape=[
            jax.ShapeDtypeStruct((rows, width), bf16),
            jax.ShapeDtypeStruct((2, rows + PAD_ROWS, 2 * HD), bf16),
        ],
        compiler_params=params(),
        cost_estimate=cost(4 * rows * width * KV * HD, 8 * rows * width),
        name="front",
    )(meta, x, gain, wk, wv, cos, sin)


def query_kernel(x_ref, w_ref, cos_ref, sin_ref, out_ref):
    raw = dot(x_ref[...], w_ref[...])
    for head in range(raw.shape[1] // HD):
        span = slice(head * HD, (head + 1) * HD)
        out_ref[:, span] = turn(raw[:, span], cos_ref[...], sin_ref[...]).astype(bf16)


def make_query(x, w, cos, sin):
    rows, width = x.shape
    wide = w.shape[1]
    tile = 4 * HD
    return pl.pallas_call(
        query_kernel,
        grid=(wide // tile,),
        in_specs=[
            fixed((rows, width)),
            pl.BlockSpec((width, tile), lambda i: (0, i)),
            fixed((rows, HD)),
            fixed((rows, HD)),
        ],
        out_specs=pl.BlockSpec((rows, tile), lambda i: (0, i)),
        out_shape=jax.ShapeDtypeStruct((rows, wide), bf16),
        compiler_params=params(),
        cost_estimate=cost(2 * rows * width * wide, 2 * width * wide),
        name="make_query",
    )(x, w, cos, sin)


def join_kernel(meta_ref, att_ref, w_ref, x_ref, gain_ref, hid_ref, xn_ref, keep_ref, send_ref):
    core = meta_ref[0]
    step = pl.program_id(0)
    tile = w_ref.shape[1]
    width = hid_ref.shape[1]
    span = pl.ds(pl.multiple_of(step * tile, LANES), tile)
    hid_ref[:, span] = x_ref[:, span].astype(f32) + dot(att_ref[...], w_ref[...])

    @pl.when(step == pl.num_programs(0) - 1)
    def _():
        hidden = hid_ref[...]
        xn_ref[...] = (hidden * norm_scale(hidden) * gain_ref[...]).astype(bf16)
        half = width // 2
        keep_ref[...] = xn_ref[:, pl.ds(pl.multiple_of(core * half, LANES), half)]
        send_ref[...] = xn_ref[:, pl.ds(pl.multiple_of((1 - core) * half, LANES), half)]


def join(meta, att, w, x, gain):
    rows, width = x.shape
    inner = att.shape[1]
    tile = width // 3
    return pl.pallas_call(
        join_kernel,
        grid_spec=pltpu.PrefetchScalarGridSpec(
            num_scalar_prefetch=1,
            grid=(width // tile,),
            in_specs=[
                fixed((rows, inner)),
                pl.BlockSpec((inner, tile), lambda i, m: (0, i)),
                fixed((rows, width)),
                fixed((1, width)),
            ],
            out_specs=[
                fixed((rows, width)),
                fixed((rows, width)),
                fixed((rows, width // 2)),
                fixed((rows, width // 2)),
            ],
        ),
        out_shape=[
            jax.ShapeDtypeStruct((rows, width), f32),
            jax.ShapeDtypeStruct((rows, width), bf16),
            jax.ShapeDtypeStruct((rows, width // 2), bf16),
            jax.ShapeDtypeStruct((rows, width // 2), bf16),
        ],
        compiler_params=params(),
        cost_estimate=cost(2 * rows * width * inner, 2 * width * inner),
        name="join",
    )(meta, att, w, x, gain)


def middle_kernel(
    meta_ref,
    own_ref,
    other_ref,
    hid_ref,
    xn_ref,
    gain_ref,
    dy_ref,
    wr_ref,
    w_ref,
    dstate_ref,
    dlow_ref,
    dlog_ref,
    dgain_ref,
    datt_ref,
    dx_ref,
):
    core = meta_ref[0]
    step = pl.program_id(0)
    width = hid_ref.shape[1]
    half = width // 2

    @pl.when(step == 0)
    def _():
        dx_ref[:, pl.ds(pl.multiple_of(core * half, LANES), half)] = own_ref[:, :half].astype(f32)
        dx_ref[:, pl.ds(pl.multiple_of((1 - core) * half, LANES), half)] = other_ref[
            :, :half
        ].astype(f32)
        d_gate = own_ref[:, half:].astype(f32) + other_ref[:, half:].astype(f32)
        chosen = dy_ref[:, width:].astype(f32) > 0.5
        logits = dot(xn_ref[...], wr_ref[...])
        top = jnp.max(jnp.where(chosen, logits, negative), axis=-1, keepdims=True)
        shares = jnp.where(chosen, jnp.exp(logits - top), 0.0)
        gate = shares / jnp.sum(shares, axis=-1, keepdims=True)
        inner_sum = jnp.sum(gate * d_gate, axis=-1, keepdims=True)
        d_logits = (gate * (d_gate - inner_sum)).astype(bf16)
        dlog_ref[...] = d_logits
        d_xn = dx_ref[...] + dot_nt(d_logits, wr_ref[...])
        hidden = hid_ref[...]
        scale_row = norm_scale(hidden)
        normed = hidden * scale_row
        dgain_ref[...] = jnp.broadcast_to(
            jnp.sum(d_xn * normed, axis=0, keepdims=True), dgain_ref.shape
        )
        scaled = d_xn * gain_ref[...]
        inner_mean = jnp.mean(scaled * normed, axis=-1, keepdims=True)
        d_state = dy_ref[:, :width].astype(f32) + scale_row * (scaled - normed * inner_mean)
        dstate_ref[...] = d_state
        dlow_ref[...] = d_state.astype(bf16)

    datt_ref[...] = dot_nt(dlow_ref[...], w_ref[...]).astype(bf16)


def middle(meta, own, other, hidden, xn, gain, dy, wr, w):
    rows, width = hidden.shape
    inner = w.shape[0]
    tile = inner // 3
    return pl.pallas_call(
        middle_kernel,
        grid_spec=pltpu.PrefetchScalarGridSpec(
            num_scalar_prefetch=1,
            grid=(inner // tile,),
            in_specs=[fixed(a.shape) for a in (own, other, hidden, xn, gain, dy, wr)]
            + [pl.BlockSpec((tile, width), lambda i, m: (i, 0))],
            out_specs=[
                fixed((rows, width)),
                fixed((rows, width)),
                fixed((rows, LANES)),
                fixed((8, width)),
                pl.BlockSpec((rows, tile), lambda i, m: (0, i)),
            ],
            scratch_shapes=[pltpu.VMEM((rows, width), f32)],
        ),
        out_shape=[
            jax.ShapeDtypeStruct((rows, width), f32),
            jax.ShapeDtypeStruct((rows, width), bf16),
            jax.ShapeDtypeStruct((rows, LANES), bf16),
            jax.ShapeDtypeStruct((8, width), f32),
            jax.ShapeDtypeStruct((rows, inner), bf16),
        ],
        compiler_params=params(),
        cost_estimate=cost(2 * rows * width * inner, 2 * width * inner),
        name="middle",
    )(meta, own, other, hidden, xn, gain, dy, wr, w)


def times_kernel(x_ref, w_ref, out_ref):
    out_ref[...] = dot_nt(x_ref[...], w_ref[...])


def times_transposed(x, w):
    rows, inner = x.shape
    width = w.shape[0]
    tile = width // 3
    return pl.pallas_call(
        times_kernel,
        grid=(width // tile,),
        in_specs=[fixed((rows, inner)), pl.BlockSpec((tile, inner), lambda i: (i, 0))],
        out_specs=pl.BlockSpec((rows, tile), lambda i: (0, i)),
        out_shape=jax.ShapeDtypeStruct((rows, width), f32),
        compiler_params=params(),
        cost_estimate=cost(2 * rows * width * inner, 2 * width * inner),
        name="times_transposed",
    )(x, w)


def back_kernel(
    meta_ref,
    own_ref,
    other_ref,
    dxq_ref,
    x_ref,
    gain_ref,
    dstate_ref,
    wk_ref,
    wv_ref,
    cos_ref,
    sin_ref,
    din_ref,
    dkv_ref,
    dgain_ref,
    pair_ref,
):
    core = meta_ref[0]
    pair_ref[core] = own_ref[...].astype(f32)
    pair_ref[1 - core] = other_ref[...].astype(f32)
    wide = KV * HD
    for head in range(KV):
        turned = turn(pair_ref[head, :, :HD], cos_ref[...], -sin_ref[...])
        dkv_ref[:, head * HD : (head + 1) * HD] = turned.astype(bf16)
        dkv_ref[:, wide + head * HD : wide + (head + 1) * HD] = pair_ref[head, :, HD:].astype(bf16)
    d_xn = (
        dxq_ref[...]
        + dot_nt(dkv_ref[:, :wide], wk_ref[...])
        + dot_nt(dkv_ref[:, wide:], wv_ref[...])
    )
    values = x_ref[...].astype(f32)
    scale_row = norm_scale(values)
    normed = values * scale_row
    dgain_ref[...] = jnp.broadcast_to(
        jnp.sum(d_xn * normed, axis=0, keepdims=True), dgain_ref.shape
    )
    scaled = d_xn * gain_ref[...]
    inner_mean = jnp.mean(scaled * normed, axis=-1, keepdims=True)
    din_ref[...] = (dstate_ref[...] + scale_row * (scaled - normed * inner_mean)).astype(bf16)


def back(meta, own, other, dxq, x, gain, dstate, wk, wv, cos, sin):
    rows, width = x.shape
    return pl.pallas_call(
        back_kernel,
        grid_spec=pltpu.PrefetchScalarGridSpec(
            num_scalar_prefetch=1,
            grid=(1,),
            in_specs=[
                fixed(a.shape) for a in (own, other, dxq, x, gain, dstate, wk, wv, cos, sin)
            ],
            out_specs=[
                fixed((rows, width)),
                fixed((rows, 2 * KV * HD)),
                fixed((8, width)),
            ],
            scratch_shapes=[pltpu.VMEM((KV, rows, 2 * HD), f32)],
        ),
        out_shape=[
            jax.ShapeDtypeStruct((rows, width), bf16),
            jax.ShapeDtypeStruct((rows, 2 * KV * HD), bf16),
            jax.ShapeDtypeStruct((8, width), f32),
        ],
        compiler_params=params(),
        cost_estimate=cost(4 * rows * width * KV * HD, 16 * rows * width),
        name="back",
    )(meta, own, other, dxq, x, gain, dstate, wk, wv, cos, sin)


def dense_kernel(extra, meta_ref, left_ref, right_ref, *refs):
    if extra:
        xn_ref, dlog_ref, gains_ref, keep_ref, send_ref, whole_ref, more_ref = refs
    else:
        keep_ref, send_ref, whole_ref = refs
    core = meta_ref[0]
    place = meta_ref[1]
    piece = keep_ref.shape[4]
    wide = right_ref.shape[1]
    half = wide // 2
    whole_ref[...] = dot_tn(left_ref[...], right_ref[...])
    here = pl.ds(pl.multiple_of(core * half, LANES), half)
    there = pl.ds(pl.multiple_of((1 - core) * half, LANES), half)
    if extra:
        router = dot_tn(xn_ref[...], dlog_ref[...])
        tall = jnp.broadcast_to(gains_ref[0, 0:1, :], (LANES, router.shape[0])).T
        second = jnp.broadcast_to(gains_ref[1, 0:1, :], (LANES, router.shape[0])).T
        lane = lax.broadcasted_iota(jnp.int32, router.shape, 1)
        more_ref[...] = jnp.where(
            lane == LANES - 2, tall, jnp.where(lane == LANES - 1, second, router)
        )
    for t in range(2):
        for c in range(2):
            for d in range(2):
                at = ((core ^ t) * 4 + (place ^ (c * 2 + d))) * piece
                rows = pl.ds(pl.multiple_of(at, 16), piece)
                keep_ref[0, t, c, d, :, :half] = whole_ref[rows, here].astype(bf16)
                send_ref[0, 1 - t, c, d, :, :half] = whole_ref[rows, there].astype(bf16)
                if extra:
                    keep_ref[0, t, c, d, :, half:] = more_ref[rows, :].astype(bf16)
                    send_ref[0, 1 - t, c, d, :, half:] = more_ref[rows, :].astype(bf16)


def dense_grad(plane, meta, left, right, extra=()):
    rows, width = left.shape
    wide = right.shape[1]
    part = width // plane.chips
    piece = part // 8
    held = wide // 2 + (LANES if extra else 0)
    shape = (plane.chips, 2, 2, 2, piece, held)
    columns = pl.BlockSpec((rows, part), lambda g, m: (0, m[2 + g]))
    more = [
        columns,
        fixed((rows, LANES)),
        pl.BlockSpec((2, 8, part), lambda g, m: (0, 0, m[2 + g])),
    ]
    return pl.pallas_call(
        functools.partial(dense_kernel, bool(extra)),
        grid_spec=pltpu.PrefetchScalarGridSpec(
            num_scalar_prefetch=1,
            grid=(plane.chips,),
            in_specs=[columns, fixed((rows, wide))] + (more if extra else []),
            out_specs=[
                pl.BlockSpec((1,) + shape[1:], lambda g, m: (g, 0, 0, 0, 0, 0)),
                pl.BlockSpec((1,) + shape[1:], lambda g, m: (plane.swapped(g), 0, 0, 0, 0, 0)),
            ],
            scratch_shapes=[pltpu.VMEM((part, wide), f32)]
            + ([pltpu.VMEM((part, LANES), f32)] if extra else []),
        ),
        out_shape=[jax.ShapeDtypeStruct(shape, bf16)] * 2,
        compiler_params=params(),
        cost_estimate=cost(2 * rows * width * wide, 2 * width * wide),
        name="dense_grad",
    )(meta, left, right, *extra)


class Plane:
    def __init__(self, size):
        self.size = size
        bits = size.bit_length() - 1
        self.steps = bits - 1
        self.shift = self.steps // 2 if self.steps % 2 == 0 else 0
        first = list(range(1, bits))
        self.order = (first, first[self.shift :] + first[: self.shift])
        self.sibling = [(i, i ^ 1) for i in range(size)]
        self.mixed = [
            [(i, i ^ (1 << self.order[i & 1][k])) for i in range(size)] for k in range(self.steps)
        ]
        self.chips = size // 2

    def chip_offset(self, core, group):
        return sum(((group >> k) & 1) << self.order[core][k] for k in range(self.steps))

    def swapped(self, group):
        if not self.shift:
            return group
        low_mask = (1 << self.shift) - 1
        return ((group & low_mask) << (self.steps - self.shift)) | (group >> self.shift)


def gather_plane(plane, keep, send):
    held = jnp.stack([keep, lax.ppermute(send, "expert", plane.sibling)])[None]
    for k in range(plane.steps):
        held = jnp.concatenate([held, lax.ppermute(held, "expert", plane.mixed[k])])
    return held, lax.ppermute(held, "expert", plane.sibling)


def add_low(a, b):
    return (a.astype(f32) + b.astype(f32)).astype(bf16)


def reduce_plane(plane, keep, send):
    held = add_low(keep, lax.ppermute(send, "expert", plane.sibling))
    for k in reversed(range(plane.steps)):
        half = held.shape[0] // 2
        held = add_low(held[:half], lax.ppermute(held[half:], "expert", plane.mixed[k]))
    held = held[0]
    return held[0], lax.ppermute(held[1], "expert", plane.sibling)


def place_keys(bases_ref, at, buf_ref, keys_ref, vals_ref, half, blocks):
    for block in range(blocks):
        for part in range(2):
            rows = pl.ds(pl.multiple_of(bases_ref[at + block * 2 + part] * half, 16), half)
            keys_ref[rows, :] = buf_ref[block, part * half : (part + 1) * half, :HD]
            vals_ref[rows, :] = buf_ref[block, part * half : (part + 1) * half, HD:]


def stack_heads(ref, part, half, groups):
    return jnp.concatenate(
        [
            ref[part * half : (part + 1) * half, g * HD : (g + 1) * HD]
            for g in range(groups)
        ],
        axis=0,
    )


def attend_kernel(
    meta_ref, q_ref, mine_ref, theirs_ref, offs_ref, att_ref, attt_ref, lse_ref, keys_ref, vals_ref
):
    blocks = mine_ref.shape[0]
    half = q_ref.shape[0] // 2
    groups = q_ref.shape[1] // HD
    width = groups * half
    chunk = 4 * half
    factor = LOG2E / math.sqrt(HD)
    step = pl.program_id(0)

    @pl.when(step == 0)
    def _():
        place_keys(meta_ref, 4, mine_ref, keys_ref, vals_ref, half, blocks)

    @pl.when(step == 1)
    def _():
        place_keys(meta_ref, 4 + 2 * blocks, theirs_ref, keys_ref, vals_ref, half, blocks)

    for part in range(2):
        base = meta_ref[1 + part]
        query = stack_heads(q_ref, part, half, groups)

        def step_chunk(j, carry, masked):
            top, total, acc = carry
            rows = pl.ds(pl.multiple_of(j * chunk, 16), chunk)
            scores = dot_nt(keys_ref[rows, :], query)
            if masked:
                row = lax.broadcasted_iota(jnp.int32, scores.shape, 0) + (j * chunk - base * half)
                seen = row <= offs_ref[0:1, :]
                scores = jnp.where(seen, scores, negative)
            new_top = jnp.maximum(top, jnp.max(scores, axis=0, keepdims=True))
            weights = jnp.exp2((scores - new_top) * factor)
            shrink = jnp.exp2((top - new_top) * factor)
            total = total * shrink + jnp.sum(weights, axis=0, keepdims=True)
            acc = acc * shrink + dot_tn(vals_ref[rows, :], weights.astype(bf16))
            return new_top, total, acc

        start = (
            jnp.full((1, width), negative, f32),
            jnp.zeros((1, width), f32),
            jnp.zeros((HD, width), f32),
        )
        full = (base * half) // chunk
        carry = lax.fori_loop(0, full, lambda j, c: step_chunk(j, c, False), start)
        top, total, acc = step_chunk(full, carry, True)
        acc = acc / total
        attt_ref[0, part] = acc
        lse_ref[0, part] = jnp.broadcast_to(top * factor + jnp.log2(total), (8, width))
        rowwise = acc.T.astype(bf16)
        for g in range(groups):
            att_ref[part * half : (part + 1) * half, g * HD : (g + 1) * HD] = rowwise[
                g * half : (g + 1) * half
            ]


def attend(meta, query, mine, theirs, offs):
    rows = query.shape[0]
    groups = H // KV
    half = rows // 2
    blocks, padded, wide = mine.shape
    span = groups * HD
    width = groups * half
    head = lambda i, m: (0, jnp.where(i == 0, m[0], 1 - m[0]))
    head4 = lambda i, m: (jnp.where(i == 0, m[0], 1 - m[0]), 0, 0, 0)
    whole = lambda i, m: (0, 0, 0)
    keys = blocks * rows
    return pl.pallas_call(
        attend_kernel,
        grid_spec=pltpu.PrefetchScalarGridSpec(
            num_scalar_prefetch=1,
            grid=(2,),
            in_specs=[
                pl.BlockSpec((rows, span), head),
                pl.BlockSpec((blocks, padded, wide), whole, pipeline_mode=pl.Buffered(1)),
                pl.BlockSpec((blocks, padded, wide), whole, pipeline_mode=pl.Buffered(1)),
                pl.BlockSpec((8, width), lambda i, m: (0, 0)),
            ],
            out_specs=[
                pl.BlockSpec((rows, span), head),
                pl.BlockSpec((1, 2, HD, width), head4),
                pl.BlockSpec((1, 2, 8, width), head4),
            ],
            scratch_shapes=[pltpu.VMEM((keys, HD), bf16), pltpu.VMEM((keys, HD), bf16)],
        ),
        out_shape=[
            jax.ShapeDtypeStruct((rows, H * HD), bf16),
            jax.ShapeDtypeStruct((KV, 2, HD, width), f32),
            jax.ShapeDtypeStruct((KV, 2, 8, width), f32),
        ],
        compiler_params=params(),
        cost_estimate=cost(
            2 * 2 * rows * keys * H * HD, 2 * blocks * padded * wide * 2, rows * keys * H // 2
        ),
        name="attend",
    )(meta, query, mine, theirs, offs)


def attend_back_kernel(
    meta_ref,
    q_ref,
    do_ref,
    mine_ref,
    theirs_ref,
    offs_ref,
    attt_ref,
    lse_ref,
    cos_ref,
    sin_ref,
    dq_ref,
    dmine_ref,
    dtheirs_ref,
    keys_ref,
    vals_ref,
    dkeys_ref,
    dvals_ref,
):
    blocks = mine_ref.shape[0]
    half = q_ref.shape[0] // 2
    groups = q_ref.shape[1] // HD
    width = groups * half
    chunk = 4 * half
    scale = 1.0 / math.sqrt(HD)
    factor = LOG2E * scale
    step = pl.program_id(0)

    @pl.when(step == 0)
    def _():
        place_keys(meta_ref, 4, mine_ref, keys_ref, vals_ref, half, blocks)

    @pl.when(step == 1)
    def _():
        place_keys(meta_ref, 4 + 2 * blocks, theirs_ref, keys_ref, vals_ref, half, blocks)

    dkeys_ref[...] = jnp.zeros_like(dkeys_ref)
    dvals_ref[...] = jnp.zeros_like(dvals_ref)
    for part in range(2):
        base = meta_ref[1 + part]
        query = stack_heads(q_ref, part, half, groups)
        grad = stack_heads(do_ref, part, half, groups)
        delta = jnp.sum(grad.astype(f32).T * attt_ref[0, part], axis=0, keepdims=True)
        lse = lse_ref[0, part, 0:1, :]

        def step_chunk(j, dquery, masked):
            rows = pl.ds(pl.multiple_of(j * chunk, 16), chunk)
            keys = keys_ref[rows, :]
            scores = dot_nt(keys, query)
            weights = jnp.exp2(scores * factor - lse)
            if masked:
                row = lax.broadcasted_iota(jnp.int32, scores.shape, 0) + (j * chunk - base * half)
                seen = row <= offs_ref[0:1, :]
                weights = jnp.where(seen, weights, 0.0)
            dweights = dot_nt(vals_ref[rows, :], grad)
            dscores = (weights * (dweights - delta)).astype(bf16)
            dvals_ref[rows, :] += dot(weights.astype(bf16), grad)
            dkeys_ref[rows, :] += dot(dscores, query)
            return dquery + dot_tn(keys, dscores)

        full = (base * half) // chunk
        dquery = lax.fori_loop(
            0, full, lambda j, c: step_chunk(j, c, False), jnp.zeros((HD, width), f32)
        )
        dquery = step_chunk(full, dquery, True)
        rowwise = dquery.T * scale
        these = slice(part * half, (part + 1) * half)
        for g in range(groups):
            turned = turn(rowwise[g * half : (g + 1) * half], cos_ref[these], -sin_ref[these])
            dq_ref[these, g * HD : (g + 1) * HD] = turned.astype(bf16)

    def give(at, out_ref):
        for block in range(blocks):
            for part in range(2):
                rows = pl.ds(pl.multiple_of(meta_ref[at + block * 2 + part] * half, 16), half)
                here = slice(part * half, (part + 1) * half)
                out_ref[block, here, :HD] = (dkeys_ref[rows, :] * scale).astype(bf16)
                out_ref[block, here, HD:] = dvals_ref[rows, :].astype(bf16)

    @pl.when(step == 0)
    def _():
        give(4, dmine_ref)

    @pl.when(step == 1)
    def _():
        give(4 + 2 * blocks, dtheirs_ref)


def attend_back(meta, query, grad, mine, theirs, offs, attt, lse, cos, sin):
    rows = query.shape[0]
    groups = H // KV
    half = rows // 2
    blocks, padded, wide = mine.shape
    span = groups * HD
    width = groups * half
    keys = blocks * rows
    head = lambda i, m: (0, jnp.where(i == 0, m[0], 1 - m[0]))
    head4 = lambda i, m: (jnp.where(i == 0, m[0], 1 - m[0]), 0, 0, 0)
    whole = lambda i, m: (0, 0, 0)
    return pl.pallas_call(
        attend_back_kernel,
        grid_spec=pltpu.PrefetchScalarGridSpec(
            num_scalar_prefetch=1,
            grid=(2,),
            in_specs=[
                pl.BlockSpec((rows, span), head),
                pl.BlockSpec((rows, span), head),
                pl.BlockSpec((blocks, padded, wide), whole, pipeline_mode=pl.Buffered(1)),
                pl.BlockSpec((blocks, padded, wide), whole, pipeline_mode=pl.Buffered(1)),
                pl.BlockSpec((8, width), lambda i, m: (0, 0)),
                pl.BlockSpec((1, 2, HD, width), head4),
                pl.BlockSpec((1, 2, 8, width), head4),
                pl.BlockSpec((rows, HD), lambda i, m: (0, 0)),
                pl.BlockSpec((rows, HD), lambda i, m: (0, 0)),
            ],
            out_specs=[
                pl.BlockSpec((rows, span), head),
                pl.BlockSpec((blocks, rows, wide), whole, pipeline_mode=pl.Buffered(1)),
                pl.BlockSpec((blocks, rows, wide), whole, pipeline_mode=pl.Buffered(1)),
            ],
            scratch_shapes=[
                pltpu.VMEM((keys, HD), bf16),
                pltpu.VMEM((keys, HD), bf16),
                pltpu.VMEM((keys, HD), f32),
                pltpu.VMEM((keys, HD), f32),
            ],
        ),
        out_shape=[
            jax.ShapeDtypeStruct((rows, H * HD), bf16),
            jax.ShapeDtypeStruct((blocks, rows, wide), bf16),
            jax.ShapeDtypeStruct((blocks, rows, wide), bf16),
        ],
        compiler_params=params(),
        cost_estimate=cost(
            5 * rows * keys * H * HD, 2 * blocks * padded * wide * 4, rows * keys * H // 2
        ),
        name="attend_back",
    )(meta, query, grad, mine, theirs, offs, attt, lse, cos, sin)


def expert_kernel(
    plane,
    meta_ref,
    mine_ref,
    theirs_ref,
    dy_ref,
    wg_ref,
    wu_ref,
    wd_ref,
    wr_ref,
    out_mine_ref,
    out_theirs_ref,
    dx_mine_ref,
    dx_theirs_ref,
    hidden_ref,
    dhid_ref,
    gate_ref,
):
    core = meta_ref[0]
    expert = meta_ref[1]
    rows, half_width = mine_ref.shape[2], mine_ref.shape[3]
    width = 2 * half_width
    here = pl.ds(pl.multiple_of(core * half_width, LANES), half_width)
    there = pl.ds(pl.multiple_of((1 - core) * half_width, LANES), half_width)
    x_mine = mine_ref[0].reshape(2 * rows, half_width)
    x_theirs = jnp.concatenate([theirs_ref[0, 1], theirs_ref[0, 0]], axis=0)
    gate_pre = dot(x_mine, wg_ref[here, :]) + dot(x_theirs, wg_ref[there, :])
    up_pre = dot(x_mine, wu_ref[here, :]) + dot(x_theirs, wu_ref[there, :])
    logits = dot(x_mine, wr_ref[here, :]) + dot(x_theirs, wr_ref[there, :])
    dy_pair = jnp.concatenate([dy_ref[0, core], dy_ref[0, 1 - core]], axis=0)
    dy = dy_pair[:, :width].astype(f32)
    chosen = dy_pair[:, width:].astype(f32) > 0.5
    top = jnp.max(jnp.where(chosen, logits, negative), axis=-1, keepdims=True)
    shares = jnp.where(chosen, jnp.exp(logits - top), 0.0)
    lane = lax.broadcasted_iota(jnp.int32, logits.shape, 1)
    own = jnp.sum(jnp.where(lane == expert, shares, 0.0), axis=-1, keepdims=True)
    gate = own / jnp.sum(shares, axis=-1, keepdims=True)
    routed = jnp.sum(jnp.where((lane == expert) & chosen, 1.0, 0.0), axis=-1, keepdims=True)

    sig = jax.nn.sigmoid(gate_pre)
    silu = gate_pre * sig
    hidden = (silu * up_pre).astype(bf16)
    hidden_ref[...] = hidden
    result = dot(hidden, wd_ref[...]).astype(bf16).astype(f32)
    d_gate = routed * jnp.sum(dy * result, axis=-1, keepdims=True)
    share_out = (gate * result).astype(bf16)
    d_expert = (gate * dy).astype(bf16)
    gate_ref[...] = jnp.broadcast_to(gate, gate_ref.shape)
    d_hidden = dot_nt(d_expert, wd_ref[...])
    d_up = (d_hidden * silu).astype(bf16)
    d_gp = (d_hidden * up_pre * (sig * (1.0 + gate_pre * (1.0 - sig)))).astype(bf16)
    inner = d_gp.shape[1]
    dhid_ref[:, :inner] = d_gp
    dhid_ref[:, inner:] = d_up
    high = d_gate.astype(bf16).astype(f32)
    low = d_gate - high
    spot = jnp.where(lane == expert, 1.0, 0.0)
    dx_here = (dot_nt(d_gp, wg_ref[here, :]) + dot_nt(d_up, wu_ref[here, :])).astype(bf16)
    dx_there = (dot_nt(d_gp, wg_ref[there, :]) + dot_nt(d_up, wu_ref[there, :])).astype(bf16)
    col_here = (spot * jnp.where(core == 0, high, low)).astype(bf16)
    col_there = (spot * jnp.where(core == 0, low, high)).astype(bf16)
    for t in range(2):
        these = slice(t * rows, (t + 1) * rows)
        dx_mine_ref[0, t, :, :half_width] = dx_here[these]
        dx_mine_ref[0, t, :, half_width:] = col_here[these]
        dx_theirs_ref[0, 1 - t, :, :half_width] = dx_there[these]
        dx_theirs_ref[0, 1 - t, :, half_width:] = col_there[these]
    first = share_out[:, :half_width]
    second = share_out[:, half_width:]
    out_here = jnp.where(core == 0, first.astype(f32), second.astype(f32)).astype(bf16)
    out_there = jnp.where(core == 0, second.astype(f32), first.astype(f32)).astype(bf16)
    for t in range(2):
        these = slice(t * rows, (t + 1) * rows)
        out_mine_ref[0, t] = out_here[these]
        out_theirs_ref[0, 1 - t] = out_there[these]


def run_expert(plane, meta, mine, theirs, dy_all, wg, wu, wd, wr):
    chips, _, rows, half_width = mine.shape
    width, inner = wg.shape
    wide = dy_all.shape[-1]
    swap = plane.swapped
    pair = lambda w: pl.BlockSpec((1, 2, rows, w), lambda g, m: (g, 0, 0, 0))
    swapped = lambda w: pl.BlockSpec((1, 2, rows, w), lambda g, m: (swap(g), 0, 0, 0))
    flat = lambda w: pl.BlockSpec((2 * rows, w), lambda g, m: (g, 0))
    weight = lambda shape: pl.BlockSpec(shape, lambda g, m: (0, 0), pipeline_mode=pl.Buffered(1))
    total = chips * 2 * rows
    return pl.pallas_call(
        functools.partial(expert_kernel, plane),
        grid_spec=pltpu.PrefetchScalarGridSpec(
            num_scalar_prefetch=1,
            grid=(chips,),
            in_specs=[
                pair(half_width),
                swapped(half_width),
                pl.BlockSpec((1, 2, rows, wide), lambda g, m: (m[2 + g], 0, 0, 0)),
                weight((width, inner)),
                weight((width, inner)),
                weight((inner, width)),
                weight((width, wr.shape[1])),
            ],
            out_specs=[
                pair(half_width),
                swapped(half_width),
                pair(half_width + LANES),
                swapped(half_width + LANES),
                flat(inner),
                flat(2 * inner),
                flat(LANES),
            ],
        ),
        out_shape=[
            jax.ShapeDtypeStruct((chips, 2, rows, half_width), bf16),
            jax.ShapeDtypeStruct((chips, 2, rows, half_width), bf16),
            jax.ShapeDtypeStruct((chips, 2, rows, half_width + LANES), bf16),
            jax.ShapeDtypeStruct((chips, 2, rows, half_width + LANES), bf16),
            jax.ShapeDtypeStruct((total, inner), bf16),
            jax.ShapeDtypeStruct((total, 2 * inner), bf16),
            jax.ShapeDtypeStruct((total, LANES), f32),
        ],
        compiler_params=params(),
        cost_estimate=cost(12 * total * width * inner, 20 * total * width, total * inner),
        name="expert",
    )(meta, mine, theirs, dy_all, wg, wu, wd, wr)


def expert_grad_kernel(
    meta_ref, mine_ref, theirs_ref, dy_ref, hid_ref, dhid_ref, gate_ref, out_ref, sum_ref
):
    core = meta_ref[0]
    step = pl.program_id(0)
    rows, half = mine_ref.shape[2], mine_ref.shape[3]
    width = 2 * half
    double = dhid_ref.shape[1]

    @pl.when(step == 0)
    def _():
        sum_ref[...] = jnp.zeros_like(sum_ref)

    here = pl.ds(pl.multiple_of(core * half, LANES), half)
    there = pl.ds(pl.multiple_of((1 - core) * half, LANES), half)
    x_mine = mine_ref[0].reshape(2 * rows, half)
    x_theirs = jnp.concatenate([theirs_ref[0, 1], theirs_ref[0, 0]], axis=0)
    sum_ref[here, :double] += dot_tn(x_mine, dhid_ref[...])
    sum_ref[there, :double] += dot_tn(x_theirs, dhid_ref[...])
    dy = jnp.concatenate([dy_ref[0, core], dy_ref[0, 1 - core]], axis=0)[:, :width].astype(f32)
    d_expert = (gate_ref[:, 0:1] * dy).astype(bf16)
    sum_ref[:, double:] += dot_tn(d_expert, hid_ref[...])

    @pl.when(step == pl.num_programs(0) - 1)
    def _():
        out_ref[...] = sum_ref[...].astype(bf16)


def expert_grad(plane, meta, mine, theirs, dy_all, hid, dhid, gate):
    chips, _, rows, half = mine.shape
    width, inner = 2 * half, hid.shape[1]
    wide = dy_all.shape[-1]
    flat = lambda w: pl.BlockSpec((2 * rows, w), lambda g, m: (g, 0))
    total = chips * 2 * rows
    return pl.pallas_call(
        expert_grad_kernel,
        grid_spec=pltpu.PrefetchScalarGridSpec(
            num_scalar_prefetch=1,
            grid=(chips,),
            in_specs=[
                pl.BlockSpec((1, 2, rows, half), lambda g, m: (g, 0, 0, 0)),
                pl.BlockSpec((1, 2, rows, half), lambda g, m: (plane.swapped(g), 0, 0, 0)),
                pl.BlockSpec((1, 2, rows, wide), lambda g, m: (m[2 + g], 0, 0, 0)),
                flat(inner),
                flat(2 * inner),
                flat(LANES),
            ],
            out_specs=fixed((width, 3 * inner)),
            scratch_shapes=[pltpu.VMEM((width, 3 * inner), f32)],
        ),
        out_shape=jax.ShapeDtypeStruct((width, 3 * inner), bf16),
        compiler_params=params(),
        cost_estimate=cost(6 * total * width * inner, 8 * total * width),
        name="expert_grad",
    )(meta, mine, theirs, dy_all, hid, dhid, gate)


def swap_pair(values, axis):
    return lax.ppermute(values, axis, [(0, 1), (1, 0)])


def reduce_everyone(plane, keep, send):
    held = add_low(keep, lax.ppermute(send, "expert", plane.sibling))
    for k in reversed(range(plane.steps)):
        half = held.shape[0] // 2
        held = add_low(held[:half], lax.ppermute(held[half:], "expert", plane.mixed[k]))
    held = held[0]
    held = add_low(held[:, :, 0], swap_pair(held[:, :, 1], "dp"))
    held = add_low(held[:, 0], swap_pair(held[:, 1], "context"))
    return held[0], lax.ppermute(held[1], "expert", plane.sibling)


def per_device(
    tokens,
    gain_attn,
    w_query,
    w_key,
    w_value,
    w_out,
    gain_moe,
    w_router,
    w_gate,
    w_up,
    w_down,
    routes,
    positions,
    cotangent,
):
    rows = tokens.shape[1]
    width = tokens.shape[2]
    half_width = width // 2
    half = rows // 2
    groups = H // KV
    kv_width = KV * HD
    experts = w_router.shape[1]
    plane = Plane(w_gate.shape[0] * lax.axis_size("expert"))
    contexts = lax.axis_size("context")
    copies = lax.axis_size("dp")
    blocks = plane.size * contexts
    index = lax.axis_index("expert")
    core = index % 2
    places = positions[0]
    x = tokens[0]

    lanes = jnp.arange(LANES, dtype=jnp.int32)
    marks = jnp.any(routes[0][:, :, None] == lanes[None, None, :], axis=1).astype(bf16)
    marked = jnp.concatenate([cotangent[0], marks], axis=1)
    dy_all = lax.all_gather(marked, "expert", axis=0).reshape(
        plane.chips, 2, rows, width + LANES
    )

    cos, sin = rope_tables(places)
    own_bases = jnp.stack([places[0], places[half]]) // half
    front_meta = jnp.concatenate([core[None], own_bases]).astype(jnp.int32)
    xn_one, packed = front(front_meta, x, gain_attn[None], w_key, w_value, cos, sin)
    swap_context = [(i, i ^ 1) for i in range(contexts)]
    if contexts > 1:
        packed = jnp.stack([packed, lax.ppermute(packed, "context", swap_context)], axis=1)
    else:
        packed = packed[:, None]
    mine, theirs = gather_plane(plane, packed[0], packed[1])
    mine = mine.reshape(blocks, rows + PAD_ROWS, kv_width)
    theirs = theirs.reshape(blocks, rows + PAD_ROWS, kv_width)

    def bases(buf):
        return buf[:, rows :: PAD_ROWS // 2, 0].astype(f32).astype(jnp.int32).reshape(-1)

    meta = jnp.concatenate([front_meta, front_meta[:1], bases(mine), bases(theirs)])
    offs = jnp.broadcast_to(
        (jnp.arange(groups * half, dtype=jnp.int32) % half)[None, :], (8, groups * half)
    )

    query = make_query(xn_one, w_query, cos, sin)
    attended, attended_t, lse = attend(meta, query, mine, theirs, offs)
    hidden, xn_two, keep, send = join(front_meta, attended, w_out, x, gain_moe[None])
    x_mine, x_theirs = gather_plane(plane, keep, send)

    offsets = jnp.array(
        [[plane.chip_offset(c, g) // 2 for g in range(plane.chips)] for c in range(2)], jnp.int32
    )
    chips = (index // 2) ^ jnp.where(core == 0, offsets[0], offsets[1])
    expert_meta = jnp.concatenate([core[None], index[None], chips]).astype(jnp.int32)
    router_wide = jnp.pad(w_router, ((0, 0), (0, LANES - experts)))
    out_mine, out_theirs, dx_mine, dx_theirs, hid_rows, dhid_rows, gates = run_expert(
        plane, expert_meta, x_mine, x_theirs, dy_all, w_gate[0], w_up[0], w_down[0], router_wide
    )
    inner = w_gate.shape[2]
    dx_keep, dx_other = reduce_plane(plane, dx_mine, dx_theirs)

    grads = expert_grad(
        plane, expert_meta, x_mine, x_theirs, dy_all, hid_rows, dhid_rows, gates
    )
    grads = lax.psum_scatter(grads, ("context", "dp"), scatter_dimension=0, tiled=True)
    grad_gate = grads[:, :inner].astype(f32)[None]
    grad_up = grads[:, inner : 2 * inner].astype(f32)[None]
    grad_down = grads[:, 2 * inner :].astype(f32).T[None]

    def in_order(own, other):
        return jnp.where(
            core == 0,
            jnp.concatenate([own, other], axis=1),
            jnp.concatenate([other, own], axis=1),
        )

    d_state, d_low, d_logits, d_gain_moe, d_attended = middle(
        front_meta, dx_keep, dx_other, hidden, xn_two, gain_moe[None], marked, router_wide, w_out
    )
    d_query, d_mine, d_theirs = attend_back(
        meta, query, d_attended, mine, theirs, offs, attended_t, lse, cos, sin
    )
    kv_shape = (plane.chips, 2, contexts, rows, kv_width)
    dkv_keep, dkv_other = reduce_plane(plane, d_mine.reshape(kv_shape), d_theirs.reshape(kv_shape))
    dkv = jnp.stack([dkv_keep, dkv_other], axis=1)
    if contexts > 1:
        dkv = dkv[0].astype(f32) + lax.ppermute(dkv[1], "context", swap_context).astype(f32)
    else:
        dkv = dkv[0].astype(f32)
    out_keep, out_other = reduce_plane(plane, out_mine, out_theirs)
    output = (hidden + in_order(out_keep, out_other).astype(f32)).astype(bf16)[None]

    dxq = times_transposed(d_query, w_query)
    d_in, d_kv, d_gain_attn = back(
        front_meta, dkv[0], dkv[1], dxq, x, gain_attn[None], d_state, w_key, w_value, cos, sin
    )

    if contexts == 2 and copies == 2 and (width // plane.chips) % LANES == 0:
        place = lax.axis_index("context") * 2 + lax.axis_index("dp")
        dense_meta = jnp.concatenate([core[None], place[None], chips]).astype(jnp.int32)
        reduced = lambda *a: in_order(
            *reduce_everyone(plane, *dense_grad(plane, dense_meta, *a))
        ).astype(f32)
        grad_query = reduced(xn_one, d_query)
        grad_out = reduced(d_low, attended)
        small = reduced(xn_one, d_kv, (xn_two, d_logits, jnp.stack([d_gain_attn, d_gain_moe])))
        grad_key = small[:, :kv_width]
        extra = small[:, kv_width : kv_width + LANES]
        grad_value = small[:, kv_width + LANES : 2 * kv_width + LANES]
    else:
        scatter = lambda v: lax.psum_scatter(
            v.astype(bf16), ("expert", "context", "dp"), scatter_dimension=0, tiled=True
        ).astype(f32)
        grad_query = scatter(dot_tn(xn_one, d_query))
        grad_out = scatter(dot_tn(d_low, attended))
        grad_kv = scatter(dot_tn(xn_one, d_kv))
        grad_key, grad_value = grad_kv[:, :kv_width], grad_kv[:, kv_width:]
        router = dot_tn(xn_two, d_logits)[:, : LANES - 2]
        extra = scatter(
            jnp.concatenate([router, d_gain_attn[:1].T, d_gain_moe[:1].T], axis=1)
        )
    return (
        output,
        d_in[None],
        extra[:, LANES - 2],
        grad_query,
        grad_key,
        grad_value,
        grad_out.T,
        extra[:, LANES - 1],
        extra[:, :experts],
        grad_gate,
        grad_up,
        grad_down,
    )


def solution(mesh):
    in_specs = (
        P("dp", ("expert", "context"), None),
        P(),
        P(),
        P(),
        P(),
        P(),
        P(),
        P(),
        P("expert", None, None),
        P("expert", None, None),
        P("expert", None, None),
        P("dp", ("expert", "context"), None),
        P("dp", ("expert", "context")),
        P("dp", ("expert", "context"), None),
    )
    out_specs = (
        P("dp", ("expert", "context"), None),
        P("dp", ("expert", "context"), None),
        P(("expert", "context", "dp")),
        P(("expert", "context", "dp"), None),
        P(("expert", "context", "dp"), None),
        P(("expert", "context", "dp"), None),
        P(None, ("expert", "context", "dp")),
        P(("expert", "context", "dp")),
        P(("expert", "context", "dp"), None),
        P("expert", ("context", "dp"), None),
        P("expert", ("context", "dp"), None),
        P("expert", None, ("context", "dp")),
    )
    return jax.shard_map(
        per_device, mesh=mesh, in_specs=in_specs, out_specs=out_specs, check_vma=False
    )
```

```python
import functools
import math

import jax
import jax.numpy as jnp
import numpy as np
from jax import lax
from jax.experimental import pallas as pl
from jax.experimental.pallas import tpu as pltpu
from jax.sharding import PartitionSpec as P

H = 12
KV = 2
HD = 128
TOP = 4

eps = 1e-06
rope_base = 1000000.0
negative = -1e30
LANES = 128
JOIN_TILES = 3
CHUNK_BLOCKS = 8
SCATTER_TIE = 1
PAD_ROWS = 16
bf16 = jnp.bfloat16
f32 = jnp.float32
LOG2E = 1.4426950408889634


def dot(a, b):
    return lax.dot_general(a, b, (((1,), (0,)), ((), ())), preferred_element_type=f32)


def dot_nt(a, b):
    return lax.dot_general(a, b, (((1,), (1,)), ((), ())), preferred_element_type=f32)


def dot_tn(a, b):
    return lax.dot_general(a, b, (((0,), (0,)), ((), ())), preferred_element_type=f32)


def params(mebibytes):
    return pltpu.CompilerParams(
        dimension_semantics=("arbitrary",), vmem_limit_bytes=min(int(mebibytes), 60) * 1024 * 1024
    )


def after(value, *others):
    return lax.optimization_barrier((value,) + others)[0]


def cost(flops, moved, exps=0):
    return pl.CostEstimate(flops=int(flops), bytes_accessed=int(moved), transcendentals=int(exps))


def turn(values, cos, sin):
    return values * cos + pltpu.roll(values, HD // 2, 1) * sin


def norm_scale(values):
    return lax.rsqrt(jnp.mean(values * values, axis=-1, keepdims=True) + eps)


def rope_tables(count, half):
    freqs = rope_base ** (-np.arange(0, HD, 2) / HD)
    angles = np.concatenate([np.arange(count) * half, np.arange(half)])[:, None] * freqs[None, :]
    twice = np.concatenate([angles, angles], axis=1)
    return jnp.asarray(np.cos(twice), f32), jnp.asarray(np.sin(twice), f32)


def fixed(shape):
    zeros = (0,) * len(shape)
    return pl.BlockSpec(shape, lambda *_: zeros, pipeline_mode=pl.Buffered(1))


def front_kernel(
    core_ref,
    places_ref,
    x_ref,
    gain_ref,
    wk_ref,
    wv_ref,
    tcos_ref,
    tsin_ref,
    xn_ref,
    packed_ref,
    cos_ref,
    sin_ref,
):
    core = core_ref[0]
    rows = x_ref.shape[0]
    half = rows // 2
    bases = [lax.div(places_ref[part * half], half) for part in range(2)]
    count = tcos_ref.shape[0] - half
    sign = jnp.where(lax.broadcasted_iota(jnp.int32, (half, HD), 1) < HD // 2, -1.0, 1.0)
    for part in range(2):
        these = slice(part * half, (part + 1) * half)
        base = pl.ds(bases[part], 1)
        cos_base, sin_base = tcos_ref[base, :], tsin_ref[base, :]
        cos_off, sin_off = tcos_ref[count:, :], tsin_ref[count:, :]
        cos_ref[these, :] = cos_base * cos_off - sin_base * sin_off
        sin_ref[these, :] = (sin_base * cos_off + cos_base * sin_off) * sign
    values = x_ref[...].astype(f32)
    normed = (values * norm_scale(values) * gain_ref[...]).astype(bf16)
    xn_ref[...] = normed
    keys = dot(normed, wk_ref[...])
    vals = dot(normed, wv_ref[...]).astype(bf16)
    edge = lax.broadcasted_iota(jnp.int32, (PAD_ROWS, 2 * HD), 0) < PAD_ROWS // 2
    tail = jnp.where(edge, bases[0].astype(f32), bases[1].astype(f32)).astype(bf16)
    for head in range(KV):
        slot = jnp.where(core == head, 0, 1)
        span = slice(head * HD, (head + 1) * HD)
        turned = turn(keys[:, span], cos_ref[...], sin_ref[...]).astype(bf16)
        packed_ref[slot, :rows, :HD] = turned
        packed_ref[slot, :rows, HD:] = vals[:, span]
        packed_ref[slot, rows:, :] = tail


def front(core, places, x, gain, wk, wv, tcos, tsin):
    rows, width = x.shape
    return pl.pallas_call(
        front_kernel,
        grid_spec=pltpu.PrefetchScalarGridSpec(
            num_scalar_prefetch=2,
            grid=(1,),
            in_specs=[fixed(a.shape) for a in (x, gain, wk, wv, tcos, tsin)],
            out_specs=[
                fixed((rows, width)),
                fixed((2, rows + PAD_ROWS, 2 * HD)),
                fixed((rows, HD)),
                fixed((rows, HD)),
            ],
        ),
        out_shape=[
            jax.ShapeDtypeStruct((rows, width), bf16),
            jax.ShapeDtypeStruct((2, rows + PAD_ROWS, 2 * HD), bf16),
            jax.ShapeDtypeStruct((rows, HD), f32),
            jax.ShapeDtypeStruct((rows, HD), f32),
        ],
        compiler_params=params(60),
        cost_estimate=cost(4 * rows * width * KV * HD, 8 * rows * width),
        name="front",
    )(core, places, x, gain, wk, wv, tcos, tsin)


def query_kernel(x_ref, w_ref, cos_ref, sin_ref, out_ref):
    raw = dot(x_ref[...], w_ref[...])
    for head in range(raw.shape[1] // HD):
        span = slice(head * HD, (head + 1) * HD)
        out_ref[:, span] = turn(raw[:, span], cos_ref[...], sin_ref[...]).astype(bf16)


def make_query(x, w, cos, sin):
    rows, width = x.shape
    wide = w.shape[1]
    tile = 4 * HD
    return pl.pallas_call(
        query_kernel,
        grid=(wide // tile,),
        in_specs=[
            fixed((rows, width)),
            pl.BlockSpec((width, tile), lambda i: (0, i)),
            fixed((rows, HD)),
            fixed((rows, HD)),
        ],
        out_specs=pl.BlockSpec((rows, tile), lambda i: (0, i)),
        out_shape=jax.ShapeDtypeStruct((rows, wide), bf16),
        compiler_params=params(12),
        cost_estimate=cost(2 * rows * width * wide, 2 * width * wide),
        name="make_query",
    )(x, w, cos, sin)


def join_kernel(meta_ref, att_ref, w_ref, x_ref, gain_ref, hid_ref, xn_ref, keep_ref, send_ref):
    core = meta_ref[0]
    step = pl.program_id(0)
    width = hid_ref.shape[1]
    tile = width // JOIN_TILES
    span = pl.ds(pl.multiple_of(step * tile, LANES), tile)
    hid_ref[:, span] = x_ref[:, span].astype(f32) + dot(att_ref[...], w_ref[...])

    @pl.when(step == pl.num_programs(0) - 1)
    def _():
        hidden = hid_ref[...]
        xn_ref[...] = (hidden * norm_scale(hidden) * gain_ref[...]).astype(bf16)
        half = width // 2
        keep_ref[...] = xn_ref[:, pl.ds(pl.multiple_of(core * half, LANES), half)]
        send_ref[...] = xn_ref[:, pl.ds(pl.multiple_of((1 - core) * half, LANES), half)]


def join(meta, att, w, x, gain):
    rows, width = x.shape
    inner = att.shape[1]
    tile = width // JOIN_TILES
    return pl.pallas_call(
        join_kernel,
        grid_spec=pltpu.PrefetchScalarGridSpec(
            num_scalar_prefetch=1,
            grid=(width // tile,),
            in_specs=[
                fixed((rows, inner)),
                pl.BlockSpec((inner, tile), lambda i, m: (0, i)),
                fixed((rows, width)),
                fixed((width,)),
            ],
            out_specs=[
                fixed((rows, width)),
                fixed((rows, width)),
                fixed((rows, width // 2)),
                fixed((rows, width // 2)),
            ],
        ),
        out_shape=[
            jax.ShapeDtypeStruct((rows, width), f32),
            jax.ShapeDtypeStruct((rows, width), bf16),
            jax.ShapeDtypeStruct((rows, width // 2), bf16),
            jax.ShapeDtypeStruct((rows, width // 2), bf16),
        ],
        compiler_params=params(16),
        cost_estimate=cost(2 * rows * width * inner, 2 * width * inner),
        name="join",
    )(meta, att, w, x, gain)


def middle_kernel(
    meta_ref,
    own_ref,
    other_ref,
    hid_ref,
    xn_ref,
    gain_ref,
    dy_ref,
    wr_ref,
    w_ref,
    dstate_ref,
    dlow_ref,
    dlog_ref,
    dgain_ref,
    datt_ref,
    dx_ref,
):
    core = meta_ref[0]
    step = pl.program_id(0)
    width = hid_ref.shape[1]
    half = width // 2

    @pl.when(step == 0)
    def _():
        dx_ref[:, pl.ds(pl.multiple_of(core * half, LANES), half)] = own_ref[:, :half].astype(f32)
        dx_ref[:, pl.ds(pl.multiple_of((1 - core) * half, LANES), half)] = other_ref[
            :, :half
        ].astype(f32)
        d_gate = own_ref[:, half:].astype(f32) + other_ref[:, half:].astype(f32)
        chosen = dy_ref[:, width:].astype(f32) > 0.5
        logits = dot(xn_ref[...], wr_ref[...])
        top = jnp.max(jnp.where(chosen, logits, negative), axis=-1, keepdims=True)
        shares = jnp.where(chosen, jnp.exp(logits - top), 0.0)
        gate = shares / jnp.sum(shares, axis=-1, keepdims=True)
        inner_sum = jnp.sum(gate * d_gate, axis=-1, keepdims=True)
        d_logits = (gate * (d_gate - inner_sum)).astype(bf16)
        dlog_ref[...] = d_logits
        d_xn = dx_ref[...] + dot_nt(d_logits, wr_ref[...])
        hidden = hid_ref[...]
        scale_row = norm_scale(hidden)
        normed = hidden * scale_row
        dgain_ref[...] = jnp.broadcast_to(
            jnp.sum(d_xn * normed, axis=0, keepdims=True), dgain_ref.shape
        )
        scaled = d_xn * gain_ref[...]
        inner_mean = jnp.mean(scaled * normed, axis=-1, keepdims=True)
        d_state = dy_ref[:, :width].astype(f32) + scale_row * (scaled - normed * inner_mean)
        dstate_ref[...] = d_state
        dlow_ref[...] = d_state.astype(bf16)

    datt_ref[...] = dot_nt(dlow_ref[...], w_ref[...]).astype(bf16)


def middle(meta, own, other, hidden, xn, gain, dy, wr, w):
    rows, width = hidden.shape
    inner = w.shape[0]
    tile = inner // JOIN_TILES
    return pl.pallas_call(
        middle_kernel,
        grid_spec=pltpu.PrefetchScalarGridSpec(
            num_scalar_prefetch=1,
            grid=(inner // tile,),
            in_specs=[fixed(a.shape) for a in (own, other, hidden, xn, gain, dy, wr)]
            + [pl.BlockSpec((tile, width), lambda i, m: (i, 0))],
            out_specs=[
                fixed((rows, width)),
                fixed((rows, width)),
                fixed((rows, LANES)),
                fixed((8, width)),
                pl.BlockSpec((rows, tile), lambda i, m: (0, i)),
            ],
            scratch_shapes=[pltpu.VMEM((rows, width), f32)],
        ),
        out_shape=[
            jax.ShapeDtypeStruct((rows, width), f32),
            jax.ShapeDtypeStruct((rows, width), bf16),
            jax.ShapeDtypeStruct((rows, LANES), bf16),
            jax.ShapeDtypeStruct((8, width), f32),
            jax.ShapeDtypeStruct((rows, inner), bf16),
        ],
        compiler_params=params(20),
        cost_estimate=cost(2 * rows * width * inner, 2 * width * inner),
        name="middle",
    )(meta, own, other, hidden, xn, gain, dy, wr, w)


def times_kernel(x_ref, w_ref, out_ref):
    out_ref[...] = dot_nt(x_ref[...], w_ref[...])


def times_transposed(x, w):
    rows, inner = x.shape
    width = w.shape[0]
    tile = width // 3
    return pl.pallas_call(
        times_kernel,
        grid=(width // tile,),
        in_specs=[fixed((rows, inner)), pl.BlockSpec((tile, inner), lambda i: (i, 0))],
        out_specs=pl.BlockSpec((rows, tile), lambda i: (0, i)),
        out_shape=jax.ShapeDtypeStruct((rows, width), f32),
        compiler_params=params(12),
        cost_estimate=cost(2 * rows * width * inner, 2 * width * inner),
        name="times_transposed",
    )(x, w)


def back_kernel(
    meta_ref,
    own_ref,
    other_ref,
    dxq_ref,
    x_ref,
    gain_ref,
    dstate_ref,
    wk_ref,
    wv_ref,
    cos_ref,
    sin_ref,
    din_ref,
    dkv_ref,
    dgain_ref,
    pair_ref,
):
    core = meta_ref[0]
    pair_ref[core] = own_ref[...].astype(f32)
    pair_ref[1 - core] = other_ref[...].astype(f32)
    wide = KV * HD
    for head in range(KV):
        turned = turn(pair_ref[head, :, :HD], cos_ref[...], -sin_ref[...])
        dkv_ref[:, head * HD : (head + 1) * HD] = turned.astype(bf16)
        dkv_ref[:, wide + head * HD : wide + (head + 1) * HD] = pair_ref[head, :, HD:].astype(bf16)
    d_xn = (
        dxq_ref[...]
        + dot_nt(dkv_ref[:, :wide], wk_ref[...])
        + dot_nt(dkv_ref[:, wide:], wv_ref[...])
    )
    values = x_ref[...].astype(f32)
    scale_row = norm_scale(values)
    normed = values * scale_row
    dgain_ref[...] = jnp.broadcast_to(
        jnp.sum(d_xn * normed, axis=0, keepdims=True), dgain_ref.shape
    )
    scaled = d_xn * gain_ref[...]
    inner_mean = jnp.mean(scaled * normed, axis=-1, keepdims=True)
    din_ref[...] = (dstate_ref[...] + scale_row * (scaled - normed * inner_mean)).astype(bf16)


def back(meta, own, other, dxq, x, gain, dstate, wk, wv, cos, sin):
    rows, width = x.shape
    return pl.pallas_call(
        back_kernel,
        grid_spec=pltpu.PrefetchScalarGridSpec(
            num_scalar_prefetch=1,
            grid=(1,),
            in_specs=[
                fixed(a.shape) for a in (own, other, dxq, x, gain, dstate, wk, wv, cos, sin)
            ],
            out_specs=[
                fixed((rows, width)),
                fixed((rows, 2 * KV * HD)),
                fixed((8, width)),
            ],
            scratch_shapes=[pltpu.VMEM((KV, rows, 2 * HD), f32)],
        ),
        out_shape=[
            jax.ShapeDtypeStruct((rows, width), bf16),
            jax.ShapeDtypeStruct((rows, 2 * KV * HD), bf16),
            jax.ShapeDtypeStruct((8, width), f32),
        ],
        compiler_params=params(16),
        cost_estimate=cost(4 * rows * width * KV * HD, 16 * rows * width),
        name="back",
    )(meta, own, other, dxq, x, gain, dstate, wk, wv, cos, sin)


def dense_kernel(steps, extra, meta_ref, left_ref, left2_ref, right_ref, right2_ref, *refs):
    if extra:
        xn_ref, dlog_ref, gain1_ref, gain2_ref = refs[:4]
        refs = refs[4:]
        more_ref = refs[-1]
        refs = refs[:-1]
    outs, whole_ref = refs[:-1], refs[-1]
    core = meta_ref[0]
    place = meta_ref[1]
    group = pl.program_id(0)
    piece = outs[0].shape[4]
    wide = right_ref.shape[1]
    left = jnp.concatenate([left_ref[...], left2_ref[...]], axis=0)
    right = jnp.concatenate([right_ref[...], right2_ref[...]], axis=0)
    whole_ref[...] = dot_tn(left, right)
    if extra:
        router = dot_tn(xn_ref[...], dlog_ref[...])
        first = jnp.broadcast_to(gain1_ref[0:1, :], (LANES, router.shape[0])).T
        second = jnp.broadcast_to(gain2_ref[0:1, :], (LANES, router.shape[0])).T
        lane = lax.broadcasted_iota(jnp.int32, router.shape, 1)
        more_ref[...] = jnp.where(
            lane == LANES - 2, first, jnp.where(lane == LANES - 1, second, router)
        )

    def give(out_ref):
        for d in range(2):
            for c in range(2):
                for t in range(2):
                    at = ((core ^ t) * 4 + (place ^ (c * 2 + d))) * piece
                    rows = pl.ds(pl.multiple_of(at, 16), piece)
                    out_ref[0, d, c, t, :, :wide] = whole_ref[rows, :].astype(bf16)
                    if extra:
                        out_ref[0, d, c, t, :, wide:] = more_ref[rows, :].astype(bf16)

    for k in range(steps):

        @pl.when((group >= 2**k) & (group < 2 ** (k + 1)))
        def _():
            give(outs[k])

    @pl.when(group == 0)
    def _():
        give(outs[steps])


def dense_grad(plane, meta, left, left2, right, right2, extra=()):
    rows, width = left.shape
    wide = right.shape[1]
    part = width // plane.chips
    piece = part // 8
    held = wide + (LANES if extra else 0)
    columns = pl.BlockSpec((rows, part), lambda g, m: (0, m[2 + g]))
    gains = pl.BlockSpec((8, part), lambda g, m: (0, m[2 + g]))
    more = [columns, fixed((rows, LANES)), gains, gains]

    def out(first, size):
        where = lambda g, m: (jnp.clip(g - first, 0, size - 1), 0, 0, 0, 0, 0)
        return pl.BlockSpec((1, 2, 2, 2, piece, held), where)

    ranges = [(2**k, 2**k) for k in range(plane.steps)] + [(0, 1)]
    return pl.pallas_call(
        functools.partial(dense_kernel, plane.steps, bool(extra)),
        grid_spec=pltpu.PrefetchScalarGridSpec(
            num_scalar_prefetch=1,
            grid=(plane.chips,),
            in_specs=[columns, columns, fixed((rows, wide)), fixed((rows, wide))]
            + (more if extra else []),
            out_specs=[out(*r) for r in ranges],
            scratch_shapes=[pltpu.VMEM((part, wide), f32)]
            + ([pltpu.VMEM((part, LANES), f32)] if extra else []),
        ),
        out_shape=[
            jax.ShapeDtypeStruct((size, 2, 2, 2, piece, held), bf16) for _, size in ranges
        ],
        compiler_params=params(28),
        cost_estimate=cost(4 * rows * width * wide, 2 * width * wide),
        name="dense_grad",
    )(meta, left, left2, right, right2, *extra)


class Plane:
    def __init__(self, size):
        self.size = size
        bits = size.bit_length() - 1
        self.steps = bits - 1
        self.shift = self.steps // 2 if self.steps % 2 == 0 else 0
        first = list(range(1, bits))
        self.order = (first, first[self.shift :] + first[: self.shift])
        self.sibling = [(i, i ^ 1) for i in range(size)]
        self.mixed = [
            [(i, i ^ (1 << self.order[i & 1][k])) for i in range(size)] for k in range(self.steps)
        ]
        self.chips = size // 2

    def chip_offset(self, core, group):
        return sum(((group >> k) & 1) << self.order[core][k] for k in range(self.steps))

    def swapped(self, group):
        if not self.shift:
            return group
        low_mask = (1 << self.shift) - 1
        return ((group & low_mask) << (self.steps - self.shift)) | (group >> self.shift)


def total(values):
    summed = values[0].astype(f32)
    for value in values[1:]:
        summed = summed + value.astype(f32)
    return summed.astype(bf16)


def reduce_steps(plane, terms, hold=()):
    terms = list(terms)

    def pick(first, last):
        return [
            a[first - at : last - at] for at, a in terms if at <= first and last - at <= a.shape[0]
        ]

    for k in reversed(range(plane.steps)):
        send = total(pick(2**k, 2 ** (k + 1)))
        terms.append((0, lax.ppermute(send, "expert", plane.mixed[k])))
    return [a[0] for a in pick(0, 1)]


def to_sibling(plane, value):
    return lax.ppermute(value, "expert", plane.sibling)


def place_keys(bases_ref, at, buf_ref, keys_ref, vals_ref, half, blocks):
    for block in range(blocks):
        for part in range(2):
            rows = pl.ds(pl.multiple_of(bases_ref[at + block * 2 + part] * half, 16), half)
            keys_ref[rows, :] = buf_ref[block, part * half : (part + 1) * half, :HD]
            vals_ref[rows, :] = buf_ref[block, part * half : (part + 1) * half, HD:]


def stack_heads(ref, part, half, groups):
    return jnp.concatenate(
        [
            ref[part * half : (part + 1) * half, g * HD : (g + 1) * HD]
            for g in range(groups)
        ],
        axis=0,
    )


def for_steps(count, body):
    if count <= 8:
        for n in range(count):
            body(n)
    else:
        lax.fori_loop(0, count, lambda n, _: (body(n), 0)[1], 0)


def attend_kernel(at, unread, meta_ref, q_ref, buf_ref, offs_ref, *refs):
    (
        att_ref,
        attt_ref,
        lse_ref,
        keys_ref,
        vals_ref,
        query_ref,
        top_ref,
        sum_ref,
        mix_ref,
    ) = refs[unread:]
    blocks = buf_ref.shape[0]
    half = q_ref.shape[0] // 2
    groups = q_ref.shape[1] // HD
    chunk = CHUNK_BLOCKS * half
    factor = LOG2E / math.sqrt(HD)
    count = 2 * blocks // CHUNK_BLOCKS - 1
    place_keys(meta_ref, at, buf_ref, keys_ref, vals_ref, half, blocks)
    for part in range(2):
        query_ref[part] = stack_heads(q_ref, part, half, groups)
    full = [lax.div(meta_ref[1 + part], CHUNK_BLOCKS) for part in range(2)]

    def step(n, part, j, edge):
        rows = pl.ds(pl.multiple_of(j * chunk, 16), chunk)
        scores = dot_nt(keys_ref[rows, :], query_ref[part])
        if edge is not None:
            row = lax.broadcasted_iota(jnp.int32, scores.shape, 0) + (j * chunk - edge * half)
            scores = jnp.where(row <= offs_ref[0:1, :], scores, negative)
        top = jnp.max(scores, axis=0, keepdims=True)
        weights = jnp.exp2((scores - top) * factor)
        top_ref[n, 0:1, :] = top
        sum_ref[n, 0:1, :] = jnp.sum(weights, axis=0, keepdims=True)
        mix_ref[n] = dot_tn(vals_ref[rows, :], weights.astype(bf16))

    def full_step(n):
        late = n >= full[0]
        part = jnp.where(late, 1, 0)
        step(n, part, n - jnp.where(late, full[0], 0), None)

    for_steps(count, full_step)
    for part in range(2):
        step(count + part, part, full[part], meta_ref[1 + part])
    for part in range(2):
        edge = count + part
        top = top_ref[edge, 0:1, :]

        def mine(n):
            return (n < full[0]) if part == 0 else (n >= full[0])

        def find(n, top):
            return jnp.where(mine(n), jnp.maximum(top, top_ref[n, 0:1, :]), top)

        def add(n, carry):
            summed, acc = carry
            share = jnp.exp2((top_ref[n, 0:1, :] - top) * factor)
            share = jnp.where(mine(n), jnp.minimum(share, 1.0), 0.0)
            return summed + share * sum_ref[n, 0:1, :], acc + share * mix_ref[n]

        top = fold_steps(count, find, top)
        share = jnp.exp2((top_ref[edge, 0:1, :] - top) * factor)
        summed, acc = fold_steps(
            count, add, (share * sum_ref[edge, 0:1, :], share * mix_ref[edge])
        )
        acc = acc / summed
        attt_ref[part] = acc
        lse_ref[part] = jnp.broadcast_to(top * factor + jnp.log2(summed), lse_ref.shape[1:])
        rowwise = acc.T.astype(bf16)
        for g in range(groups):
            att_ref[part * half : (part + 1) * half, g * HD : (g + 1) * HD] = rowwise[
                g * half : (g + 1) * half
            ]


def fold_steps(count, body, carry):
    if count <= 8:
        for n in range(count):
            carry = body(n, carry)
        return carry
    return lax.fori_loop(0, count, body, carry)


def attend(own, meta, query, buf, offs, *earlier):
    rows = query.shape[0]
    groups = H // KV
    half = rows // 2
    blocks, padded, wide = buf.shape
    span = groups * HD
    width = groups * half
    keys = blocks * rows
    steps = 2 * blocks // CHUNK_BLOCKS + 1
    which = (lambda m: m[0]) if own else (lambda m: 1 - m[0])
    head = lambda i, m: (0, which(m))
    return pl.pallas_call(
        functools.partial(attend_kernel, 4 if own else 4 + 2 * blocks, len(earlier)),
        grid_spec=pltpu.PrefetchScalarGridSpec(
            num_scalar_prefetch=1,
            grid=(1,),
            in_specs=[
                pl.BlockSpec((rows, span), head),
                fixed((blocks, padded, wide)),
                fixed((8, width)),
            ]
            + [pl.BlockSpec(memory_space=pl.ANY) for _ in earlier],
            out_specs=[
                pl.BlockSpec((rows, span), head),
                fixed((2, HD, width)),
                fixed((2, 8, width)),
            ],
            scratch_shapes=[
                pltpu.VMEM((keys, HD), bf16),
                pltpu.VMEM((keys, HD), bf16),
                pltpu.VMEM((2, width, HD), bf16),
                pltpu.VMEM((steps, 8, width), f32),
                pltpu.VMEM((steps, 8, width), f32),
                pltpu.VMEM((steps, HD, width), f32),
            ],
        ),
        out_shape=[
            jax.ShapeDtypeStruct((rows, H * HD), bf16),
            jax.ShapeDtypeStruct((2, HD, width), f32),
            jax.ShapeDtypeStruct((2, 8, width), f32),
        ],
        input_output_aliases={4: 0} if earlier else {},
        compiler_params=params(20 + blocks * rows * HD // 2**16),
        cost_estimate=cost(
            rows * keys * H * HD, blocks * padded * wide * 2, rows * keys * H // 4
        ),
        name="attend",
    )(meta, query, buf, offs, *earlier)


def attend_back_kernel(
    at,
    unread,
    meta_ref,
    q_ref,
    do_ref,
    buf_ref,
    offs_ref,
    attt_ref,
    lse_ref,
    cos_ref,
    sin_ref,
    *refs,
):
    (
        dq_ref,
        dbuf_ref,
        keys_ref,
        vals_ref,
        dkeys_ref,
        dvals_ref,
        query_ref,
        grad_ref,
        delta_ref,
        dquery_ref,
    ) = refs[unread:]
    blocks = buf_ref.shape[0]
    half = q_ref.shape[0] // 2
    groups = q_ref.shape[1] // HD
    chunk = CHUNK_BLOCKS * half
    scale = 1.0 / math.sqrt(HD)
    factor = LOG2E * scale
    count = 2 * blocks // CHUNK_BLOCKS - 1
    place_keys(meta_ref, at, buf_ref, keys_ref, vals_ref, half, blocks)
    dkeys_ref[...] = jnp.zeros_like(dkeys_ref)
    dvals_ref[...] = jnp.zeros_like(dvals_ref)
    dquery_ref[...] = jnp.zeros_like(dquery_ref)
    for part in range(2):
        query_ref[part] = stack_heads(q_ref, part, half, groups)
        grad = stack_heads(do_ref, part, half, groups)
        grad_ref[part] = grad
        delta = jnp.sum(grad.astype(f32).T * attt_ref[part], axis=0, keepdims=True)
        delta_ref[part] = jnp.broadcast_to(delta, delta_ref.shape[1:])
    full = [lax.div(meta_ref[1 + part], CHUNK_BLOCKS) for part in range(2)]

    def step(part, j, edge):
        rows = pl.ds(pl.multiple_of(j * chunk, 16), chunk)
        keys = keys_ref[rows, :]
        query, grad = query_ref[part], grad_ref[part]
        scores = dot_nt(keys, query)
        weights = jnp.exp2(scores * factor - lse_ref[part, 0:1, :])
        if edge is not None:
            row = lax.broadcasted_iota(jnp.int32, scores.shape, 0) + (j * chunk - edge * half)
            weights = jnp.where(row <= offs_ref[0:1, :], weights, 0.0)
        dweights = dot_nt(vals_ref[rows, :], grad)
        dscores = (weights * (dweights - delta_ref[part, 0:1, :])).astype(bf16)
        dvals_ref[rows, :] += dot(weights.astype(bf16), grad)
        dkeys_ref[rows, :] += dot(dscores, query)
        dquery_ref[part] += dot_tn(keys, dscores)

    def full_step(n):
        late = n >= full[0]
        step(jnp.where(late, 1, 0), n - jnp.where(late, full[0], 0), None)

    for_steps(count, full_step)
    for part in range(2):
        step(part, full[part], meta_ref[1 + part])
    for part in range(2):
        rowwise = dquery_ref[part].T * scale
        these = slice(part * half, (part + 1) * half)
        for g in range(groups):
            turned = turn(rowwise[g * half : (g + 1) * half], cos_ref[these], -sin_ref[these])
            dq_ref[these, g * HD : (g + 1) * HD] = turned.astype(bf16)

    for block in range(blocks):
        for part in range(2):
            rows = pl.ds(pl.multiple_of(meta_ref[at + block * 2 + part] * half, 16), half)
            here = slice(part * half, (part + 1) * half)
            dbuf_ref[block, here, :HD] = (dkeys_ref[rows, :] * scale).astype(bf16)
            dbuf_ref[block, here, HD:] = dvals_ref[rows, :].astype(bf16)


def attend_back(own, meta, query, grad, buf, offs, attt, lse, cos, sin, *earlier):
    rows = query.shape[0]
    groups = H // KV
    half = rows // 2
    blocks, padded, wide = buf.shape
    span = groups * HD
    width = groups * half
    keys = blocks * rows
    which = (lambda m: m[0]) if own else (lambda m: 1 - m[0])
    head = lambda i, m: (0, which(m))
    need = blocks * rows * (2 * HD * 2 + 2 * HD * 4 + 3 * wide * 2)
    return pl.pallas_call(
        functools.partial(attend_back_kernel, 4 if own else 4 + 2 * blocks, len(earlier)),
        grid_spec=pltpu.PrefetchScalarGridSpec(
            num_scalar_prefetch=1,
            grid=(1,),
            in_specs=[
                pl.BlockSpec((rows, span), head),
                pl.BlockSpec((rows, span), head),
                fixed((blocks, padded, wide)),
                fixed((8, width)),
                fixed((2, HD, width)),
                fixed((2, 8, width)),
                fixed((rows, HD)),
                fixed((rows, HD)),
            ]
            + [pl.BlockSpec(memory_space=pl.ANY) for _ in earlier],
            out_specs=[pl.BlockSpec((rows, span), head), fixed((blocks, rows, wide))],
            scratch_shapes=[
                pltpu.VMEM((keys, HD), bf16),
                pltpu.VMEM((keys, HD), bf16),
                pltpu.VMEM((keys, HD), f32),
                pltpu.VMEM((keys, HD), f32),
                pltpu.VMEM((2, width, HD), bf16),
                pltpu.VMEM((2, width, HD), bf16),
                pltpu.VMEM((2, 8, width), f32),
                pltpu.VMEM((2, HD, width), f32),
            ],
        ),
        out_shape=[
            jax.ShapeDtypeStruct((rows, H * HD), bf16),
            jax.ShapeDtypeStruct((blocks, rows, wide), bf16),
        ],
        input_output_aliases={9: 0} if earlier else {},
        compiler_params=params(24 + need // 2**20),
        cost_estimate=cost(
            2.5 * rows * keys * H * HD, blocks * padded * wide * 4, rows * keys * H // 4
        ),
        name="attend_back",
    )(meta, query, grad, buf, offs, attt, lse, cos, sin, *earlier)


def expert_kernel(
    plane,
    meta_ref,
    mine_ref,
    theirs_ref,
    dy_mine_ref,
    dy_theirs_ref,
    wg_ref,
    wu_ref,
    wd_ref,
    wr_ref,
    out_mine_ref,
    out_theirs_ref,
    dx_mine_ref,
    dx_theirs_ref,
    hidden_ref,
    dhid_ref,
    gate_ref,
):
    core = meta_ref[0]
    expert = meta_ref[1]
    rows, half = mine_ref.shape[2], mine_ref.shape[3]
    here = pl.ds(pl.multiple_of(core * half, LANES), half)
    there = pl.ds(pl.multiple_of((1 - core) * half, LANES), half)
    x_mine = mine_ref[0].reshape(2 * rows, half)
    x_theirs = jnp.concatenate([theirs_ref[0, 1], theirs_ref[0, 0]], axis=0)
    gate_pre = dot(x_mine, wg_ref[here, :]) + dot(x_theirs, wg_ref[there, :])
    up_pre = dot(x_mine, wu_ref[here, :]) + dot(x_theirs, wu_ref[there, :])
    logits = dot(x_mine, wr_ref[here, :]) + dot(x_theirs, wr_ref[there, :])
    marked = dy_mine_ref[0].reshape(2 * rows, half + LANES)
    dy_here = marked[:, :half].astype(f32)
    dy_there = jnp.concatenate(
        [dy_theirs_ref[0, 1, :, :half], dy_theirs_ref[0, 0, :, :half]], axis=0
    ).astype(f32)
    chosen = marked[:, half:].astype(f32) > 0.5
    top = jnp.max(jnp.where(chosen, logits, negative), axis=-1, keepdims=True)
    shares = jnp.where(chosen, jnp.exp(logits - top), 0.0)
    lane = lax.broadcasted_iota(jnp.int32, logits.shape, 1)
    own = jnp.sum(jnp.where(lane == expert, shares, 0.0), axis=-1, keepdims=True)
    gate = own / jnp.sum(shares, axis=-1, keepdims=True)
    routed = jnp.sum(jnp.where((lane == expert) & chosen, 1.0, 0.0), axis=-1, keepdims=True)
    gate_ref[...] = jnp.broadcast_to(gate, gate_ref.shape)

    sig = jax.nn.sigmoid(gate_pre)
    silu = gate_pre * sig
    hidden = (silu * up_pre).astype(bf16)
    hidden_ref[...] = hidden
    result_here = dot(hidden, wd_ref[:, here]).astype(bf16).astype(f32)
    result_there = dot(hidden, wd_ref[:, there]).astype(bf16).astype(f32)
    d_gate = routed * (
        jnp.sum(dy_here * result_here, axis=-1, keepdims=True)
        + jnp.sum(dy_there * result_there, axis=-1, keepdims=True)
    )
    out_here = (gate * result_here).astype(bf16)
    out_there = (gate * result_there).astype(bf16)
    d_hidden = dot_nt((gate * dy_here).astype(bf16), wd_ref[:, here]) + dot_nt(
        (gate * dy_there).astype(bf16), wd_ref[:, there]
    )
    d_up = (d_hidden * silu).astype(bf16)
    d_gp = (d_hidden * up_pre * (sig * (1.0 + gate_pre * (1.0 - sig)))).astype(bf16)
    inner = d_gp.shape[1]
    dhid_ref[:, :inner] = d_gp
    dhid_ref[:, inner:] = d_up
    high = d_gate.astype(bf16).astype(f32)
    low = d_gate - high
    spot = jnp.where(lane == expert, 1.0, 0.0)
    dx_here = (dot_nt(d_gp, wg_ref[here, :]) + dot_nt(d_up, wu_ref[here, :])).astype(bf16)
    dx_there = (dot_nt(d_gp, wg_ref[there, :]) + dot_nt(d_up, wu_ref[there, :])).astype(bf16)
    col_here = (spot * jnp.where(core == 0, high, low)).astype(bf16)
    col_there = (spot * jnp.where(core == 0, low, high)).astype(bf16)
    for t in range(2):
        these = slice(t * rows, (t + 1) * rows)
        dx_mine_ref[0, t, :, :half] = dx_here[these]
        dx_mine_ref[0, t, :, half:] = col_here[these]
        dx_theirs_ref[0, 1 - t, :, :half] = dx_there[these]
        dx_theirs_ref[0, 1 - t, :, half:] = col_there[these]
        out_mine_ref[0, t] = out_here[these]
        out_theirs_ref[0, 1 - t] = out_there[these]


def run_expert(plane, first, meta, mine, theirs, dy_mine, dy_theirs, wg, wu, wd, wr):
    chips, _, rows, half = mine.shape
    width, inner = wg.shape
    swap = lambda g: plane.swapped(g + first) - first
    pair = lambda w: pl.BlockSpec((1, 2, rows, w), lambda g, m: (g, 0, 0, 0))
    swapped = lambda w: pl.BlockSpec((1, 2, rows, w), lambda g, m: (swap(g), 0, 0, 0))
    flat = lambda w: pl.BlockSpec((2 * rows, w), lambda g, m: (g, 0))
    total_rows = chips * 2 * rows
    return pl.pallas_call(
        functools.partial(expert_kernel, plane),
        grid_spec=pltpu.PrefetchScalarGridSpec(
            num_scalar_prefetch=1,
            grid=(chips,),
            in_specs=[
                pair(half),
                swapped(half),
                pair(half + LANES),
                swapped(half + LANES),
                fixed((width, inner)),
                fixed((width, inner)),
                fixed((inner, width)),
                fixed((width, wr.shape[1])),
            ],
            out_specs=[
                pair(half),
                swapped(half),
                pair(half + LANES),
                swapped(half + LANES),
                flat(inner),
                flat(2 * inner),
                flat(LANES),
            ],
        ),
        out_shape=[
            jax.ShapeDtypeStruct((chips, 2, rows, half), bf16),
            jax.ShapeDtypeStruct((chips, 2, rows, half), bf16),
            jax.ShapeDtypeStruct((chips, 2, rows, half + LANES), bf16),
            jax.ShapeDtypeStruct((chips, 2, rows, half + LANES), bf16),
            jax.ShapeDtypeStruct((total_rows, inner), bf16),
            jax.ShapeDtypeStruct((total_rows, 2 * inner), bf16),
            jax.ShapeDtypeStruct((total_rows, LANES), f32),
        ],
        compiler_params=params(36),
        cost_estimate=cost(
            12 * total_rows * width * inner, 20 * total_rows * width, total_rows * inner
        ),
        name="expert",
    )(meta, mine, theirs, dy_mine, dy_theirs, wg, wu, wd, wr)


def rows_in_order(plane, own0, own, other0, other, mine):
    if mine:
        return [ref[g, t] for ref in (own0, own) for g in range(ref.shape[0]) for t in range(2)]
    parts = [other0[0, 1], other0[0, 0]]
    for g in range(1, plane.chips):
        at = plane.swapped(g) - 1
        parts += [other[at, 1], other[at, 0]]
    return parts


def expert_grad_kernel(plane, weigh, meta_ref, *refs):
    lefts, refs = refs[:4], refs[4:]
    if weigh:
        gate0_ref, gate_ref, right0_ref, right_ref, _, out_ref = refs
    else:
        right0_ref, right_ref, out_ref = refs
    step = pl.program_id(0)
    halves = pl.num_programs(0) // 2
    first = right0_ref.shape[0]

    def give(parts):
        if weigh:
            rows = parts[0].shape[0]
            gates = [gate0_ref[t * rows : (t + 1) * rows, 0:1] for t in range(2)]
            gates += [
                gate_ref[n * rows : (n + 1) * rows, 0:1] for n in range(len(parts) - 2)
            ]
            parts = [(g * p.astype(f32)).astype(bf16) for g, p in zip(gates, parts)]
        near = jnp.concatenate(parts[:2], axis=0)
        far = jnp.concatenate(parts[2:], axis=0)
        out_ref[...] = (dot_tn(near, right0_ref[...]) + dot_tn(far, right_ref[...])).astype(bf16)

    @pl.when(step < halves)
    def _():
        give(rows_in_order(plane, *lefts, True))

    @pl.when(step >= halves)
    def _():
        give(rows_in_order(plane, *lefts, False))


def expert_grad(plane, meta, lefts, right0, right, half, gates=None, grads=None):
    tile = half // 2
    rows = lefts[0].shape[2]
    inner = right.shape[1]
    own = lambda a: pl.BlockSpec(
        a.shape[:3] + (tile,), lambda i, m: (0, 0, 0, jnp.minimum(i, 1))
    )
    other = lambda a: pl.BlockSpec(
        a.shape[:3] + (tile,), lambda i, m: (0, 0, 0, jnp.maximum(i - 2, 0))
    )
    count = right0.shape[0] + right.shape[0]
    need = count * (8 * tile * 2 + inner * 2) + 3 * tile * inner * 4
    specs = [own(lefts[0]), own(lefts[1]), other(lefts[2]), other(lefts[3])]
    args = list(lefts)
    if gates:
        specs += [fixed(g.shape) for g in gates]
        args += list(gates)
    specs += [fixed(right0.shape), fixed(right.shape)]
    args += [right0, right]
    if gates:
        specs.append(pl.BlockSpec(memory_space=pl.ANY))
        args.append(grads)
        need += count * LANES * 4
        out_shape, place = grads.shape, 2
    else:
        out_shape, place = (2 * half, inner + inner // 2), 0
    return pl.pallas_call(
        functools.partial(expert_grad_kernel, plane, bool(gates)),
        grid_spec=pltpu.PrefetchScalarGridSpec(
            num_scalar_prefetch=1,
            grid=(4,),
            in_specs=specs,
            out_specs=pl.BlockSpec(
                (tile, inner), lambda i, m: ((m[0] ^ (i // 2)) * 2 + i % 2, place)
            ),
        ),
        out_shape=jax.ShapeDtypeStruct(out_shape, bf16),
        input_output_aliases={len(args): 0} if gates else {},
        compiler_params=params(8 + need // 2**20),
        cost_estimate=cost(4 * count * half * inner, 6 * count * half),
        name="down_grad" if gates else "up_grad",
    )(meta, *args)


def together(*values):
    return lax.optimization_barrier(values)


def per_device(
    tokens,
    gain_attn,
    w_query,
    w_key,
    w_value,
    w_out,
    gain_moe,
    w_router,
    w_gate,
    w_up,
    w_down,
    routes,
    positions,
    cotangent,
):
    rows = tokens.shape[1]
    width = tokens.shape[2]
    half = rows // 2
    split = width // 2
    groups = H // KV
    kv_width = KV * HD
    experts = w_router.shape[1]
    inner = w_gate.shape[2]
    plane = Plane(w_gate.shape[0] * lax.axis_size("expert"))
    last = plane.steps - 1
    contexts = lax.axis_size("context")
    copies = lax.axis_size("dp")
    blocks = plane.size * contexts
    index = lax.axis_index("expert")
    core = index % 2
    places = positions[0]
    x = tokens[0]
    gain_one, gain_two = gain_attn, gain_moe
    swap_context = [(i, i ^ 1) for i in range(contexts)]
    swap_copies = [(i, i ^ 1) for i in range(copies)]

    def by_core(zero, one):
        return jnp.where(core == 0, zero, one)

    def mix(value, k):
        return lax.ppermute(value, "expert", plane.mixed[k])

    def sibling(value):
        return lax.ppermute(value, "expert", plane.sibling)

    tcos, tsin = rope_tables(2 * blocks, half)
    own_bases = jnp.stack([places[0], places[half]]) // half
    front_meta = jnp.concatenate([core[None], own_bases]).astype(jnp.int32)
    core_row = jnp.reshape(core, (1,)).astype(jnp.int32)
    xn_one, packed, cos, sin = front(
        core_row, places, x, gain_one, w_key, w_value, tcos, tsin
    )

    lanes = jnp.arange(LANES, dtype=jnp.int32)
    marks = jnp.any(routes[0][:, :, None] == lanes[None, None, :], axis=1).astype(bf16)
    dy, marks = after(cotangent[0], packed), after(marks, packed)
    dy_keep = jnp.concatenate([by_core(dy[:, :split], dy[:, split:]), marks], axis=1)
    dy_send = jnp.concatenate([by_core(dy[:, split:], dy[:, :split]), marks], axis=1)

    router_wide = jnp.pad(w_router, ((0, 0), (0, LANES - experts)))
    weights = (w_gate[0], w_up[0], w_down[0], router_wide)
    dy_m0 = jnp.stack([dy_keep, sibling(dy_send)])[None]
    dy_t0 = jnp.stack([sibling(dy_keep), dy_send])[None]
    if contexts > 1:
        arrived = lax.ppermute(packed, "context", swap_context)
        arrived, dy_m0, dy_t0, front_meta = together(arrived, dy_m0, dy_t0, front_meta)
        packed = jnp.stack([packed, arrived], axis=1)
    else:
        packed = packed[:, None]
    held = jnp.stack([packed[0], sibling(packed[1])])[None]
    query = make_query(xn_one, w_query, cos, sin)
    for k in range(plane.steps):
        if k == last:
            held, query = together(held, query)
        held = jnp.concatenate([held, mix(held, k)])
    mine = held.reshape(blocks, rows + PAD_ROWS, kv_width)
    theirs = sibling(held).reshape(blocks, rows + PAD_ROWS, kv_width)
    own_order = mine[:, rows :: PAD_ROWS // 2, 0].astype(f32).astype(jnp.int32).reshape(-1)
    spots = [
        ((plane.swapped(g) * 2 + 1 - t) * contexts + c) * 2 + part
        for g in range(plane.chips)
        for t in range(2)
        for c in range(contexts)
        for part in range(2)
    ]
    other_order = jnp.stack([own_order[spot] for spot in spots])
    meta = jnp.concatenate([front_meta, front_meta[:1], own_order, other_order])
    offs = jnp.asarray(np.tile(np.arange(groups * half, dtype=np.int32) % half, (8, 1)))

    dy_held, meta = together(dy_m0, meta)
    dy_came = mix(dy_held, 0)
    attended, *own_stats = attend(True, meta, query, mine, offs)
    dy_came, theirs, attended = together(dy_came, theirs, attended)
    dy_held = jnp.concatenate([dy_held, dy_came])
    for k in range(1, last):
        dy_held = jnp.concatenate([dy_held, mix(dy_held, k)])
    dy_held, attended = together(dy_held, attended)
    dy_came = mix(dy_held, last)
    attended, *other_stats = attend(False, meta, query, theirs, offs, attended)
    hidden, xn_two, keep, send = join(front_meta, attended, w_out, x, gain_two)

    offsets = np.array(
        [[plane.chip_offset(c, g) // 2 for g in range(plane.chips)] for c in range(2)], np.int32
    )
    chips = (index // 2) ^ by_core(offsets[0], offsets[1])
    expert_meta = jnp.concatenate([core[None], index[None], chips]).astype(jnp.int32)
    mine0 = jnp.stack([keep, sibling(send)])[None]
    theirs0 = jnp.stack([sibling(keep), send])[None]
    held = mine0
    for k in range(plane.steps):
        came = mix(held, k)
        if k == last - 1:
            came, dy_came = together(came, dy_came)
        if k == last:
            out_m0, out_t0, dx_m0, dx_t0, hid0, dhid0, gate0 = run_expert(
                plane, 0, expert_meta, after(mine0, held), theirs0, dy_m0, dy_t0, *weights
            )
            dy_m1 = jnp.concatenate([dy_held, dy_came])[1:]
            dy_t1 = sibling(dy_m1)
            came, hid0, dy_t1 = together(came, hid0, dy_t1)
        held = jnp.concatenate([held, came])
    mine1 = held[1:]
    theirs1 = sibling(mine1)
    out_m1, out_t1, dx_m1, dx_t1, hid1, dhid1, gate1 = run_expert(
        plane, 1, expert_meta, mine1, theirs1, dy_m1, dy_t1, *weights
    )

    def pick(terms, k):
        lo, hi = 2**k, 2 ** (k + 1)
        return total([a[lo - at : hi - at] for at, a in terms if at <= lo and hi - at <= a.shape[0]])

    def parts_of(terms, slot):
        return total([a[0, slot] for at, a in terms if at == 0])

    dx_r0, dx_r1 = sibling(dx_t0), sibling(dx_t1)
    grads = expert_grad(
        plane, expert_meta, (mine0, mine1, theirs0, theirs1), dhid0, dhid1, split
    )
    dx_r1, grads = together(dx_r1, grads)
    terms = [(0, dx_m0), (1, dx_m1), (0, dx_r0), (1, dx_r1)]
    for k in reversed(range(plane.steps)):
        send = pick(terms, k)
        arrived = mix(send, k)
        if k == last:
            grads = expert_grad(
                plane,
                expert_meta,
                (dy_m0, dy_m1, dy_t0, dy_t1),
                after(hid0, send),
                hid1,
                split,
                (gate0, gate1),
                grads,
            )
            arrived, grads = together(arrived, grads)
        terms.append((0, arrived))
    expert_grads = lax.psum_scatter(grads, ("context", "dp"), scatter_dimension=0, tiled=True)
    dx_keep = parts_of(terms, 0)
    dx_other = sibling(parts_of(terms, 1))

    marked = jnp.concatenate([dy, marks], axis=1)
    d_state, d_low, d_logits, d_gain_moe, d_attended = middle(
        front_meta,
        dx_keep,
        dx_other,
        hidden,
        xn_two,
        gain_two,
        marked,
        router_wide,
        w_out,
    )
    d_query, d_theirs = attend_back(
        False, meta, query, d_attended, theirs, offs, *other_stats, cos, sin
    )
    d_sent = sibling(d_theirs)
    d_query, d_mine = attend_back(
        True, meta, query, d_attended, mine, offs, *own_stats, cos, sin, d_query
    )

    custom = contexts == 2 and copies == 2 and (width // plane.chips) % LANES == 0
    kv_shape = (plane.chips, 2, contexts, rows, kv_width)
    terms = [(0, d_mine.reshape(kv_shape)), (0, d_sent.reshape(kv_shape))]
    xn_other = sibling(xn_one)
    for k in reversed(range(plane.steps)):
        send = pick(terms, k)
        arrived = mix(send, k)
        if k == last and custom:
            place = lax.axis_index("context") * 2 + lax.axis_index("dp")
            dense_meta = jnp.concatenate([core[None], place[None], chips]).astype(jnp.int32)
            d_query = after(d_query, send)
            left, right = by_core(xn_one, d_low), by_core(d_query, attended)
            sends = by_core(jnp.stack([d_low, attended]), jnp.stack([xn_one, d_query]))
            sends = sibling(sends)
            *steps, own = dense_grad(plane, dense_meta, left, sends[0], right, sends[1])
            arrived, steps, own = together(arrived, steps, own)
        if k == 0:
            dxq = times_transposed(after(d_query, send), w_query)
            arrived, dxq = together(arrived, dxq)
        terms.append((0, arrived))
    dkv_keep = parts_of(terms, 0)
    dkv_other = sibling(parts_of(terms, 1))
    dkv = jnp.stack([dkv_keep, dkv_other], axis=1)
    if custom:
        came = [mix(steps[last], last)]
    out_t0, out_t1, dkv = together(out_t0, out_t1, dkv)
    out_terms = [(0, out_m0), (1, out_m1), (0, sibling(out_t0)), (1, sibling(out_t1))]
    out_send = pick(out_terms, last)
    if contexts > 1:
        dkv_came = lax.ppermute(dkv[1], "context", swap_context)
        dkv_came, out_send = together(dkv_came, out_send)
        if custom:
            for k in reversed(range(last)):
                send = total([steps[k]] + [a[2**k : 2 ** (k + 1)] for a in came])
                dkv_came, send = together(dkv_came, send)
                came.append(mix(send, k))
        dkv = dkv[0].astype(f32) + dkv_came.astype(f32)
    else:
        dkv = dkv[0].astype(f32)

    d_in, d_kv, d_gain_attn = back(
        front_meta, dkv[0], dkv[1], dxq, x, gain_one, d_state, w_key, w_value, cos, sin
    )

    if custom:
        d_own = by_core(d_kv[:, :kv_width], d_kv[:, kv_width:])
        d_sends = sibling(by_core(d_kv[:, kv_width:], d_kv[:, :kv_width]))
        *small_steps, small_own = dense_grad(
            plane,
            dense_meta,
            xn_one,
            xn_other,
            d_own,
            d_sends,
            (xn_two, d_logits, d_gain_attn, d_gain_moe),
        )
        small_came = []
        for k in reversed(range(plane.steps)):
            send = total([small_steps[k]] + [a[2**k : 2 ** (k + 1)] for a in small_came])
            small_came.append(mix(send, k))
        if SCATTER_TIE == 1:
            small_came[-1], expert_grads = together(small_came[-1], expert_grads)
        came[-1], small_came[-1] = together(came[-1], small_came[-1])
        wide = [own[0]] + [a[0] for a in came]
        small = [small_own[0]] + [a[0] for a in small_came]

    def reduce_output(send):
        for k in reversed(range(plane.steps)):
            if k < last:
                send = pick(out_terms, k)
            out_terms.append((0, mix(send, k)))
        keep, other = parts_of(out_terms, 0), sibling(parts_of(out_terms, 1))
        mixture = jnp.concatenate([by_core(keep, other), by_core(other, keep)], axis=1)
        return (hidden + mixture.astype(f32)).astype(bf16)[None]

    def split_grads(grads):
        return (
            grads[:, :inner].astype(f32)[None],
            grads[:, inner : 2 * inner].astype(f32)[None],
            grads[:, 2 * inner :].astype(f32).T[None],
        )

    if custom:
        for n, (axis, pairs) in enumerate((("dp", swap_copies), ("context", swap_context))):
            send = jnp.concatenate([total([a[1] for a in v]) for v in (wide, small)], -1)
            if n == 0:
                out_send, send = together(out_send, send)
            arrived = lax.ppermute(send, axis, pairs)
            wide = [a[0] for a in wide] + [arrived[..., :width]]
            small = [a[0] for a in small] + [arrived[..., width:]]
        output = reduce_output(out_send)
        grad_gate, grad_up, grad_down = split_grads(expert_grads)
        wide[-1], grad_gate, grad_up, grad_down, output = together(
            wide[-1], grad_gate, grad_up, grad_down, output
        )
        send = jnp.concatenate([total([a[1] for a in v]) for v in (wide, small)], -1)
        arrived = sibling(send).astype(f32)
        second = [arrived[:, :width], arrived[:, width:]]
        first = [sum(a[0].astype(f32) for a in v) for v in (wide, small)]
        grad_query, grad_out = by_core(first[0], second[0]), by_core(second[0], first[0])
        grad_key = by_core(first[1], second[1])[:, :kv_width]
        grad_value = by_core(second[1], first[1])[:, :kv_width]
        extra = first[1][:, kv_width:] + second[1][:, kv_width:]
    else:
        output = reduce_output(out_send)
        grad_gate, grad_up, grad_down = split_grads(expert_grads)
        scatter = lambda v: lax.psum_scatter(
            v.astype(bf16), ("expert", "context", "dp"), scatter_dimension=0, tiled=True
        ).astype(f32)
        grad_query = scatter(dot_tn(xn_one, d_query))
        grad_out = scatter(dot_tn(d_low, attended))
        grad_kv = scatter(dot_tn(xn_one, d_kv))
        grad_key, grad_value = grad_kv[:, :kv_width], grad_kv[:, kv_width:]
        router = dot_tn(xn_two, d_logits)[:, : LANES - 2]
        extra = scatter(
            jnp.concatenate([router, d_gain_attn[:1].T, d_gain_moe[:1].T], axis=1)
        )
    return (
        output,
        d_in[None],
        extra[:, LANES - 2],
        grad_query,
        grad_key,
        grad_value,
        grad_out.T,
        extra[:, LANES - 1],
        extra[:, :experts],
        grad_gate,
        grad_up,
        grad_down,
    )


def solution(mesh):
    in_specs = (
        P("dp", ("expert", "context"), None),
        P(),
        P(),
        P(),
        P(),
        P(),
        P(),
        P(),
        P("expert", None, None),
        P("expert", None, None),
        P("expert", None, None),
        P("dp", ("expert", "context"), None),
        P("dp", ("expert", "context")),
        P("dp", ("expert", "context"), None),
    )
    out_specs = (
        P("dp", ("expert", "context"), None),
        P("dp", ("expert", "context"), None),
        P(("expert", "context", "dp")),
        P(("expert", "context", "dp"), None),
        P(("expert", "context", "dp"), None),
        P(("expert", "context", "dp"), None),
        P(None, ("expert", "context", "dp")),
        P(("expert", "context", "dp")),
        P(("expert", "context", "dp"), None),
        P("expert", ("context", "dp"), None),
        P("expert", ("context", "dp"), None),
        P("expert", None, ("context", "dp")),
    )
    return jax.shard_map(
        per_device, mesh=mesh, in_specs=in_specs, out_specs=out_specs, check_vma=False
    )
```

```python
import functools
import math

import jax
import jax.numpy as jnp
import numpy as np
from jax import lax
from jax.experimental import pallas as pl
from jax.experimental.pallas import tpu as pltpu
from jax.sharding import PartitionSpec as P

H = 12
KV = 2
HD = 128
TOP = 4

eps = 1e-06
rope_base = 1000000.0
negative = -1e30
LANES = 128
JOIN_TILES = 3
CHUNK_BLOCKS = 8
PAD_ROWS = 16
bf16 = jnp.bfloat16
f32 = jnp.float32
LOG2E = 1.4426950408889634


def dot(a, b):
    return lax.dot_general(a, b, (((1,), (0,)), ((), ())), preferred_element_type=f32)


def dot_nt(a, b):
    return lax.dot_general(a, b, (((1,), (1,)), ((), ())), preferred_element_type=f32)


def dot_tn(a, b):
    return lax.dot_general(a, b, (((0,), (0,)), ((), ())), preferred_element_type=f32)


def params(mebibytes):
    return pltpu.CompilerParams(
        dimension_semantics=("arbitrary",), vmem_limit_bytes=min(int(mebibytes), 60) * 1024 * 1024
    )


def after(value, *others):
    return lax.optimization_barrier((value,) + others)[0]


def cost(flops, moved, exps=0):
    return pl.CostEstimate(flops=int(flops), bytes_accessed=int(moved), transcendentals=int(exps))


def turn(values, cos, sin):
    return values * cos + pltpu.roll(values, HD // 2, 1) * sin


def norm_scale(values):
    return lax.rsqrt(jnp.mean(values * values, axis=-1, keepdims=True) + eps)


def rope_tables(count, half):
    freqs = rope_base ** (-np.arange(0, HD, 2) / HD)
    angles = np.concatenate([np.arange(count) * half, np.arange(half)])[:, None] * freqs[None, :]
    twice = np.concatenate([angles, angles], axis=1)
    return jnp.asarray(np.cos(twice), f32), jnp.asarray(np.sin(twice), f32)


def fixed(shape):
    zeros = (0,) * len(shape)
    return pl.BlockSpec(shape, lambda *_: zeros, pipeline_mode=pl.Buffered(1))


def front_kernel(
    core_ref,
    places_ref,
    x_ref,
    gain_ref,
    wk_ref,
    wv_ref,
    tcos_ref,
    tsin_ref,
    xn_ref,
    packed_ref,
    cos_ref,
    sin_ref,
):
    core = core_ref[0]
    rows = x_ref.shape[0]
    half = rows // 2
    bases = [lax.div(places_ref[part * half], half) for part in range(2)]
    count = tcos_ref.shape[0] - half
    sign = jnp.where(lax.broadcasted_iota(jnp.int32, (half, HD), 1) < HD // 2, -1.0, 1.0)
    for part in range(2):
        these = slice(part * half, (part + 1) * half)
        base = pl.ds(bases[part], 1)
        cos_base, sin_base = tcos_ref[base, :], tsin_ref[base, :]
        cos_off, sin_off = tcos_ref[count:, :], tsin_ref[count:, :]
        cos_ref[these, :] = cos_base * cos_off - sin_base * sin_off
        sin_ref[these, :] = (sin_base * cos_off + cos_base * sin_off) * sign
    values = x_ref[...].astype(f32)
    normed = (values * norm_scale(values) * gain_ref[...]).astype(bf16)
    xn_ref[...] = normed
    keys = dot(normed, wk_ref[...])
    vals = dot(normed, wv_ref[...]).astype(bf16)
    edge = lax.broadcasted_iota(jnp.int32, (PAD_ROWS, 2 * HD), 0) < PAD_ROWS // 2
    tail = jnp.where(edge, bases[0].astype(f32), bases[1].astype(f32)).astype(bf16)
    for head in range(KV):
        slot = jnp.where(core == head, 0, 1)
        span = slice(head * HD, (head + 1) * HD)
        turned = turn(keys[:, span], cos_ref[...], sin_ref[...]).astype(bf16)
        packed_ref[slot, :rows, :HD] = turned
        packed_ref[slot, :rows, HD:] = vals[:, span]
        packed_ref[slot, rows:, :] = tail


def front(core, places, x, gain, wk, wv, tcos, tsin):
    rows, width = x.shape
    return pl.pallas_call(
        front_kernel,
        grid_spec=pltpu.PrefetchScalarGridSpec(
            num_scalar_prefetch=2,
            grid=(1,),
            in_specs=[fixed(a.shape) for a in (x, gain, wk, wv, tcos, tsin)],
            out_specs=[
                fixed((rows, width)),
                fixed((2, rows + PAD_ROWS, 2 * HD)),
                fixed((rows, HD)),
                fixed((rows, HD)),
            ],
        ),
        out_shape=[
            jax.ShapeDtypeStruct((rows, width), bf16),
            jax.ShapeDtypeStruct((2, rows + PAD_ROWS, 2 * HD), bf16),
            jax.ShapeDtypeStruct((rows, HD), f32),
            jax.ShapeDtypeStruct((rows, HD), f32),
        ],
        compiler_params=params(60),
        cost_estimate=cost(4 * rows * width * KV * HD, 8 * rows * width),
        name="front",
    )(core, places, x, gain, wk, wv, tcos, tsin)


def query_kernel(x_ref, w_ref, cos_ref, sin_ref, out_ref):
    raw = dot(x_ref[...], w_ref[...])
    for head in range(raw.shape[1] // HD):
        span = slice(head * HD, (head + 1) * HD)
        out_ref[:, span] = turn(raw[:, span], cos_ref[...], sin_ref[...]).astype(bf16)


def make_query(x, w, cos, sin):
    rows, width = x.shape
    wide = w.shape[1]
    tile = 4 * HD
    return pl.pallas_call(
        query_kernel,
        grid=(wide // tile,),
        in_specs=[
            fixed((rows, width)),
            pl.BlockSpec((width, tile), lambda i: (0, i)),
            fixed((rows, HD)),
            fixed((rows, HD)),
        ],
        out_specs=pl.BlockSpec((rows, tile), lambda i: (0, i)),
        out_shape=jax.ShapeDtypeStruct((rows, wide), bf16),
        compiler_params=params(12),
        cost_estimate=cost(2 * rows * width * wide, 2 * width * wide),
        name="make_query",
    )(x, w, cos, sin)


def join_kernel(meta_ref, mine_ref, theirs_ref, w_ref, x_ref, gain_ref, hid_ref, xn_ref, keep_ref, send_ref):
    core = meta_ref[0]
    step = pl.program_id(0)
    width = hid_ref.shape[1]
    tile = width // JOIN_TILES
    span = pl.ds(pl.multiple_of(step * tile, LANES), tile)
    inner = mine_ref.shape[1]
    here = pl.ds(pl.multiple_of(core * inner, LANES), inner)
    there = pl.ds(pl.multiple_of((1 - core) * inner, LANES), inner)
    mixed = dot(mine_ref[...], w_ref[here, :]) + dot(theirs_ref[...], w_ref[there, :])
    hid_ref[:, span] = x_ref[:, span].astype(f32) + mixed

    @pl.when(step == pl.num_programs(0) - 1)
    def _():
        hidden = hid_ref[...]
        xn_ref[...] = (hidden * norm_scale(hidden) * gain_ref[...]).astype(bf16)
        half = width // 2
        keep_ref[...] = xn_ref[:, pl.ds(pl.multiple_of(core * half, LANES), half)]
        send_ref[...] = xn_ref[:, pl.ds(pl.multiple_of((1 - core) * half, LANES), half)]


def join(meta, mine, theirs, w, x, gain):
    rows, width = x.shape
    inner = w.shape[0]
    tile = width // JOIN_TILES
    return pl.pallas_call(
        join_kernel,
        grid_spec=pltpu.PrefetchScalarGridSpec(
            num_scalar_prefetch=1,
            grid=(width // tile,),
            in_specs=[
                fixed(mine.shape),
                fixed(theirs.shape),
                pl.BlockSpec((inner, tile), lambda i, m: (0, i)),
                fixed((rows, width)),
                fixed((width,)),
            ],
            out_specs=[
                fixed((rows, width)),
                fixed((rows, width)),
                fixed((rows, width // 2)),
                fixed((rows, width // 2)),
            ],
        ),
        out_shape=[
            jax.ShapeDtypeStruct((rows, width), f32),
            jax.ShapeDtypeStruct((rows, width), bf16),
            jax.ShapeDtypeStruct((rows, width // 2), bf16),
            jax.ShapeDtypeStruct((rows, width // 2), bf16),
        ],
        compiler_params=params(16),
        cost_estimate=cost(2 * rows * width * inner, 2 * width * inner),
        name="join",
    )(meta, mine, theirs, w, x, gain)


def middle_kernel(
    meta_ref,
    own_ref,
    other_ref,
    hid_ref,
    xn_ref,
    gain_ref,
    dy_ref,
    wr_ref,
    w_ref,
    dstate_ref,
    dlow_ref,
    dlog_ref,
    dgain_ref,
    datt_ref,
    dx_ref,
):
    core = meta_ref[0]
    step = pl.program_id(0)
    width = hid_ref.shape[1]
    half = width // 2

    @pl.when(step == 0)
    def _():
        dx_ref[:, pl.ds(pl.multiple_of(core * half, LANES), half)] = own_ref[:, :half].astype(f32)
        dx_ref[:, pl.ds(pl.multiple_of((1 - core) * half, LANES), half)] = other_ref[
            :, :half
        ].astype(f32)
        d_gate = own_ref[:, half:].astype(f32) + other_ref[:, half:].astype(f32)
        chosen = dy_ref[:, width:].astype(f32) > 0.5
        logits = dot(xn_ref[...], wr_ref[...])
        top = jnp.max(jnp.where(chosen, logits, negative), axis=-1, keepdims=True)
        shares = jnp.where(chosen, jnp.exp(logits - top), 0.0)
        gate = shares / jnp.sum(shares, axis=-1, keepdims=True)
        inner_sum = jnp.sum(gate * d_gate, axis=-1, keepdims=True)
        d_logits = (gate * (d_gate - inner_sum)).astype(bf16)
        dlog_ref[...] = d_logits
        d_xn = dx_ref[...] + dot_nt(d_logits, wr_ref[...])
        hidden = hid_ref[...]
        scale_row = norm_scale(hidden)
        normed = hidden * scale_row
        dgain_ref[...] = jnp.broadcast_to(
            jnp.sum(d_xn * normed, axis=0, keepdims=True), dgain_ref.shape
        )
        scaled = d_xn * gain_ref[...]
        inner_mean = jnp.mean(scaled * normed, axis=-1, keepdims=True)
        d_state = dy_ref[:, :width].astype(f32) + scale_row * (scaled - normed * inner_mean)
        dstate_ref[...] = d_state
        dlow_ref[...] = d_state.astype(bf16)

    datt_ref[...] = dot_nt(dlow_ref[...], w_ref[...]).astype(bf16)


def middle(meta, own, other, hidden, xn, gain, dy, wr, w):
    rows, width = hidden.shape
    inner = w.shape[0]
    tile = inner // JOIN_TILES
    return pl.pallas_call(
        middle_kernel,
        grid_spec=pltpu.PrefetchScalarGridSpec(
            num_scalar_prefetch=1,
            grid=(inner // tile,),
            in_specs=[fixed(a.shape) for a in (own, other, hidden, xn, gain, dy, wr)]
            + [pl.BlockSpec((tile, width), lambda i, m: (i, 0))],
            out_specs=[
                fixed((rows, width)),
                fixed((rows, width)),
                fixed((rows, LANES)),
                fixed((8, width)),
                pl.BlockSpec((rows, tile), lambda i, m: (0, i)),
            ],
            scratch_shapes=[pltpu.VMEM((rows, width), f32)],
        ),
        out_shape=[
            jax.ShapeDtypeStruct((rows, width), f32),
            jax.ShapeDtypeStruct((rows, width), bf16),
            jax.ShapeDtypeStruct((rows, LANES), bf16),
            jax.ShapeDtypeStruct((8, width), f32),
            jax.ShapeDtypeStruct((rows, inner), bf16),
        ],
        compiler_params=params(20),
        cost_estimate=cost(2 * rows * width * inner, 2 * width * inner),
        name="middle",
    )(meta, own, other, hidden, xn, gain, dy, wr, w)


def times_kernel(meta_ref, mine_ref, theirs_ref, w_ref, out_ref):
    core = meta_ref[0]
    inner = mine_ref.shape[1]
    here = pl.ds(pl.multiple_of(core * inner, LANES), inner)
    there = pl.ds(pl.multiple_of((1 - core) * inner, LANES), inner)
    out_ref[...] = dot_nt(mine_ref[...], w_ref[:, here]) + dot_nt(theirs_ref[...], w_ref[:, there])


def times_transposed(meta, mine, theirs, w):
    rows = mine.shape[0]
    width, inner = w.shape
    tile = width // JOIN_TILES
    return pl.pallas_call(
        times_kernel,
        grid_spec=pltpu.PrefetchScalarGridSpec(
            num_scalar_prefetch=1,
            grid=(width // tile,),
            in_specs=[
                fixed(mine.shape),
                fixed(theirs.shape),
                pl.BlockSpec((tile, inner), lambda i, m: (i, 0)),
            ],
            out_specs=pl.BlockSpec((rows, tile), lambda i, m: (0, i)),
        ),
        out_shape=jax.ShapeDtypeStruct((rows, width), f32),
        compiler_params=params(12),
        cost_estimate=cost(2 * rows * width * inner, 2 * width * inner),
        name="times_transposed",
    )(meta, mine, theirs, w)


def back_kernel(
    meta_ref,
    own_ref,
    other_ref,
    dxq_ref,
    x_ref,
    gain_ref,
    dstate_ref,
    wk_ref,
    wv_ref,
    cos_ref,
    sin_ref,
    din_ref,
    dkv_ref,
    dgain_ref,
    pair_ref,
):
    core = meta_ref[0]
    pair_ref[core] = own_ref[...].astype(f32)
    pair_ref[1 - core] = other_ref[...].astype(f32)
    wide = KV * HD
    for head in range(KV):
        turned = turn(pair_ref[head, :, :HD], cos_ref[...], -sin_ref[...])
        dkv_ref[:, head * HD : (head + 1) * HD] = turned.astype(bf16)
        dkv_ref[:, wide + head * HD : wide + (head + 1) * HD] = pair_ref[head, :, HD:].astype(bf16)
    d_xn = (
        dxq_ref[...]
        + dot_nt(dkv_ref[:, :wide], wk_ref[...])
        + dot_nt(dkv_ref[:, wide:], wv_ref[...])
    )
    values = x_ref[...].astype(f32)
    scale_row = norm_scale(values)
    normed = values * scale_row
    dgain_ref[...] = jnp.broadcast_to(
        jnp.sum(d_xn * normed, axis=0, keepdims=True), dgain_ref.shape
    )
    scaled = d_xn * gain_ref[...]
    inner_mean = jnp.mean(scaled * normed, axis=-1, keepdims=True)
    din_ref[...] = (dstate_ref[...] + scale_row * (scaled - normed * inner_mean)).astype(bf16)


def back(meta, own, other, dxq, x, gain, dstate, wk, wv, cos, sin):
    rows, width = x.shape
    return pl.pallas_call(
        back_kernel,
        grid_spec=pltpu.PrefetchScalarGridSpec(
            num_scalar_prefetch=1,
            grid=(1,),
            in_specs=[
                fixed(a.shape) for a in (own, other, dxq, x, gain, dstate, wk, wv, cos, sin)
            ],
            out_specs=[
                fixed((rows, width)),
                fixed((rows, 2 * KV * HD)),
                fixed((8, width)),
            ],
            scratch_shapes=[pltpu.VMEM((KV, rows, 2 * HD), f32)],
        ),
        out_shape=[
            jax.ShapeDtypeStruct((rows, width), bf16),
            jax.ShapeDtypeStruct((rows, 2 * KV * HD), bf16),
            jax.ShapeDtypeStruct((8, width), f32),
        ],
        compiler_params=params(16),
        cost_estimate=cost(4 * rows * width * KV * HD, 16 * rows * width),
        name="back",
    )(meta, own, other, dxq, x, gain, dstate, wk, wv, cos, sin)


def dense_kernel(steps, extra, meta_ref, left_ref, left2_ref, right_ref, right2_ref, *refs):
    if extra:
        xn_ref, dlog_ref, gain1_ref, gain2_ref = refs[:4]
        refs = refs[4:]
        more_ref = refs[-1]
        refs = refs[:-1]
    outs, whole_ref = refs[:-1], refs[-1]
    core = meta_ref[0]
    place = meta_ref[1]
    group = pl.program_id(0)
    piece = outs[0].shape[4]
    wide = right_ref.shape[1]
    left = jnp.concatenate([left_ref[...], left2_ref[...]], axis=0)
    right = jnp.concatenate([right_ref[...], right2_ref[...]], axis=0)
    whole_ref[...] = dot_tn(left, right)
    if extra:
        router = dot_tn(xn_ref[...], dlog_ref[...])
        first = jnp.broadcast_to(gain1_ref[0:1, :], (LANES, router.shape[0])).T
        second = jnp.broadcast_to(gain2_ref[0:1, :], (LANES, router.shape[0])).T
        lane = lax.broadcasted_iota(jnp.int32, router.shape, 1)
        more_ref[...] = jnp.where(
            lane == LANES - 2, first, jnp.where(lane == LANES - 1, second, router)
        )

    def give(out_ref):
        for d in range(2):
            for c in range(2):
                for t in range(2):
                    at = ((core ^ t) * 4 + (place ^ (c * 2 + d))) * piece
                    rows = pl.ds(pl.multiple_of(at, 16), piece)
                    out_ref[0, d, c, t, :, :wide] = whole_ref[rows, :].astype(bf16)
                    if extra:
                        out_ref[0, d, c, t, :, wide:] = more_ref[rows, :].astype(bf16)

    for k in range(steps):

        @pl.when((group >= 2**k) & (group < 2 ** (k + 1)))
        def _():
            give(outs[k])

    @pl.when(group == 0)
    def _():
        give(outs[steps])


def dense_grad(plane, meta, left, left2, right, right2, extra=()):
    rows, width = left.shape
    wide = right.shape[1]
    part = width // plane.chips
    piece = part // 8
    held = wide + (LANES if extra else 0)
    columns = pl.BlockSpec((rows, part), lambda g, m: (0, m[2 + g]))
    gains = pl.BlockSpec((8, part), lambda g, m: (0, m[2 + g]))
    more = [columns, fixed((rows, LANES)), gains, gains]

    def out(first, size):
        where = lambda g, m: (jnp.clip(g - first, 0, size - 1), 0, 0, 0, 0, 0)
        return pl.BlockSpec((1, 2, 2, 2, piece, held), where)

    ranges = [(2**k, 2**k) for k in range(plane.steps)] + [(0, 1)]
    return pl.pallas_call(
        functools.partial(dense_kernel, plane.steps, bool(extra)),
        grid_spec=pltpu.PrefetchScalarGridSpec(
            num_scalar_prefetch=1,
            grid=(plane.chips,),
            in_specs=[columns, columns, fixed((rows, wide)), fixed((rows, wide))]
            + (more if extra else []),
            out_specs=[out(*r) for r in ranges],
            scratch_shapes=[pltpu.VMEM((part, wide), f32)]
            + ([pltpu.VMEM((part, LANES), f32)] if extra else []),
        ),
        out_shape=[
            jax.ShapeDtypeStruct((size, 2, 2, 2, piece, held), bf16) for _, size in ranges
        ],
        compiler_params=params(28),
        cost_estimate=cost(4 * rows * width * wide, 2 * width * wide),
        name="dense_grad",
    )(meta, left, left2, right, right2, *extra)


def finish_kernel(core_ref, own_ref, came_ref, que_ref, out_ref, key_ref, val_ref, more_ref):
    core = core_ref[0]
    split = que_ref.shape[1] // 2
    wide = key_ref.shape[1]

    def place(first, second):
        here = pl.ds(pl.multiple_of(core * split, LANES), split)
        there = pl.ds(pl.multiple_of((1 - core) * split, LANES), split)
        out_ref[:, here] = first[:, :split]
        out_ref[:, there] = second[:, :split]
        que_ref[:, here] = first[:, split : 2 * split]
        que_ref[:, there] = second[:, split : 2 * split]
        more_ref[...] = first[:, 2 * split + wide :] + second[:, 2 * split + wide :]

    own, came = own_ref[...], came_ref[...].astype(f32)
    place(own, came)
    small_own, small_came = own[:, 2 * split : 2 * split + wide], came[:, 2 * split : 2 * split + wide]
    key_ref[...] = jnp.where(core == 0, small_own, small_came)
    val_ref[...] = jnp.where(core == 0, small_came, small_own)


def finish(core, own, came, split, wide):
    rows = own.shape[0]
    shapes = [(rows, 2 * split), (rows, 2 * split), (rows, wide), (rows, wide), (rows, LANES)]
    return pl.pallas_call(
        finish_kernel,
        grid_spec=pltpu.PrefetchScalarGridSpec(
            num_scalar_prefetch=1,
            grid=(1,),
            in_specs=[fixed(own.shape), fixed(came.shape)],
            out_specs=[fixed(shape) for shape in shapes],
        ),
        out_shape=[jax.ShapeDtypeStruct(shape, f32) for shape in shapes],
        compiler_params=params(8),
        name="finish",
    )(core, own, came)


class Plane:
    def __init__(self, size):
        self.size = size
        bits = size.bit_length() - 1
        self.steps = bits - 1
        self.shift = self.steps // 2 if self.steps % 2 == 0 else 0
        first = list(range(1, bits))
        self.order = (first, first[self.shift :] + first[: self.shift])
        self.sibling = [(i, i ^ 1) for i in range(size)]
        self.mixed = [
            [(i, i ^ (1 << self.order[i & 1][k])) for i in range(size)] for k in range(self.steps)
        ]
        self.chips = size // 2

    def chip_offset(self, core, group):
        return sum(((group >> k) & 1) << self.order[core][k] for k in range(self.steps))

    def swapped(self, group):
        if not self.shift:
            return group
        low_mask = (1 << self.shift) - 1
        return ((group & low_mask) << (self.steps - self.shift)) | (group >> self.shift)


def total(values):
    summed = values[0].astype(f32)
    for value in values[1:]:
        summed = summed + value.astype(f32)
    return summed.astype(bf16)


def reduce_steps(plane, terms, hold=()):
    terms = list(terms)

    def pick(first, last):
        return [
            a[first - at : last - at] for at, a in terms if at <= first and last - at <= a.shape[0]
        ]

    for k in reversed(range(plane.steps)):
        send = total(pick(2**k, 2 ** (k + 1)))
        terms.append((0, lax.ppermute(send, "expert", plane.mixed[k])))
    return [a[0] for a in pick(0, 1)]


def to_sibling(plane, value):
    return lax.ppermute(value, "expert", plane.sibling)


def place_keys(bases_ref, at, buf_ref, keys_ref, vals_ref, half, blocks):
    for block in range(blocks):
        for part in range(2):
            rows = pl.ds(pl.multiple_of(bases_ref[at + block * 2 + part] * half, 16), half)
            keys_ref[rows, :] = buf_ref[block, part * half : (part + 1) * half, :HD]
            vals_ref[rows, :] = buf_ref[block, part * half : (part + 1) * half, HD:]


def stack_heads(ref, part, half, groups):
    return jnp.concatenate(
        [
            ref[part * half : (part + 1) * half, g * HD : (g + 1) * HD]
            for g in range(groups)
        ],
        axis=0,
    )


def for_steps(count, body):
    if count <= 8:
        for n in range(count):
            body(n)
    else:
        lax.fori_loop(0, count, lambda n, _: (body(n), 0)[1], 0)


def attend_kernel(at, meta_ref, q_ref, buf_ref, offs_ref, *refs):
    (
        att_ref,
        attt_ref,
        lse_ref,
        keys_ref,
        vals_ref,
        query_ref,
        top_ref,
        sum_ref,
        mix_ref,
    ) = refs
    blocks = buf_ref.shape[0]
    half = q_ref.shape[0] // 2
    groups = q_ref.shape[1] // HD
    chunk = CHUNK_BLOCKS * half
    factor = LOG2E / math.sqrt(HD)
    count = 2 * blocks // CHUNK_BLOCKS - 1
    place_keys(meta_ref, at, buf_ref, keys_ref, vals_ref, half, blocks)
    for part in range(2):
        query_ref[part] = stack_heads(q_ref, part, half, groups)
    full = [lax.div(meta_ref[1 + part], CHUNK_BLOCKS) for part in range(2)]

    def step(n, part, j, edge):
        rows = pl.ds(pl.multiple_of(j * chunk, 16), chunk)
        scores = dot_nt(keys_ref[rows, :], query_ref[part])
        if edge is not None:
            row = lax.broadcasted_iota(jnp.int32, scores.shape, 0) + (j * chunk - edge * half)
            scores = jnp.where(row <= offs_ref[0:1, :], scores, negative)
        top = jnp.max(scores, axis=0, keepdims=True)
        weights = jnp.exp2((scores - top) * factor)
        top_ref[n, 0:1, :] = top
        sum_ref[n, 0:1, :] = jnp.sum(weights, axis=0, keepdims=True)
        mix_ref[n] = dot_tn(vals_ref[rows, :], weights.astype(bf16))

    def full_step(n):
        late = n >= full[0]
        part = jnp.where(late, 1, 0)
        step(n, part, n - jnp.where(late, full[0], 0), None)

    for_steps(count, full_step)
    for part in range(2):
        step(count + part, part, full[part], meta_ref[1 + part])
    for part in range(2):
        edge = count + part
        top = top_ref[edge, 0:1, :]

        def mine(n):
            return (n < full[0]) if part == 0 else (n >= full[0])

        def find(n, top):
            return jnp.where(mine(n), jnp.maximum(top, top_ref[n, 0:1, :]), top)

        def add(n, carry):
            summed, acc = carry
            share = jnp.exp2((top_ref[n, 0:1, :] - top) * factor)
            share = jnp.where(mine(n), jnp.minimum(share, 1.0), 0.0)
            return summed + share * sum_ref[n, 0:1, :], acc + share * mix_ref[n]

        top = fold_steps(count, find, top)
        share = jnp.exp2((top_ref[edge, 0:1, :] - top) * factor)
        summed, acc = fold_steps(
            count, add, (share * sum_ref[edge, 0:1, :], share * mix_ref[edge])
        )
        acc = acc / summed
        attt_ref[part] = acc
        lse_ref[part] = jnp.broadcast_to(top * factor + jnp.log2(summed), lse_ref.shape[1:])
        rowwise = acc.T.astype(bf16)
        for g in range(groups):
            att_ref[part * half : (part + 1) * half, g * HD : (g + 1) * HD] = rowwise[
                g * half : (g + 1) * half
            ]


def fold_steps(count, body, carry):
    if count <= 8:
        for n in range(count):
            carry = body(n, carry)
        return carry
    return lax.fori_loop(0, count, body, carry)


def attend(own, meta, query, buf, offs):
    rows = query.shape[0]
    groups = H // KV
    half = rows // 2
    blocks, padded, wide = buf.shape
    span = groups * HD
    width = groups * half
    keys = blocks * rows
    steps = 2 * blocks // CHUNK_BLOCKS + 1
    which = (lambda m: m[0]) if own else (lambda m: 1 - m[0])
    head = lambda i, m: (0, which(m))
    return pl.pallas_call(
        functools.partial(attend_kernel, 4 if own else 4 + 2 * blocks),
        grid_spec=pltpu.PrefetchScalarGridSpec(
            num_scalar_prefetch=1,
            grid=(1,),
            in_specs=[
                pl.BlockSpec((rows, span), head),
                fixed((blocks, padded, wide)),
                fixed((8, width)),
            ],
            out_specs=[
                fixed((rows, span)),
                fixed((2, HD, width)),
                fixed((2, 8, width)),
            ],
            scratch_shapes=[
                pltpu.VMEM((keys, HD), bf16),
                pltpu.VMEM((keys, HD), bf16),
                pltpu.VMEM((2, width, HD), bf16),
                pltpu.VMEM((steps, 8, width), f32),
                pltpu.VMEM((steps, 8, width), f32),
                pltpu.VMEM((steps, HD, width), f32),
            ],
        ),
        out_shape=[
            jax.ShapeDtypeStruct((rows, span), bf16),
            jax.ShapeDtypeStruct((2, HD, width), f32),
            jax.ShapeDtypeStruct((2, 8, width), f32),
        ],
        compiler_params=params(20 + blocks * rows * HD // 2**16),
        cost_estimate=cost(
            rows * keys * H * HD, blocks * padded * wide * 2, rows * keys * H // 4
        ),
        name="attend",
    )(meta, query, buf, offs)


def attend_back_kernel(
    at,
    meta_ref,
    q_ref,
    do_ref,
    buf_ref,
    offs_ref,
    attt_ref,
    lse_ref,
    cos_ref,
    sin_ref,
    *refs,
):
    (
        dq_ref,
        dbuf_ref,
        keys_ref,
        vals_ref,
        dkeys_ref,
        dvals_ref,
        query_ref,
        grad_ref,
        delta_ref,
        dquery_ref,
    ) = refs
    blocks = buf_ref.shape[0]
    half = q_ref.shape[0] // 2
    groups = q_ref.shape[1] // HD
    chunk = CHUNK_BLOCKS * half
    scale = 1.0 / math.sqrt(HD)
    factor = LOG2E * scale
    count = 2 * blocks // CHUNK_BLOCKS - 1
    place_keys(meta_ref, at, buf_ref, keys_ref, vals_ref, half, blocks)
    dkeys_ref[...] = jnp.zeros_like(dkeys_ref)
    dvals_ref[...] = jnp.zeros_like(dvals_ref)
    dquery_ref[...] = jnp.zeros_like(dquery_ref)
    for part in range(2):
        query_ref[part] = stack_heads(q_ref, part, half, groups)
        grad = stack_heads(do_ref, part, half, groups)
        grad_ref[part] = grad
        delta = jnp.sum(grad.astype(f32).T * attt_ref[part], axis=0, keepdims=True)
        delta_ref[part] = jnp.broadcast_to(delta, delta_ref.shape[1:])
    full = [lax.div(meta_ref[1 + part], CHUNK_BLOCKS) for part in range(2)]

    def step(part, j, edge):
        rows = pl.ds(pl.multiple_of(j * chunk, 16), chunk)
        keys = keys_ref[rows, :]
        query, grad = query_ref[part], grad_ref[part]
        scores = dot_nt(keys, query)
        weights = jnp.exp2(scores * factor - lse_ref[part, 0:1, :])
        if edge is not None:
            row = lax.broadcasted_iota(jnp.int32, scores.shape, 0) + (j * chunk - edge * half)
            weights = jnp.where(row <= offs_ref[0:1, :], weights, 0.0)
        dweights = dot_nt(vals_ref[rows, :], grad)
        dscores = (weights * (dweights - delta_ref[part, 0:1, :])).astype(bf16)
        dvals_ref[rows, :] += dot(weights.astype(bf16), grad)
        dkeys_ref[rows, :] += dot(dscores, query)
        dquery_ref[part] += dot_tn(keys, dscores)

    def full_step(n):
        late = n >= full[0]
        step(jnp.where(late, 1, 0), n - jnp.where(late, full[0], 0), None)

    for_steps(count, full_step)
    for part in range(2):
        step(part, full[part], meta_ref[1 + part])
    for part in range(2):
        rowwise = dquery_ref[part].T * scale
        these = slice(part * half, (part + 1) * half)
        for g in range(groups):
            turned = turn(rowwise[g * half : (g + 1) * half], cos_ref[these], -sin_ref[these])
            dq_ref[these, g * HD : (g + 1) * HD] = turned.astype(bf16)

    for block in range(blocks):
        for part in range(2):
            rows = pl.ds(pl.multiple_of(meta_ref[at + block * 2 + part] * half, 16), half)
            here = slice(part * half, (part + 1) * half)
            dbuf_ref[block, here, :HD] = (dkeys_ref[rows, :] * scale).astype(bf16)
            dbuf_ref[block, here, HD:] = dvals_ref[rows, :].astype(bf16)


def attend_back(own, meta, query, grad, buf, offs, attt, lse, cos, sin):
    rows = query.shape[0]
    groups = H // KV
    half = rows // 2
    blocks, padded, wide = buf.shape
    span = groups * HD
    width = groups * half
    keys = blocks * rows
    which = (lambda m: m[0]) if own else (lambda m: 1 - m[0])
    head = lambda i, m: (0, which(m))
    need = blocks * rows * (2 * HD * 2 + 2 * HD * 4 + 3 * wide * 2)
    return pl.pallas_call(
        functools.partial(attend_back_kernel, 4 if own else 4 + 2 * blocks),
        grid_spec=pltpu.PrefetchScalarGridSpec(
            num_scalar_prefetch=1,
            grid=(1,),
            in_specs=[
                pl.BlockSpec((rows, span), head),
                pl.BlockSpec((rows, span), head),
                fixed((blocks, padded, wide)),
                fixed((8, width)),
                fixed((2, HD, width)),
                fixed((2, 8, width)),
                fixed((rows, HD)),
                fixed((rows, HD)),
            ],
            out_specs=[fixed((rows, span)), fixed((blocks, rows, wide))],
            scratch_shapes=[
                pltpu.VMEM((keys, HD), bf16),
                pltpu.VMEM((keys, HD), bf16),
                pltpu.VMEM((keys, HD), f32),
                pltpu.VMEM((keys, HD), f32),
                pltpu.VMEM((2, width, HD), bf16),
                pltpu.VMEM((2, width, HD), bf16),
                pltpu.VMEM((2, 8, width), f32),
                pltpu.VMEM((2, HD, width), f32),
            ],
        ),
        out_shape=[
            jax.ShapeDtypeStruct((rows, span), bf16),
            jax.ShapeDtypeStruct((blocks, rows, wide), bf16),
        ],
        compiler_params=params(24 + need // 2**20),
        cost_estimate=cost(
            2.5 * rows * keys * H * HD, blocks * padded * wide * 4, rows * keys * H // 4
        ),
        name="attend_back",
    )(meta, query, grad, buf, offs, attt, lse, cos, sin)


def expert_kernel(
    plane,
    meta_ref,
    mine_ref,
    theirs_ref,
    dy_mine_ref,
    dy_theirs_ref,
    wg_ref,
    wu_ref,
    wd_ref,
    wr_ref,
    out_mine_ref,
    out_theirs_ref,
    dx_mine_ref,
    dx_theirs_ref,
    hidden_ref,
    dhid_ref,
    gate_ref,
):
    core = meta_ref[0]
    expert = meta_ref[1]
    rows, half = mine_ref.shape[2], mine_ref.shape[3]
    here = pl.ds(pl.multiple_of(core * half, LANES), half)
    there = pl.ds(pl.multiple_of((1 - core) * half, LANES), half)
    x_mine = mine_ref[0].reshape(2 * rows, half)
    x_theirs = jnp.concatenate([theirs_ref[0, 1], theirs_ref[0, 0]], axis=0)
    gate_pre = dot(x_mine, wg_ref[here, :]) + dot(x_theirs, wg_ref[there, :])
    up_pre = dot(x_mine, wu_ref[here, :]) + dot(x_theirs, wu_ref[there, :])
    logits = dot(x_mine, wr_ref[here, :]) + dot(x_theirs, wr_ref[there, :])
    marked = dy_mine_ref[0].reshape(2 * rows, half + LANES)
    dy_here = marked[:, :half].astype(f32)
    dy_there = jnp.concatenate(
        [dy_theirs_ref[0, 1, :, :half], dy_theirs_ref[0, 0, :, :half]], axis=0
    ).astype(f32)
    chosen = marked[:, half:].astype(f32) > 0.5
    top = jnp.max(jnp.where(chosen, logits, negative), axis=-1, keepdims=True)
    shares = jnp.where(chosen, jnp.exp(logits - top), 0.0)
    lane = lax.broadcasted_iota(jnp.int32, logits.shape, 1)
    own = jnp.sum(jnp.where(lane == expert, shares, 0.0), axis=-1, keepdims=True)
    gate = own / jnp.sum(shares, axis=-1, keepdims=True)
    routed = jnp.sum(jnp.where((lane == expert) & chosen, 1.0, 0.0), axis=-1, keepdims=True)
    gate_ref[...] = jnp.broadcast_to(gate, gate_ref.shape)

    sig = jax.nn.sigmoid(gate_pre)
    silu = gate_pre * sig
    hidden = (silu * up_pre).astype(bf16)
    hidden_ref[...] = hidden
    result_here = dot(hidden, wd_ref[:, here]).astype(bf16).astype(f32)
    result_there = dot(hidden, wd_ref[:, there]).astype(bf16).astype(f32)
    d_gate = routed * (
        jnp.sum(dy_here * result_here, axis=-1, keepdims=True)
        + jnp.sum(dy_there * result_there, axis=-1, keepdims=True)
    )
    out_here = (gate * result_here).astype(bf16)
    out_there = (gate * result_there).astype(bf16)
    d_hidden = dot_nt((gate * dy_here).astype(bf16), wd_ref[:, here]) + dot_nt(
        (gate * dy_there).astype(bf16), wd_ref[:, there]
    )
    d_up = (d_hidden * silu).astype(bf16)
    d_gp = (d_hidden * up_pre * (sig * (1.0 + gate_pre * (1.0 - sig)))).astype(bf16)
    inner = d_gp.shape[1]
    dhid_ref[:, :inner] = d_gp
    dhid_ref[:, inner:] = d_up
    high = d_gate.astype(bf16).astype(f32)
    low = d_gate - high
    spot = jnp.where(lane == expert, 1.0, 0.0)
    dx_here = (dot_nt(d_gp, wg_ref[here, :]) + dot_nt(d_up, wu_ref[here, :])).astype(bf16)
    dx_there = (dot_nt(d_gp, wg_ref[there, :]) + dot_nt(d_up, wu_ref[there, :])).astype(bf16)
    col_here = (spot * jnp.where(core == 0, high, low)).astype(bf16)
    col_there = (spot * jnp.where(core == 0, low, high)).astype(bf16)
    for t in range(2):
        these = slice(t * rows, (t + 1) * rows)
        dx_mine_ref[0, t, :, :half] = dx_here[these]
        dx_mine_ref[0, t, :, half:] = col_here[these]
        dx_theirs_ref[0, 1 - t, :, :half] = dx_there[these]
        dx_theirs_ref[0, 1 - t, :, half:] = col_there[these]
        out_mine_ref[0, t] = out_here[these]
        out_theirs_ref[0, 1 - t] = out_there[these]


def run_expert(plane, first, meta, mine, theirs, dy_mine, dy_theirs, wg, wu, wd, wr):
    chips, _, rows, half = mine.shape
    width, inner = wg.shape
    swap = lambda g: plane.swapped(g + first) - first
    pair = lambda w: pl.BlockSpec((1, 2, rows, w), lambda g, m: (g, 0, 0, 0))
    swapped = lambda w: pl.BlockSpec((1, 2, rows, w), lambda g, m: (swap(g), 0, 0, 0))
    flat = lambda w: pl.BlockSpec((2 * rows, w), lambda g, m: (g, 0))
    total_rows = chips * 2 * rows
    return pl.pallas_call(
        functools.partial(expert_kernel, plane),
        grid_spec=pltpu.PrefetchScalarGridSpec(
            num_scalar_prefetch=1,
            grid=(chips,),
            in_specs=[
                pair(half),
                swapped(half),
                pair(half + LANES),
                swapped(half + LANES),
                fixed((width, inner)),
                fixed((width, inner)),
                fixed((inner, width)),
                fixed((width, wr.shape[1])),
            ],
            out_specs=[
                pair(half),
                swapped(half),
                pair(half + LANES),
                swapped(half + LANES),
                flat(inner),
                flat(2 * inner),
                flat(LANES),
            ],
        ),
        out_shape=[
            jax.ShapeDtypeStruct((chips, 2, rows, half), bf16),
            jax.ShapeDtypeStruct((chips, 2, rows, half), bf16),
            jax.ShapeDtypeStruct((chips, 2, rows, half + LANES), bf16),
            jax.ShapeDtypeStruct((chips, 2, rows, half + LANES), bf16),
            jax.ShapeDtypeStruct((total_rows, inner), bf16),
            jax.ShapeDtypeStruct((total_rows, 2 * inner), bf16),
            jax.ShapeDtypeStruct((total_rows, LANES), f32),
        ],
        compiler_params=params(36),
        cost_estimate=cost(
            12 * total_rows * width * inner, 20 * total_rows * width, total_rows * inner
        ),
        name="expert",
    )(meta, mine, theirs, dy_mine, dy_theirs, wg, wu, wd, wr)


def rows_in_order(plane, own0, own, other0, other, mine):
    if mine:
        return [ref[g, t] for ref in (own0, own) for g in range(ref.shape[0]) for t in range(2)]
    parts = [other0[0, 1], other0[0, 0]]
    for g in range(1, plane.chips):
        at = plane.swapped(g) - 1
        parts += [other[at, 1], other[at, 0]]
    return parts


def expert_grad_kernel(plane, weigh, meta_ref, *refs):
    lefts, refs = refs[:4], refs[4:]
    if weigh:
        gate0_ref, gate_ref, right0_ref, right_ref, _, out_ref = refs
    else:
        right0_ref, right_ref, out_ref = refs
    step = pl.program_id(0)
    halves = pl.num_programs(0) // 2
    first = right0_ref.shape[0]

    def give(parts):
        if weigh:
            rows = parts[0].shape[0]
            gates = [gate0_ref[t * rows : (t + 1) * rows, 0:1] for t in range(2)]
            gates += [
                gate_ref[n * rows : (n + 1) * rows, 0:1] for n in range(len(parts) - 2)
            ]
            parts = [(g * p.astype(f32)).astype(bf16) for g, p in zip(gates, parts)]
        near = jnp.concatenate(parts[:2], axis=0)
        far = jnp.concatenate(parts[2:], axis=0)
        out_ref[...] = (dot_tn(near, right0_ref[...]) + dot_tn(far, right_ref[...])).astype(bf16)

    @pl.when(step < halves)
    def _():
        give(rows_in_order(plane, *lefts, True))

    @pl.when(step >= halves)
    def _():
        give(rows_in_order(plane, *lefts, False))


def expert_grad(plane, meta, lefts, right0, right, half, gates=None, grads=None):
    tile = half // 2
    rows = lefts[0].shape[2]
    inner = right.shape[1]
    own = lambda a: pl.BlockSpec(
        a.shape[:3] + (tile,), lambda i, m: (0, 0, 0, jnp.minimum(i, 1))
    )
    other = lambda a: pl.BlockSpec(
        a.shape[:3] + (tile,), lambda i, m: (0, 0, 0, jnp.maximum(i - 2, 0))
    )
    count = right0.shape[0] + right.shape[0]
    need = count * (8 * tile * 2 + inner * 2) + 3 * tile * inner * 4
    specs = [own(lefts[0]), own(lefts[1]), other(lefts[2]), other(lefts[3])]
    args = list(lefts)
    if gates:
        specs += [fixed(g.shape) for g in gates]
        args += list(gates)
    specs += [fixed(right0.shape), fixed(right.shape)]
    args += [right0, right]
    if gates:
        specs.append(pl.BlockSpec(memory_space=pl.ANY))
        args.append(grads)
        need += count * LANES * 4
        out_shape, place = grads.shape, 2
    else:
        out_shape, place = (2 * half, inner + inner // 2), 0
    return pl.pallas_call(
        functools.partial(expert_grad_kernel, plane, bool(gates)),
        grid_spec=pltpu.PrefetchScalarGridSpec(
            num_scalar_prefetch=1,
            grid=(4,),
            in_specs=specs,
            out_specs=pl.BlockSpec(
                (tile, inner), lambda i, m: ((m[0] ^ (i // 2)) * 2 + i % 2, place)
            ),
        ),
        out_shape=jax.ShapeDtypeStruct(out_shape, bf16),
        input_output_aliases={len(args): 0} if gates else {},
        compiler_params=params(8 + need // 2**20),
        cost_estimate=cost(4 * count * half * inner, 6 * count * half),
        name="down_grad" if gates else "up_grad",
    )(meta, *args)


def together(*values):
    return lax.optimization_barrier(values)


def per_device(
    tokens,
    gain_attn,
    w_query,
    w_key,
    w_value,
    w_out,
    gain_moe,
    w_router,
    w_gate,
    w_up,
    w_down,
    routes,
    positions,
    cotangent,
):
    rows = tokens.shape[1]
    width = tokens.shape[2]
    half = rows // 2
    split = width // 2
    groups = H // KV
    kv_width = KV * HD
    experts = w_router.shape[1]
    inner = w_gate.shape[2]
    plane = Plane(w_gate.shape[0] * lax.axis_size("expert"))
    last = plane.steps - 1
    contexts = lax.axis_size("context")
    copies = lax.axis_size("dp")
    blocks = plane.size * contexts
    index = lax.axis_index("expert")
    core = index % 2
    places = positions[0]
    x = tokens[0]
    gain_one, gain_two = gain_attn, gain_moe
    swap_context = [(i, i ^ 1) for i in range(contexts)]
    swap_copies = [(i, i ^ 1) for i in range(copies)]

    def by_core(zero, one):
        return jnp.where(core == 0, zero, one)

    def mix(value, k):
        return lax.ppermute(value, "expert", plane.mixed[k])

    def sibling(value):
        return lax.ppermute(value, "expert", plane.sibling)

    tcos, tsin = rope_tables(2 * blocks, half)
    own_bases = jnp.stack([places[0], places[half]]) // half
    front_meta = jnp.concatenate([core[None], own_bases]).astype(jnp.int32)
    core_row = jnp.reshape(core, (1,)).astype(jnp.int32)
    xn_one, packed, cos, sin = front(
        core_row, places, x, gain_one, w_key, w_value, tcos, tsin
    )

    lanes = jnp.arange(LANES, dtype=jnp.int32)
    marks = jnp.any(routes[0][:, :, None] == lanes[None, None, :], axis=1).astype(bf16)
    dy, marks = after(cotangent[0], packed), after(marks, packed)
    dy_keep = jnp.concatenate([by_core(dy[:, :split], dy[:, split:]), marks], axis=1)
    dy_send = jnp.concatenate([by_core(dy[:, split:], dy[:, :split]), marks], axis=1)

    router_wide = jnp.pad(w_router, ((0, 0), (0, LANES - experts)))
    weights = (w_gate[0], w_up[0], w_down[0], router_wide)
    dy_m0 = jnp.stack([dy_keep, sibling(dy_send)])[None]
    dy_t0 = jnp.stack([sibling(dy_keep), dy_send])[None]
    if contexts > 1:
        arrived = lax.ppermute(packed, "context", swap_context)
        arrived, dy_m0, dy_t0, front_meta = together(arrived, dy_m0, dy_t0, front_meta)
        packed = jnp.stack([packed, arrived], axis=1)
    else:
        packed = packed[:, None]
    held = jnp.stack([packed[0], sibling(packed[1])])[None]
    query = make_query(xn_one, w_query, cos, sin)
    for k in range(plane.steps):
        if k == last:
            held, query = together(held, query)
        held = jnp.concatenate([held, mix(held, k)])
    mine = held.reshape(blocks, rows + PAD_ROWS, kv_width)
    theirs = sibling(held).reshape(blocks, rows + PAD_ROWS, kv_width)
    own_order = mine[:, rows :: PAD_ROWS // 2, 0].astype(f32).astype(jnp.int32).reshape(-1)
    spots = [
        ((plane.swapped(g) * 2 + 1 - t) * contexts + c) * 2 + part
        for g in range(plane.chips)
        for t in range(2)
        for c in range(contexts)
        for part in range(2)
    ]
    other_order = jnp.stack([own_order[spot] for spot in spots])
    meta = jnp.concatenate([front_meta, front_meta[:1], own_order, other_order])
    offs = jnp.asarray(np.tile(np.arange(groups * half, dtype=np.int32) % half, (8, 1)))

    dy_held, meta = together(dy_m0, meta)
    dy_came = mix(dy_held, 0)
    att_mine, *own_stats = attend(True, meta, query, mine, offs)
    dy_came, theirs, att_mine = together(dy_came, theirs, att_mine)
    dy_held = jnp.concatenate([dy_held, dy_came])
    for k in range(1, last):
        dy_held = jnp.concatenate([dy_held, mix(dy_held, k)])
    dy_held, theirs = together(dy_held, theirs)
    dy_came = mix(dy_held, last)
    att_theirs, *other_stats = attend(False, meta, query, theirs, offs)
    hidden, xn_two, keep, send = join(front_meta, att_mine, att_theirs, w_out, x, gain_two)

    offsets = np.array(
        [[plane.chip_offset(c, g) // 2 for g in range(plane.chips)] for c in range(2)], np.int32
    )
    chips = (index // 2) ^ by_core(offsets[0], offsets[1])
    expert_meta = jnp.concatenate([core[None], index[None], chips]).astype(jnp.int32)
    mine0 = jnp.stack([keep, sibling(send)])[None]
    theirs0 = jnp.stack([sibling(keep), send])[None]
    held = mine0
    for k in range(plane.steps):
        came = mix(held, k)
        if k == last - 1:
            came, dy_came = together(came, dy_came)
        if k == last:
            out_m0, out_t0, dx_m0, dx_t0, hid0, dhid0, gate0 = run_expert(
                plane, 0, expert_meta, after(mine0, held), theirs0, dy_m0, dy_t0, *weights
            )
            dy_m1 = jnp.concatenate([dy_held, dy_came])[1:]
            dy_t1 = sibling(dy_m1)
            came, hid0, dy_t1 = together(came, hid0, dy_t1)
        held = jnp.concatenate([held, came])
    mine1 = held[1:]
    theirs1 = sibling(mine1)
    out_m1, out_t1, dx_m1, dx_t1, hid1, dhid1, gate1 = run_expert(
        plane, 1, expert_meta, mine1, theirs1, dy_m1, dy_t1, *weights
    )

    def pick(terms, k):
        lo, hi = 2**k, 2 ** (k + 1)
        return total([a[lo - at : hi - at] for at, a in terms if at <= lo and hi - at <= a.shape[0]])

    def parts_of(terms, slot):
        return total([a[0, slot] for at, a in terms if at == 0])

    dx_r0, dx_r1 = sibling(dx_t0), sibling(dx_t1)
    grads = expert_grad(
        plane, expert_meta, (mine0, mine1, theirs0, theirs1), dhid0, dhid1, split
    )
    dx_r1, grads = together(dx_r1, grads)
    terms = [(0, dx_m0), (1, dx_m1), (0, dx_r0), (1, dx_r1)]
    for k in reversed(range(plane.steps)):
        send = pick(terms, k)
        arrived = mix(send, k)
        if k == last:
            grads = expert_grad(
                plane,
                expert_meta,
                (dy_m0, dy_m1, dy_t0, dy_t1),
                after(hid0, send),
                hid1,
                split,
                (gate0, gate1),
                grads,
            )
            arrived, grads = together(arrived, grads)
        terms.append((0, arrived))
    expert_grads = lax.psum_scatter(grads, ("context", "dp"), scatter_dimension=0, tiled=True)
    dx_keep = parts_of(terms, 0)
    dx_other = sibling(parts_of(terms, 1))

    marked = jnp.concatenate([dy, marks], axis=1)
    d_state, d_low, d_logits, d_gain_moe, d_attended = middle(
        front_meta,
        dx_keep,
        dx_other,
        hidden,
        xn_two,
        gain_two,
        marked,
        router_wide,
        w_out,
    )
    dq_theirs, d_theirs = attend_back(
        False, meta, query, d_attended, theirs, offs, *other_stats, cos, sin
    )
    d_sent = sibling(d_theirs)
    d_attended = after(d_attended, dq_theirs)
    dq_mine, d_mine = attend_back(
        True, meta, query, d_attended, mine, offs, *own_stats, cos, sin
    )

    custom = contexts == 2 and copies == 2 and (width // plane.chips) % LANES == 0
    kv_shape = (plane.chips, 2, contexts, rows, kv_width)
    terms = [(0, d_mine.reshape(kv_shape)), (0, d_sent.reshape(kv_shape))]
    if custom:
        place = lax.axis_index("context") * 2 + lax.axis_index("dp")
        dense_meta = jnp.concatenate([core[None], place[None], chips]).astype(jnp.int32)
        xn_other, low_other = sibling(xn_one), sibling(d_low)
        att_other, dq_other = sibling(att_theirs), sibling(dq_theirs)

    def step_sum(steps, came, k):
        return total([steps[k]] + [a[2**k : 2 ** (k + 1)] for a in came])

    def fold(values, axis, pairs):
        return lax.ppermute(total([a[1] for a in values]), axis, pairs)

    for k in reversed(range(plane.steps)):
        send = pick(terms, k)
        arrived = mix(send, k)
        if k == last and custom:
            *out_steps, out_own = dense_grad(
                plane, dense_meta, after(d_low, send), low_other, att_mine, att_other
            )
            *que_steps, que_own = dense_grad(
                plane, dense_meta, xn_one, xn_other, after(dq_mine, out_own), dq_other
            )
            arrived, out_steps, que_own = together(arrived, out_steps, que_own)
        if k == 0:
            dxq = times_transposed(front_meta, after(dq_mine, send), dq_theirs, w_query)
            arrived, dxq = together(arrived, dxq)
            if custom:
                out_steps[last], send = together(out_steps[last], send)
                out_came = [mix(out_steps[last], last)]
        terms.append((0, arrived))
    dkv_keep = parts_of(terms, 0)
    dkv_other = sibling(parts_of(terms, 1))
    dkv = jnp.stack([dkv_keep, dkv_other], axis=1)
    mix_t0, mix_t1, dkv = together(out_t0, out_t1, dkv)
    mix_terms = [(0, out_m0), (1, out_m1), (0, sibling(mix_t0)), (1, sibling(mix_t1))]
    mix_send = pick(mix_terms, last)
    if custom:
        que_steps[last], dkv = together(que_steps[last], dkv)
        que_came = [mix(que_steps[last], last)]
    if contexts > 1:
        dkv_came = lax.ppermute(dkv[1], "context", swap_context)
        dkv_came, mix_send = together(dkv_came, mix_send)
        if custom:
            for k in reversed(range(last)):
                send = step_sum(out_steps, out_came, k)
                dkv_came, send = together(dkv_came, send)
                out_came.append(mix(send, k))
        dkv = dkv[0].astype(f32) + dkv_came.astype(f32)
    else:
        dkv = dkv[0].astype(f32)

    d_in, d_kv, d_gain_attn = back(
        front_meta, dkv[0], dkv[1], dxq, x, gain_one, d_state, w_key, w_value, cos, sin
    )

    if custom:
        for k in reversed(range(last)):
            que_came[-1], d_kv = together(que_came[-1], d_kv)
            send = step_sum(que_steps, que_came, k)
            send, d_kv = together(send, d_kv)
            que_came.append(mix(send, k))
        d_own = by_core(d_kv[:, :kv_width], d_kv[:, kv_width:])
        d_sends = sibling(by_core(d_kv[:, kv_width:], d_kv[:, :kv_width]))
        *small_steps, small_own = dense_grad(
            plane,
            dense_meta,
            xn_one,
            xn_other,
            d_own,
            d_sends,
            (xn_two, d_logits, d_gain_attn, d_gain_moe),
        )
        outs = [out_own[0]] + [a[0] for a in out_came]
        small_steps[last], outs[-1] = together(small_steps[last], outs[-1])
        small_came = []
        for k in reversed(range(plane.steps)):
            send = step_sum(small_steps, small_came, k)
            if k == 0:
                send, que_came = together(send, que_came)
            small_came.append(mix(send, k))
        ques = [que_own[0]] + [a[0] for a in que_came]
        small = [small_own[0]] + [a[0] for a in small_came]
        values = (outs, ques, small)
        send = jnp.concatenate([total([a[1] for a in v]) for v in values], -1)
        mix_send, send = together(mix_send, send)
        arrived = lax.ppermute(send, "dp", swap_copies)
        mix_terms.append((0, mix(mix_send, last)))
        arrived, mix_came, expert_grads = together(arrived, mix_terms[-1][1], expert_grads)
        mix_terms[-1] = (0, mix_came)
        cuts = (slice(None, split), slice(split, width), slice(width, None))
        values = [[a[0] for a in v] + [arrived[..., cut]] for v, cut in zip(values, cuts)]
        send = jnp.concatenate([total([a[1] for a in v]) for v in values], -1)
        arrived = lax.ppermute(send, "context", swap_context)
        for k in reversed(range(last)):
            mix_send, send = together(pick(mix_terms, k), send)
            mix_terms.append((0, mix(mix_send, k)))
        arrived, mix_came = together(arrived, mix_terms[-1][1])
        mix_terms[-1] = (0, mix_came)
        values = [[a[0] for a in v] + [arrived[..., cut]] for v, cut in zip(values, cuts)]
    else:
        for k in reversed(range(plane.steps)):
            mix_terms.append((0, mix(mix_send if k == last else pick(mix_terms, k), k)))

    def split_grads(grads):
        return (
            grads[:, :inner].astype(f32)[None],
            grads[:, inner : 2 * inner].astype(f32)[None],
            grads[:, 2 * inner :].astype(f32).T[None],
        )

    keep, other = parts_of(mix_terms, 0), sibling(parts_of(mix_terms, 1))
    mixture = jnp.concatenate([by_core(keep, other), by_core(other, keep)], axis=1)
    output = (hidden + mixture.astype(f32)).astype(bf16)[None]
    grad_gate, grad_up, grad_down = split_grads(expert_grads)
    if custom:
        values[0][-1], grad_gate, grad_up, grad_down, output = together(
            values[0][-1], grad_gate, grad_up, grad_down, output
        )
        send = jnp.concatenate([total([a[1] for a in v]) for v in values], -1)
        own = jnp.concatenate([sum(a[0].astype(f32) for a in v) for v in values], -1)
        arrived = sibling(send)
        grad_query, grad_out, grad_key, grad_value, extra = finish(
            core_row, own, arrived, split, kv_width
        )
    else:
        in_order = lambda a, b: jnp.concatenate([by_core(a, b), by_core(b, a)], axis=1)
        scatter = lambda v: lax.psum_scatter(
            v.astype(bf16), ("expert", "context", "dp"), scatter_dimension=0, tiled=True
        ).astype(f32)
        grad_query = scatter(dot_tn(xn_one, in_order(dq_mine, dq_theirs)))
        grad_out = scatter(dot_tn(d_low, in_order(att_mine, att_theirs)))
        grad_kv = scatter(dot_tn(xn_one, d_kv))
        grad_key, grad_value = grad_kv[:, :kv_width], grad_kv[:, kv_width:]
        router = dot_tn(xn_two, d_logits)[:, : LANES - 2]
        extra = scatter(
            jnp.concatenate([router, d_gain_attn[:1].T, d_gain_moe[:1].T], axis=1)
        )
    return (
        output,
        d_in[None],
        extra[:, LANES - 2],
        grad_query,
        grad_key,
        grad_value,
        grad_out.T,
        extra[:, LANES - 1],
        extra[:, :experts],
        grad_gate,
        grad_up,
        grad_down,
    )


def solution(mesh):
    in_specs = (
        P("dp", ("expert", "context"), None),
        P(),
        P(),
        P(),
        P(),
        P(),
        P(),
        P(),
        P("expert", None, None),
        P("expert", None, None),
        P("expert", None, None),
        P("dp", ("expert", "context"), None),
        P("dp", ("expert", "context")),
        P("dp", ("expert", "context"), None),
    )
    out_specs = (
        P("dp", ("expert", "context"), None),
        P("dp", ("expert", "context"), None),
        P(("expert", "context", "dp")),
        P(("expert", "context", "dp"), None),
        P(("expert", "context", "dp"), None),
        P(("expert", "context", "dp"), None),
        P(None, ("expert", "context", "dp")),
        P(("expert", "context", "dp")),
        P(("expert", "context", "dp"), None),
        P("expert", ("context", "dp"), None),
        P("expert", ("context", "dp"), None),
        P("expert", None, ("context", "dp")),
    )
    return jax.shard_map(
        per_device, mesh=mesh, in_specs=in_specs, out_specs=out_specs, check_vma=False
    )
```

```python
import functools
import math

import jax
import jax.numpy as jnp
import numpy as np
from jax import lax
from jax.experimental import pallas as pl
from jax.experimental.pallas import tpu as pltpu
from jax.sharding import PartitionSpec as P

H = 12
KV = 2
HD = 128
TOP = 4

eps = 1e-06
rope_base = 1000000.0
negative = -1e30
LANES = 128
JOIN_TILES = 3
CHUNK_BLOCKS = 8
PAD_ROWS = 16
bf16 = jnp.bfloat16
f32 = jnp.float32
LOG2E = 1.4426950408889634


def dot(a, b):
    return lax.dot_general(a, b, (((1,), (0,)), ((), ())), preferred_element_type=f32)


def dot_nt(a, b):
    return lax.dot_general(a, b, (((1,), (1,)), ((), ())), preferred_element_type=f32)


def dot_tn(a, b):
    return lax.dot_general(a, b, (((0,), (0,)), ((), ())), preferred_element_type=f32)


def params(mebibytes):
    return pltpu.CompilerParams(
        dimension_semantics=("arbitrary",), vmem_limit_bytes=min(int(mebibytes), 60) * 1024 * 1024
    )


def after(value, *others):
    return lax.optimization_barrier((value,) + others)[0]


def cost(flops, moved, exps=0):
    return pl.CostEstimate(flops=int(flops), bytes_accessed=int(moved), transcendentals=int(exps))


def turn(values, cos, sin):
    return values * cos + pltpu.roll(values, HD // 2, 1) * sin


def norm_scale(values):
    return lax.rsqrt(jnp.mean(values * values, axis=-1, keepdims=True) + eps)


def rope_tables(count, half):
    freqs = rope_base ** (-np.arange(0, HD, 2) / HD)
    angles = np.concatenate([np.arange(count) * half, np.arange(half)])[:, None] * freqs[None, :]
    twice = np.concatenate([angles, angles], axis=1)
    return jnp.asarray(np.cos(twice), f32), jnp.asarray(np.sin(twice), f32)


def fixed(shape):
    zeros = (0,) * len(shape)
    return pl.BlockSpec(shape, lambda *_: zeros, pipeline_mode=pl.Buffered(1))


def front_kernel(
    core_ref,
    places_ref,
    x_ref,
    gain_ref,
    wk_ref,
    wv_ref,
    tcos_ref,
    tsin_ref,
    xn_ref,
    packed_ref,
    cos_ref,
    sin_ref,
):
    core = core_ref[0]
    rows = x_ref.shape[0]
    half = rows // 2
    bases = [lax.div(places_ref[part * half], half) for part in range(2)]
    count = tcos_ref.shape[0] - half
    sign = jnp.where(lax.broadcasted_iota(jnp.int32, (half, HD), 1) < HD // 2, -1.0, 1.0)
    for part in range(2):
        these = slice(part * half, (part + 1) * half)
        base = pl.ds(bases[part], 1)
        cos_base, sin_base = tcos_ref[base, :], tsin_ref[base, :]
        cos_off, sin_off = tcos_ref[count:, :], tsin_ref[count:, :]
        cos_ref[these, :] = cos_base * cos_off - sin_base * sin_off
        sin_ref[these, :] = (sin_base * cos_off + cos_base * sin_off) * sign
    values = x_ref[...].astype(f32)
    normed = (values * norm_scale(values) * gain_ref[...]).astype(bf16)
    xn_ref[...] = normed
    keys = dot(normed, wk_ref[...])
    vals = dot(normed, wv_ref[...]).astype(bf16)
    edge = lax.broadcasted_iota(jnp.int32, (PAD_ROWS, 2 * HD), 0) < PAD_ROWS // 2
    tail = jnp.where(edge, bases[0].astype(f32), bases[1].astype(f32)).astype(bf16)
    for head in range(KV):
        slot = jnp.where(core == head, 0, 1)
        span = slice(head * HD, (head + 1) * HD)
        turned = turn(keys[:, span], cos_ref[...], sin_ref[...]).astype(bf16)
        packed_ref[slot, :rows, :HD] = turned
        packed_ref[slot, :rows, HD:] = vals[:, span]
        packed_ref[slot, rows:, :] = tail


def front(core, places, x, gain, wk, wv, tcos, tsin):
    rows, width = x.shape
    return pl.pallas_call(
        front_kernel,
        grid_spec=pltpu.PrefetchScalarGridSpec(
            num_scalar_prefetch=2,
            grid=(1,),
            in_specs=[fixed(a.shape) for a in (x, gain, wk, wv, tcos, tsin)],
            out_specs=[
                fixed((rows, width)),
                fixed((2, rows + PAD_ROWS, 2 * HD)),
                fixed((rows, HD)),
                fixed((rows, HD)),
            ],
        ),
        out_shape=[
            jax.ShapeDtypeStruct((rows, width), bf16),
            jax.ShapeDtypeStruct((2, rows + PAD_ROWS, 2 * HD), bf16),
            jax.ShapeDtypeStruct((rows, HD), f32),
            jax.ShapeDtypeStruct((rows, HD), f32),
        ],
        compiler_params=params(60),
        cost_estimate=cost(4 * rows * width * KV * HD, 8 * rows * width),
        name="front",
    )(core, places, x, gain, wk, wv, tcos, tsin)


def query_kernel(x_ref, w_ref, cos_ref, sin_ref, out_ref):
    raw = dot(x_ref[...], w_ref[...])
    for head in range(raw.shape[1] // HD):
        span = slice(head * HD, (head + 1) * HD)
        out_ref[:, span] = turn(raw[:, span], cos_ref[...], sin_ref[...]).astype(bf16)


def make_query(x, w, cos, sin):
    rows, width = x.shape
    wide = w.shape[1]
    tile = 4 * HD
    return pl.pallas_call(
        query_kernel,
        grid=(wide // tile,),
        in_specs=[
            fixed((rows, width)),
            pl.BlockSpec((width, tile), lambda i: (0, i)),
            fixed((rows, HD)),
            fixed((rows, HD)),
        ],
        out_specs=pl.BlockSpec((rows, tile), lambda i: (0, i)),
        out_shape=jax.ShapeDtypeStruct((rows, wide), bf16),
        compiler_params=params(12),
        cost_estimate=cost(2 * rows * width * wide, 2 * width * wide),
        name="make_query",
    )(x, w, cos, sin)


def join_kernel(meta_ref, mine_ref, theirs_ref, w_ref, x_ref, gain_ref, hid_ref, xn_ref, keep_ref, send_ref):
    core = meta_ref[0]
    step = pl.program_id(0)
    width = hid_ref.shape[1]
    tile = width // JOIN_TILES
    span = pl.ds(pl.multiple_of(step * tile, LANES), tile)
    inner = mine_ref.shape[1]
    here = pl.ds(pl.multiple_of(core * inner, LANES), inner)
    there = pl.ds(pl.multiple_of((1 - core) * inner, LANES), inner)
    mixed = dot(mine_ref[...], w_ref[here, :]) + dot(theirs_ref[...], w_ref[there, :])
    hid_ref[:, span] = x_ref[:, span].astype(f32) + mixed

    @pl.when(step == pl.num_programs(0) - 1)
    def _():
        hidden = hid_ref[...]
        xn_ref[...] = (hidden * norm_scale(hidden) * gain_ref[...]).astype(bf16)
        half = width // 2
        keep_ref[...] = xn_ref[:, pl.ds(pl.multiple_of(core * half, LANES), half)]
        send_ref[...] = xn_ref[:, pl.ds(pl.multiple_of((1 - core) * half, LANES), half)]


def join(meta, mine, theirs, w, x, gain):
    rows, width = x.shape
    inner = w.shape[0]
    tile = width // JOIN_TILES
    return pl.pallas_call(
        join_kernel,
        grid_spec=pltpu.PrefetchScalarGridSpec(
            num_scalar_prefetch=1,
            grid=(width // tile,),
            in_specs=[
                fixed(mine.shape),
                fixed(theirs.shape),
                pl.BlockSpec((inner, tile), lambda i, m: (0, i)),
                fixed((rows, width)),
                fixed((width,)),
            ],
            out_specs=[
                fixed((rows, width)),
                fixed((rows, width)),
                fixed((rows, width // 2)),
                fixed((rows, width // 2)),
            ],
        ),
        out_shape=[
            jax.ShapeDtypeStruct((rows, width), f32),
            jax.ShapeDtypeStruct((rows, width), bf16),
            jax.ShapeDtypeStruct((rows, width // 2), bf16),
            jax.ShapeDtypeStruct((rows, width // 2), bf16),
        ],
        compiler_params=params(16),
        cost_estimate=cost(2 * rows * width * inner, 2 * width * inner),
        name="join",
    )(meta, mine, theirs, w, x, gain)


def middle_kernel(
    meta_ref,
    own_ref,
    other_ref,
    hid_ref,
    xn_ref,
    gain_ref,
    dy_ref,
    wr_ref,
    w_ref,
    dstate_ref,
    dlow_ref,
    dlog_ref,
    dgain_ref,
    datt_ref,
    dx_ref,
):
    core = meta_ref[0]
    step = pl.program_id(0)
    width = hid_ref.shape[1]
    half = width // 2

    @pl.when(step == 0)
    def _():
        dx_ref[:, pl.ds(pl.multiple_of(core * half, LANES), half)] = own_ref[:, :half].astype(f32)
        dx_ref[:, pl.ds(pl.multiple_of((1 - core) * half, LANES), half)] = other_ref[
            :, :half
        ].astype(f32)
        d_gate = own_ref[:, half:].astype(f32) + other_ref[:, half:].astype(f32)
        chosen = dy_ref[:, width:].astype(f32) > 0.5
        logits = dot(xn_ref[...], wr_ref[...])
        top = jnp.max(jnp.where(chosen, logits, negative), axis=-1, keepdims=True)
        shares = jnp.where(chosen, jnp.exp(logits - top), 0.0)
        gate = shares / jnp.sum(shares, axis=-1, keepdims=True)
        inner_sum = jnp.sum(gate * d_gate, axis=-1, keepdims=True)
        d_logits = (gate * (d_gate - inner_sum)).astype(bf16)
        dlog_ref[...] = d_logits
        d_xn = dx_ref[...] + dot_nt(d_logits, wr_ref[...])
        hidden = hid_ref[...]
        scale_row = norm_scale(hidden)
        normed = hidden * scale_row
        dgain_ref[...] = jnp.broadcast_to(
            jnp.sum(d_xn * normed, axis=0, keepdims=True), dgain_ref.shape
        )
        scaled = d_xn * gain_ref[...]
        inner_mean = jnp.mean(scaled * normed, axis=-1, keepdims=True)
        d_state = dy_ref[:, :width].astype(f32) + scale_row * (scaled - normed * inner_mean)
        dstate_ref[...] = d_state
        dlow_ref[...] = d_state.astype(bf16)

    datt_ref[...] = dot_nt(dlow_ref[...], w_ref[...]).astype(bf16)


def middle(meta, own, other, hidden, xn, gain, dy, wr, w):
    rows, width = hidden.shape
    inner = w.shape[0]
    tile = inner // JOIN_TILES
    return pl.pallas_call(
        middle_kernel,
        grid_spec=pltpu.PrefetchScalarGridSpec(
            num_scalar_prefetch=1,
            grid=(inner // tile,),
            in_specs=[fixed(a.shape) for a in (own, other, hidden, xn, gain, dy, wr)]
            + [pl.BlockSpec((tile, width), lambda i, m: (i, 0))],
            out_specs=[
                fixed((rows, width)),
                fixed((rows, width)),
                fixed((rows, LANES)),
                fixed((8, width)),
                pl.BlockSpec((rows, tile), lambda i, m: (0, i)),
            ],
            scratch_shapes=[pltpu.VMEM((rows, width), f32)],
        ),
        out_shape=[
            jax.ShapeDtypeStruct((rows, width), f32),
            jax.ShapeDtypeStruct((rows, width), bf16),
            jax.ShapeDtypeStruct((rows, LANES), bf16),
            jax.ShapeDtypeStruct((8, width), f32),
            jax.ShapeDtypeStruct((rows, inner), bf16),
        ],
        compiler_params=params(20),
        cost_estimate=cost(2 * rows * width * inner, 2 * width * inner),
        name="middle",
    )(meta, own, other, hidden, xn, gain, dy, wr, w)


def times_kernel(meta_ref, mine_ref, theirs_ref, w_ref, out_ref):
    core = meta_ref[0]
    inner = mine_ref.shape[1]
    here = pl.ds(pl.multiple_of(core * inner, LANES), inner)
    there = pl.ds(pl.multiple_of((1 - core) * inner, LANES), inner)
    out_ref[...] = dot_nt(mine_ref[...], w_ref[:, here]) + dot_nt(theirs_ref[...], w_ref[:, there])


def times_transposed(meta, mine, theirs, w):
    rows = mine.shape[0]
    width, inner = w.shape
    tile = width // JOIN_TILES
    return pl.pallas_call(
        times_kernel,
        grid_spec=pltpu.PrefetchScalarGridSpec(
            num_scalar_prefetch=1,
            grid=(width // tile,),
            in_specs=[
                fixed(mine.shape),
                fixed(theirs.shape),
                pl.BlockSpec((tile, inner), lambda i, m: (i, 0)),
            ],
            out_specs=pl.BlockSpec((rows, tile), lambda i, m: (0, i)),
        ),
        out_shape=jax.ShapeDtypeStruct((rows, width), f32),
        compiler_params=params(12),
        cost_estimate=cost(2 * rows * width * inner, 2 * width * inner),
        name="times_transposed",
    )(meta, mine, theirs, w)


def back_kernel(
    meta_ref,
    own_ref,
    other_ref,
    dxq_ref,
    x_ref,
    gain_ref,
    dstate_ref,
    wk_ref,
    wv_ref,
    cos_ref,
    sin_ref,
    din_ref,
    dkv_ref,
    dgain_ref,
    pair_ref,
):
    core = meta_ref[0]
    pair_ref[core] = own_ref[...].astype(f32)
    pair_ref[1 - core] = other_ref[...].astype(f32)
    wide = KV * HD
    for head in range(KV):
        turned = turn(pair_ref[head, :, :HD], cos_ref[...], -sin_ref[...])
        dkv_ref[:, head * HD : (head + 1) * HD] = turned.astype(bf16)
        dkv_ref[:, wide + head * HD : wide + (head + 1) * HD] = pair_ref[head, :, HD:].astype(bf16)
    d_xn = (
        dxq_ref[...]
        + dot_nt(dkv_ref[:, :wide], wk_ref[...])
        + dot_nt(dkv_ref[:, wide:], wv_ref[...])
    )
    values = x_ref[...].astype(f32)
    scale_row = norm_scale(values)
    normed = values * scale_row
    dgain_ref[...] = jnp.broadcast_to(
        jnp.sum(d_xn * normed, axis=0, keepdims=True), dgain_ref.shape
    )
    scaled = d_xn * gain_ref[...]
    inner_mean = jnp.mean(scaled * normed, axis=-1, keepdims=True)
    din_ref[...] = (dstate_ref[...] + scale_row * (scaled - normed * inner_mean)).astype(bf16)


def back(meta, own, other, dxq, x, gain, dstate, wk, wv, cos, sin):
    rows, width = x.shape
    return pl.pallas_call(
        back_kernel,
        grid_spec=pltpu.PrefetchScalarGridSpec(
            num_scalar_prefetch=1,
            grid=(1,),
            in_specs=[
                fixed(a.shape) for a in (own, other, dxq, x, gain, dstate, wk, wv, cos, sin)
            ],
            out_specs=[
                fixed((rows, width)),
                fixed((rows, 2 * KV * HD)),
                fixed((8, width)),
            ],
            scratch_shapes=[pltpu.VMEM((KV, rows, 2 * HD), f32)],
        ),
        out_shape=[
            jax.ShapeDtypeStruct((rows, width), bf16),
            jax.ShapeDtypeStruct((rows, 2 * KV * HD), bf16),
            jax.ShapeDtypeStruct((8, width), f32),
        ],
        compiler_params=params(16),
        cost_estimate=cost(4 * rows * width * KV * HD, 16 * rows * width),
        name="back",
    )(meta, own, other, dxq, x, gain, dstate, wk, wv, cos, sin)


def dense_kernel(steps, extra, meta_ref, left_ref, left2_ref, right_ref, right2_ref, *refs):
    if extra:
        xn_ref, dlog_ref, gain1_ref, gain2_ref = refs[:4]
        refs = refs[4:]
        more_ref = refs[-1]
        refs = refs[:-1]
    outs, whole_ref = refs[:-1], refs[-1]
    core = meta_ref[0]
    place = meta_ref[1]
    group = pl.program_id(0)
    piece = outs[0].shape[4]
    wide = right_ref.shape[1]
    left = jnp.concatenate([left_ref[...], left2_ref[...]], axis=0)
    right = jnp.concatenate([right_ref[...], right2_ref[...]], axis=0)
    whole_ref[...] = dot_tn(left, right)
    if extra:
        router = dot_tn(xn_ref[...], dlog_ref[...])
        first = jnp.broadcast_to(gain1_ref[0:1, :], (LANES, router.shape[0])).T
        second = jnp.broadcast_to(gain2_ref[0:1, :], (LANES, router.shape[0])).T
        lane = lax.broadcasted_iota(jnp.int32, router.shape, 1)
        more_ref[...] = jnp.where(
            lane == LANES - 2, first, jnp.where(lane == LANES - 1, second, router)
        )

    def give(out_ref):
        for d in range(2):
            for c in range(2):
                for t in range(2):
                    at = ((core ^ t) * 4 + (place ^ (c * 2 + d))) * piece
                    rows = pl.ds(pl.multiple_of(at, 16), piece)
                    out_ref[0, d, c, t, :, :wide] = whole_ref[rows, :].astype(bf16)
                    if extra:
                        out_ref[0, d, c, t, :, wide:] = more_ref[rows, :].astype(bf16)

    for k in range(steps):

        @pl.when((group >= 2**k) & (group < 2 ** (k + 1)))
        def _():
            give(outs[k])

    @pl.when(group == 0)
    def _():
        give(outs[steps])


def dense_grad(plane, meta, left, left2, right, right2, extra=()):
    rows, width = left.shape
    wide = right.shape[1]
    part = width // plane.chips
    piece = part // 8
    held = wide + (LANES if extra else 0)
    columns = pl.BlockSpec((rows, part), lambda g, m: (0, m[2 + g]))
    gains = pl.BlockSpec((8, part), lambda g, m: (0, m[2 + g]))
    more = [columns, fixed((rows, LANES)), gains, gains]

    def out(first, size):
        where = lambda g, m: (jnp.clip(g - first, 0, size - 1), 0, 0, 0, 0, 0)
        return pl.BlockSpec((1, 2, 2, 2, piece, held), where)

    ranges = [(2**k, 2**k) for k in range(plane.steps)] + [(0, 1)]
    return pl.pallas_call(
        functools.partial(dense_kernel, plane.steps, bool(extra)),
        grid_spec=pltpu.PrefetchScalarGridSpec(
            num_scalar_prefetch=1,
            grid=(plane.chips,),
            in_specs=[columns, columns, fixed((rows, wide)), fixed((rows, wide))]
            + (more if extra else []),
            out_specs=[out(*r) for r in ranges],
            scratch_shapes=[pltpu.VMEM((part, wide), f32)]
            + ([pltpu.VMEM((part, LANES), f32)] if extra else []),
        ),
        out_shape=[
            jax.ShapeDtypeStruct((size, 2, 2, 2, piece, held), bf16) for _, size in ranges
        ],
        compiler_params=params(28),
        cost_estimate=cost(4 * rows * width * wide, 2 * width * wide),
        name="dense_grad",
    )(meta, left, left2, right, right2, *extra)


def finish_kernel(core_ref, own_ref, came_ref, que_ref, out_ref, key_ref, val_ref, more_ref):
    core = core_ref[0]
    split = que_ref.shape[1] // 2
    wide = key_ref.shape[1]

    def place(first, second):
        here = pl.ds(pl.multiple_of(core * split, LANES), split)
        there = pl.ds(pl.multiple_of((1 - core) * split, LANES), split)
        out_ref[:, here] = first[:, :split]
        out_ref[:, there] = second[:, :split]
        que_ref[:, here] = first[:, split : 2 * split]
        que_ref[:, there] = second[:, split : 2 * split]
        more_ref[...] = first[:, 2 * split + wide :] + second[:, 2 * split + wide :]

    own, came = own_ref[...], came_ref[...].astype(f32)
    place(own, came)
    small_own, small_came = own[:, 2 * split : 2 * split + wide], came[:, 2 * split : 2 * split + wide]
    key_ref[...] = jnp.where(core == 0, small_own, small_came)
    val_ref[...] = jnp.where(core == 0, small_came, small_own)


def finish(core, own, came, split, wide):
    rows = own.shape[0]
    shapes = [(rows, 2 * split), (rows, 2 * split), (rows, wide), (rows, wide), (rows, LANES)]
    return pl.pallas_call(
        finish_kernel,
        grid_spec=pltpu.PrefetchScalarGridSpec(
            num_scalar_prefetch=1,
            grid=(1,),
            in_specs=[fixed(own.shape), fixed(came.shape)],
            out_specs=[fixed(shape) for shape in shapes],
        ),
        out_shape=[jax.ShapeDtypeStruct(shape, f32) for shape in shapes],
        compiler_params=params(8),
        name="finish",
    )(core, own, came)


class Plane:
    def __init__(self, size):
        self.size = size
        bits = size.bit_length() - 1
        self.steps = bits - 1
        self.shift = self.steps // 2 if self.steps % 2 == 0 else 0
        first = list(range(1, bits))
        self.order = (first, first[self.shift :] + first[: self.shift])
        self.sibling = [(i, i ^ 1) for i in range(size)]
        self.mixed = [
            [(i, i ^ (1 << self.order[i & 1][k])) for i in range(size)] for k in range(self.steps)
        ]
        self.chips = size // 2

    def chip_offset(self, core, group):
        return sum(((group >> k) & 1) << self.order[core][k] for k in range(self.steps))

    def swapped(self, group):
        if not self.shift:
            return group
        low_mask = (1 << self.shift) - 1
        return ((group & low_mask) << (self.steps - self.shift)) | (group >> self.shift)


def total(values):
    summed = values[0].astype(f32)
    for value in values[1:]:
        summed = summed + value.astype(f32)
    return summed.astype(bf16)


def reduce_steps(plane, terms, hold=()):
    terms = list(terms)

    def pick(first, last):
        return [
            a[first - at : last - at] for at, a in terms if at <= first and last - at <= a.shape[0]
        ]

    for k in reversed(range(plane.steps)):
        send = total(pick(2**k, 2 ** (k + 1)))
        terms.append((0, lax.ppermute(send, "expert", plane.mixed[k])))
    return [a[0] for a in pick(0, 1)]


def to_sibling(plane, value):
    return lax.ppermute(value, "expert", plane.sibling)


def place_keys(bases_ref, at, buf_ref, keys_ref, vals_ref, half, blocks):
    for block in range(blocks):
        for part in range(2):
            rows = pl.ds(pl.multiple_of(bases_ref[at + block * 2 + part] * half, 16), half)
            keys_ref[rows, :] = buf_ref[block, part * half : (part + 1) * half, :HD]
            vals_ref[rows, :] = buf_ref[block, part * half : (part + 1) * half, HD:]


def stack_heads(ref, part, half, groups):
    return jnp.concatenate(
        [
            ref[part * half : (part + 1) * half, g * HD : (g + 1) * HD]
            for g in range(groups)
        ],
        axis=0,
    )


def for_steps(count, body):
    if count <= 8:
        for n in range(count):
            body(n)
    else:
        lax.fori_loop(0, count, lambda n, _: (body(n), 0)[1], 0)


def attend_kernel(at, meta_ref, q_ref, buf_ref, offs_ref, *refs):
    (
        att_ref,
        attt_ref,
        lse_ref,
        keys_ref,
        vals_ref,
        query_ref,
        top_ref,
        sum_ref,
        mix_ref,
    ) = refs
    blocks = buf_ref.shape[0]
    half = q_ref.shape[0] // 2
    groups = q_ref.shape[1] // HD
    chunk = CHUNK_BLOCKS * half
    factor = LOG2E / math.sqrt(HD)
    count = 2 * blocks // CHUNK_BLOCKS - 1
    place_keys(meta_ref, at, buf_ref, keys_ref, vals_ref, half, blocks)
    for part in range(2):
        query_ref[part] = stack_heads(q_ref, part, half, groups)
    full = [lax.div(meta_ref[1 + part], CHUNK_BLOCKS) for part in range(2)]

    def step(n, part, j, edge):
        rows = pl.ds(pl.multiple_of(j * chunk, 16), chunk)
        scores = dot_nt(keys_ref[rows, :], query_ref[part])
        if edge is not None:
            row = lax.broadcasted_iota(jnp.int32, scores.shape, 0) + (j * chunk - edge * half)
            scores = jnp.where(row <= offs_ref[0:1, :], scores, negative)
        top = jnp.max(scores, axis=0, keepdims=True)
        weights = jnp.exp2((scores - top) * factor)
        top_ref[n, 0:1, :] = top
        sum_ref[n, 0:1, :] = jnp.sum(weights, axis=0, keepdims=True)
        mix_ref[n] = dot_tn(vals_ref[rows, :], weights.astype(bf16))

    def full_step(n):
        late = n >= full[0]
        part = jnp.where(late, 1, 0)
        step(n, part, n - jnp.where(late, full[0], 0), None)

    for_steps(count, full_step)
    for part in range(2):
        step(count + part, part, full[part], meta_ref[1 + part])
    for part in range(2):
        edge = count + part
        top = top_ref[edge, 0:1, :]

        def mine(n):
            return (n < full[0]) if part == 0 else (n >= full[0])

        def find(n, top):
            return jnp.where(mine(n), jnp.maximum(top, top_ref[n, 0:1, :]), top)

        def add(n, carry):
            summed, acc = carry
            share = jnp.exp2((top_ref[n, 0:1, :] - top) * factor)
            share = jnp.where(mine(n), jnp.minimum(share, 1.0), 0.0)
            return summed + share * sum_ref[n, 0:1, :], acc + share * mix_ref[n]

        top = fold_steps(count, find, top)
        share = jnp.exp2((top_ref[edge, 0:1, :] - top) * factor)
        summed, acc = fold_steps(
            count, add, (share * sum_ref[edge, 0:1, :], share * mix_ref[edge])
        )
        acc = acc / summed
        attt_ref[part] = acc
        lse_ref[part] = jnp.broadcast_to(top * factor + jnp.log2(summed), lse_ref.shape[1:])
        rowwise = acc.T.astype(bf16)
        for g in range(groups):
            att_ref[part * half : (part + 1) * half, g * HD : (g + 1) * HD] = rowwise[
                g * half : (g + 1) * half
            ]


def fold_steps(count, body, carry):
    if count <= 8:
        for n in range(count):
            carry = body(n, carry)
        return carry
    return lax.fori_loop(0, count, body, carry)


def attend(own, meta, query, buf, offs):
    rows = query.shape[0]
    groups = H // KV
    half = rows // 2
    blocks, padded, wide = buf.shape
    span = groups * HD
    width = groups * half
    keys = blocks * rows
    steps = 2 * blocks // CHUNK_BLOCKS + 1
    which = (lambda m: m[0]) if own else (lambda m: 1 - m[0])
    head = lambda i, m: (0, which(m))
    return pl.pallas_call(
        functools.partial(attend_kernel, 4 if own else 4 + 2 * blocks),
        grid_spec=pltpu.PrefetchScalarGridSpec(
            num_scalar_prefetch=1,
            grid=(1,),
            in_specs=[
                pl.BlockSpec((rows, span), head),
                fixed((blocks, padded, wide)),
                fixed((8, width)),
            ],
            out_specs=[
                fixed((rows, span)),
                fixed((2, HD, width)),
                fixed((2, 8, width)),
            ],
            scratch_shapes=[
                pltpu.VMEM((keys, HD), bf16),
                pltpu.VMEM((keys, HD), bf16),
                pltpu.VMEM((2, width, HD), bf16),
                pltpu.VMEM((steps, 8, width), f32),
                pltpu.VMEM((steps, 8, width), f32),
                pltpu.VMEM((steps, HD, width), f32),
            ],
        ),
        out_shape=[
            jax.ShapeDtypeStruct((rows, span), bf16),
            jax.ShapeDtypeStruct((2, HD, width), f32),
            jax.ShapeDtypeStruct((2, 8, width), f32),
        ],
        compiler_params=params(20 + blocks * rows * HD // 2**16),
        cost_estimate=cost(
            rows * keys * H * HD, blocks * padded * wide * 2, rows * keys * H // 4
        ),
        name="attend",
    )(meta, query, buf, offs)


def attend_back_kernel(
    at,
    meta_ref,
    q_ref,
    do_ref,
    buf_ref,
    offs_ref,
    attt_ref,
    lse_ref,
    cos_ref,
    sin_ref,
    *refs,
):
    (
        dq_ref,
        dbuf_ref,
        keys_ref,
        vals_ref,
        dkeys_ref,
        dvals_ref,
        query_ref,
        grad_ref,
        delta_ref,
        dquery_ref,
    ) = refs
    blocks = buf_ref.shape[0]
    half = q_ref.shape[0] // 2
    groups = q_ref.shape[1] // HD
    chunk = CHUNK_BLOCKS * half
    scale = 1.0 / math.sqrt(HD)
    factor = LOG2E * scale
    count = 2 * blocks // CHUNK_BLOCKS - 1
    place_keys(meta_ref, at, buf_ref, keys_ref, vals_ref, half, blocks)
    dkeys_ref[...] = jnp.zeros_like(dkeys_ref)
    dvals_ref[...] = jnp.zeros_like(dvals_ref)
    dquery_ref[...] = jnp.zeros_like(dquery_ref)
    for part in range(2):
        query_ref[part] = stack_heads(q_ref, part, half, groups)
        grad = stack_heads(do_ref, part, half, groups)
        grad_ref[part] = grad
        delta = jnp.sum(grad.astype(f32).T * attt_ref[part], axis=0, keepdims=True)
        delta_ref[part] = jnp.broadcast_to(delta, delta_ref.shape[1:])
    full = [lax.div(meta_ref[1 + part], CHUNK_BLOCKS) for part in range(2)]

    def step(part, j, edge):
        rows = pl.ds(pl.multiple_of(j * chunk, 16), chunk)
        keys = keys_ref[rows, :]
        query, grad = query_ref[part], grad_ref[part]
        scores = dot_nt(keys, query)
        weights = jnp.exp2(scores * factor - lse_ref[part, 0:1, :])
        if edge is not None:
            row = lax.broadcasted_iota(jnp.int32, scores.shape, 0) + (j * chunk - edge * half)
            weights = jnp.where(row <= offs_ref[0:1, :], weights, 0.0)
        dweights = dot_nt(vals_ref[rows, :], grad)
        dscores = (weights * (dweights - delta_ref[part, 0:1, :])).astype(bf16)
        dvals_ref[rows, :] += dot(weights.astype(bf16), grad)
        dkeys_ref[rows, :] += dot(dscores, query)
        dquery_ref[part] += dot_tn(keys, dscores)

    def full_step(n):
        late = n >= full[0]
        step(jnp.where(late, 1, 0), n - jnp.where(late, full[0], 0), None)

    for_steps(count, full_step)
    for part in range(2):
        step(part, full[part], meta_ref[1 + part])
    for part in range(2):
        rowwise = dquery_ref[part].T * scale
        these = slice(part * half, (part + 1) * half)
        for g in range(groups):
            turned = turn(rowwise[g * half : (g + 1) * half], cos_ref[these], -sin_ref[these])
            dq_ref[these, g * HD : (g + 1) * HD] = turned.astype(bf16)

    for block in range(blocks):
        for part in range(2):
            rows = pl.ds(pl.multiple_of(meta_ref[at + block * 2 + part] * half, 16), half)
            here = slice(part * half, (part + 1) * half)
            dbuf_ref[block, here, :HD] = (dkeys_ref[rows, :] * scale).astype(bf16)
            dbuf_ref[block, here, HD:] = dvals_ref[rows, :].astype(bf16)


def attend_back(own, meta, query, grad, buf, offs, attt, lse, cos, sin):
    rows = query.shape[0]
    groups = H // KV
    half = rows // 2
    blocks, padded, wide = buf.shape
    span = groups * HD
    width = groups * half
    keys = blocks * rows
    which = (lambda m: m[0]) if own else (lambda m: 1 - m[0])
    head = lambda i, m: (0, which(m))
    need = blocks * rows * (2 * HD * 2 + 2 * HD * 4 + 3 * wide * 2)
    return pl.pallas_call(
        functools.partial(attend_back_kernel, 4 if own else 4 + 2 * blocks),
        grid_spec=pltpu.PrefetchScalarGridSpec(
            num_scalar_prefetch=1,
            grid=(1,),
            in_specs=[
                pl.BlockSpec((rows, span), head),
                pl.BlockSpec((rows, span), head),
                fixed((blocks, padded, wide)),
                fixed((8, width)),
                fixed((2, HD, width)),
                fixed((2, 8, width)),
                fixed((rows, HD)),
                fixed((rows, HD)),
            ],
            out_specs=[fixed((rows, span)), fixed((blocks, rows, wide))],
            scratch_shapes=[
                pltpu.VMEM((keys, HD), bf16),
                pltpu.VMEM((keys, HD), bf16),
                pltpu.VMEM((keys, HD), f32),
                pltpu.VMEM((keys, HD), f32),
                pltpu.VMEM((2, width, HD), bf16),
                pltpu.VMEM((2, width, HD), bf16),
                pltpu.VMEM((2, 8, width), f32),
                pltpu.VMEM((2, HD, width), f32),
            ],
        ),
        out_shape=[
            jax.ShapeDtypeStruct((rows, span), bf16),
            jax.ShapeDtypeStruct((blocks, rows, wide), bf16),
        ],
        compiler_params=params(24 + need // 2**20),
        cost_estimate=cost(
            2.5 * rows * keys * H * HD, blocks * padded * wide * 4, rows * keys * H // 4
        ),
        name="attend_back",
    )(meta, query, grad, buf, offs, attt, lse, cos, sin)


def expert_kernel(
    plane,
    meta_ref,
    mine_ref,
    theirs_ref,
    dy_mine_ref,
    dy_theirs_ref,
    wg_ref,
    wu_ref,
    wd_ref,
    wr_ref,
    out_mine_ref,
    out_theirs_ref,
    dx_mine_ref,
    dx_theirs_ref,
    hidden_ref,
    dhid_ref,
    gate_ref,
):
    core = meta_ref[0]
    expert = meta_ref[1]
    rows, half = mine_ref.shape[2], mine_ref.shape[3]
    here = pl.ds(pl.multiple_of(core * half, LANES), half)
    there = pl.ds(pl.multiple_of((1 - core) * half, LANES), half)
    x_mine = mine_ref[0].reshape(2 * rows, half)
    x_theirs = jnp.concatenate([theirs_ref[0, 1], theirs_ref[0, 0]], axis=0)
    gate_pre = dot(x_mine, wg_ref[here, :]) + dot(x_theirs, wg_ref[there, :])
    up_pre = dot(x_mine, wu_ref[here, :]) + dot(x_theirs, wu_ref[there, :])
    logits = dot(x_mine, wr_ref[here, :]) + dot(x_theirs, wr_ref[there, :])
    marked = dy_mine_ref[0].reshape(2 * rows, half + LANES)
    dy_here = marked[:, :half].astype(f32)
    dy_there = jnp.concatenate(
        [dy_theirs_ref[0, 1, :, :half], dy_theirs_ref[0, 0, :, :half]], axis=0
    ).astype(f32)
    chosen = marked[:, half:].astype(f32) > 0.5
    top = jnp.max(jnp.where(chosen, logits, negative), axis=-1, keepdims=True)
    shares = jnp.where(chosen, jnp.exp(logits - top), 0.0)
    lane = lax.broadcasted_iota(jnp.int32, logits.shape, 1)
    own = jnp.sum(jnp.where(lane == expert, shares, 0.0), axis=-1, keepdims=True)
    gate = own / jnp.sum(shares, axis=-1, keepdims=True)
    routed = jnp.sum(jnp.where((lane == expert) & chosen, 1.0, 0.0), axis=-1, keepdims=True)
    gate_ref[...] = jnp.broadcast_to(gate, gate_ref.shape)

    sig = jax.nn.sigmoid(gate_pre)
    silu = gate_pre * sig
    hidden = (silu * up_pre).astype(bf16)
    hidden_ref[...] = hidden
    result_here = dot(hidden, wd_ref[:, here]).astype(bf16).astype(f32)
    result_there = dot(hidden, wd_ref[:, there]).astype(bf16).astype(f32)
    d_gate = routed * (
        jnp.sum(dy_here * result_here, axis=-1, keepdims=True)
        + jnp.sum(dy_there * result_there, axis=-1, keepdims=True)
    )
    out_here = (gate * result_here).astype(bf16)
    out_there = (gate * result_there).astype(bf16)
    d_hidden = dot_nt((gate * dy_here).astype(bf16), wd_ref[:, here]) + dot_nt(
        (gate * dy_there).astype(bf16), wd_ref[:, there]
    )
    d_up = (d_hidden * silu).astype(bf16)
    d_gp = (d_hidden * up_pre * (sig * (1.0 + gate_pre * (1.0 - sig)))).astype(bf16)
    inner = d_gp.shape[1]
    dhid_ref[:, :inner] = d_gp
    dhid_ref[:, inner:] = d_up
    high = d_gate.astype(bf16).astype(f32)
    low = d_gate - high
    spot = jnp.where(lane == expert, 1.0, 0.0)
    dx_here = (dot_nt(d_gp, wg_ref[here, :]) + dot_nt(d_up, wu_ref[here, :])).astype(bf16)
    dx_there = (dot_nt(d_gp, wg_ref[there, :]) + dot_nt(d_up, wu_ref[there, :])).astype(bf16)
    col_here = (spot * jnp.where(core == 0, high, low)).astype(bf16)
    col_there = (spot * jnp.where(core == 0, low, high)).astype(bf16)
    for t in range(2):
        these = slice(t * rows, (t + 1) * rows)
        dx_mine_ref[0, t, :, :half] = dx_here[these]
        dx_mine_ref[0, t, :, half:] = col_here[these]
        dx_theirs_ref[0, 1 - t, :, :half] = dx_there[these]
        dx_theirs_ref[0, 1 - t, :, half:] = col_there[these]
        out_mine_ref[0, t] = out_here[these]
        out_theirs_ref[0, 1 - t] = out_there[these]


def run_expert(plane, first, meta, mine, theirs, dy_mine, dy_theirs, wg, wu, wd, wr):
    chips, _, rows, half = mine.shape
    width, inner = wg.shape
    swap = lambda g: plane.swapped(g + first) - first
    pair = lambda w: pl.BlockSpec((1, 2, rows, w), lambda g, m: (g, 0, 0, 0))
    swapped = lambda w: pl.BlockSpec((1, 2, rows, w), lambda g, m: (swap(g), 0, 0, 0))
    flat = lambda w: pl.BlockSpec((2 * rows, w), lambda g, m: (g, 0))
    total_rows = chips * 2 * rows
    return pl.pallas_call(
        functools.partial(expert_kernel, plane),
        grid_spec=pltpu.PrefetchScalarGridSpec(
            num_scalar_prefetch=1,
            grid=(chips,),
            in_specs=[
                pair(half),
                swapped(half),
                pair(half + LANES),
                swapped(half + LANES),
                fixed((width, inner)),
                fixed((width, inner)),
                fixed((inner, width)),
                fixed((width, wr.shape[1])),
            ],
            out_specs=[
                pair(half),
                swapped(half),
                pair(half + LANES),
                swapped(half + LANES),
                flat(inner),
                flat(2 * inner),
                flat(LANES),
            ],
        ),
        out_shape=[
            jax.ShapeDtypeStruct((chips, 2, rows, half), bf16),
            jax.ShapeDtypeStruct((chips, 2, rows, half), bf16),
            jax.ShapeDtypeStruct((chips, 2, rows, half + LANES), bf16),
            jax.ShapeDtypeStruct((chips, 2, rows, half + LANES), bf16),
            jax.ShapeDtypeStruct((total_rows, inner), bf16),
            jax.ShapeDtypeStruct((total_rows, 2 * inner), bf16),
            jax.ShapeDtypeStruct((total_rows, LANES), f32),
        ],
        compiler_params=params(36),
        cost_estimate=cost(
            12 * total_rows * width * inner, 20 * total_rows * width, total_rows * inner
        ),
        name="expert",
    )(meta, mine, theirs, dy_mine, dy_theirs, wg, wu, wd, wr)


def rows_in_order(plane, own0, own, other0, other, mine):
    if mine:
        return [ref[g, t] for ref in (own0, own) for g in range(ref.shape[0]) for t in range(2)]
    parts = [other0[0, 1], other0[0, 0]]
    for g in range(1, plane.chips):
        at = plane.swapped(g) - 1
        parts += [other[at, 1], other[at, 0]]
    return parts


def expert_grad_kernel(plane, weigh, meta_ref, *refs):
    lefts, refs = refs[:4], refs[4:]
    if weigh:
        gate0_ref, gate_ref, right0_ref, right_ref, _, out_ref = refs
    else:
        right0_ref, right_ref, out_ref = refs
    step = pl.program_id(0)
    halves = pl.num_programs(0) // 2
    first = right0_ref.shape[0]

    def give(parts):
        if weigh:
            rows = parts[0].shape[0]
            gates = [gate0_ref[t * rows : (t + 1) * rows, 0:1] for t in range(2)]
            gates += [
                gate_ref[n * rows : (n + 1) * rows, 0:1] for n in range(len(parts) - 2)
            ]
            parts = [(g * p.astype(f32)).astype(bf16) for g, p in zip(gates, parts)]
        near = jnp.concatenate(parts[:2], axis=0)
        far = jnp.concatenate(parts[2:], axis=0)
        out_ref[...] = (dot_tn(near, right0_ref[...]) + dot_tn(far, right_ref[...])).astype(bf16)

    @pl.when(step < halves)
    def _():
        give(rows_in_order(plane, *lefts, True))

    @pl.when(step >= halves)
    def _():
        give(rows_in_order(plane, *lefts, False))


def expert_grad(plane, meta, lefts, right0, right, half, gates=None, grads=None):
    tile = half // 2
    rows = lefts[0].shape[2]
    inner = right.shape[1]
    own = lambda a: pl.BlockSpec(
        a.shape[:3] + (tile,), lambda i, m: (0, 0, 0, jnp.minimum(i, 1))
    )
    other = lambda a: pl.BlockSpec(
        a.shape[:3] + (tile,), lambda i, m: (0, 0, 0, jnp.maximum(i - 2, 0))
    )
    count = right0.shape[0] + right.shape[0]
    need = count * (8 * tile * 2 + inner * 2) + 3 * tile * inner * 4
    specs = [own(lefts[0]), own(lefts[1]), other(lefts[2]), other(lefts[3])]
    args = list(lefts)
    if gates:
        specs += [fixed(g.shape) for g in gates]
        args += list(gates)
    specs += [fixed(right0.shape), fixed(right.shape)]
    args += [right0, right]
    if gates:
        specs.append(pl.BlockSpec(memory_space=pl.ANY))
        args.append(grads)
        need += count * LANES * 4
        out_shape, place = grads.shape, 2
    else:
        out_shape, place = (2 * half, inner + inner // 2), 0
    return pl.pallas_call(
        functools.partial(expert_grad_kernel, plane, bool(gates)),
        grid_spec=pltpu.PrefetchScalarGridSpec(
            num_scalar_prefetch=1,
            grid=(4,),
            in_specs=specs,
            out_specs=pl.BlockSpec(
                (tile, inner), lambda i, m: ((m[0] ^ (i // 2)) * 2 + i % 2, place)
            ),
        ),
        out_shape=jax.ShapeDtypeStruct(out_shape, bf16),
        input_output_aliases={len(args): 0} if gates else {},
        compiler_params=params(8 + need // 2**20),
        cost_estimate=cost(4 * count * half * inner, 6 * count * half),
        name="down_grad" if gates else "up_grad",
    )(meta, *args)


def together(*values):
    return lax.optimization_barrier(values)


def per_device(
    tokens,
    gain_attn,
    w_query,
    w_key,
    w_value,
    w_out,
    gain_moe,
    w_router,
    w_gate,
    w_up,
    w_down,
    routes,
    positions,
    cotangent,
):
    rows = tokens.shape[1]
    width = tokens.shape[2]
    half = rows // 2
    split = width // 2
    groups = H // KV
    kv_width = KV * HD
    experts = w_router.shape[1]
    inner = w_gate.shape[2]
    plane = Plane(w_gate.shape[0] * lax.axis_size("expert"))
    last = plane.steps - 1
    contexts = lax.axis_size("context")
    copies = lax.axis_size("dp")
    blocks = plane.size * contexts
    index = lax.axis_index("expert")
    core = index % 2
    places = positions[0]
    x = tokens[0]
    gain_one, gain_two = gain_attn, gain_moe
    swap_context = [(i, i ^ 1) for i in range(contexts)]
    swap_copies = [(i, i ^ 1) for i in range(copies)]

    def by_core(zero, one):
        return jnp.where(core == 0, zero, one)

    def mix(value, k):
        return lax.ppermute(value, "expert", plane.mixed[k])

    def sibling(value):
        return lax.ppermute(value, "expert", plane.sibling)

    tcos, tsin = rope_tables(2 * blocks, half)
    own_bases = jnp.stack([places[0], places[half]]) // half
    front_meta = jnp.concatenate([core[None], own_bases]).astype(jnp.int32)
    core_row = jnp.reshape(core, (1,)).astype(jnp.int32)
    xn_one, packed, cos, sin = front(
        core_row, places, x, gain_one, w_key, w_value, tcos, tsin
    )

    lanes = jnp.arange(LANES, dtype=jnp.int32)
    marks = jnp.any(routes[0][:, :, None] == lanes[None, None, :], axis=1).astype(bf16)
    dy, marks = after(cotangent[0], packed), after(marks, packed)
    dy_keep = jnp.concatenate([by_core(dy[:, :split], dy[:, split:]), marks], axis=1)
    dy_send = jnp.concatenate([by_core(dy[:, split:], dy[:, :split]), marks], axis=1)

    router_wide = jnp.pad(w_router, ((0, 0), (0, LANES - experts)))
    weights = (w_gate[0], w_up[0], w_down[0], router_wide)
    dy_m0 = jnp.stack([dy_keep, sibling(dy_send)])[None]
    dy_t0 = jnp.stack([sibling(dy_keep), dy_send])[None]
    if contexts > 1:
        arrived = lax.ppermute(packed, "context", swap_context)
        arrived, dy_m0, dy_t0, front_meta = together(arrived, dy_m0, dy_t0, front_meta)
        packed = jnp.stack([packed, arrived], axis=1)
    else:
        packed = packed[:, None]
    held = jnp.stack([packed[0], sibling(packed[1])])[None]
    query = make_query(xn_one, w_query, cos, sin)
    for k in range(plane.steps):
        if k == last:
            held, query = together(held, query)
        held = jnp.concatenate([held, mix(held, k)])
    mine = held.reshape(blocks, rows + PAD_ROWS, kv_width)
    theirs = sibling(held).reshape(blocks, rows + PAD_ROWS, kv_width)
    own_order = mine[:, rows :: PAD_ROWS // 2, 0].astype(f32).astype(jnp.int32).reshape(-1)
    spots = [
        ((plane.swapped(g) * 2 + 1 - t) * contexts + c) * 2 + part
        for g in range(plane.chips)
        for t in range(2)
        for c in range(contexts)
        for part in range(2)
    ]
    other_order = jnp.stack([own_order[spot] for spot in spots])
    meta = jnp.concatenate([front_meta, front_meta[:1], own_order, other_order])
    offs = jnp.asarray(np.tile(np.arange(groups * half, dtype=np.int32) % half, (8, 1)))

    dy_held, meta = together(dy_m0, meta)
    dy_came = mix(dy_held, 0)
    att_mine, *own_stats = attend(True, meta, query, mine, offs)
    dy_came, theirs, att_mine = together(dy_came, theirs, att_mine)
    dy_held = jnp.concatenate([dy_held, dy_came])
    for k in range(1, last):
        dy_held = jnp.concatenate([dy_held, mix(dy_held, k)])
    dy_held, theirs = together(dy_held, theirs)
    dy_came = mix(dy_held, last)
    att_theirs, *other_stats = attend(False, meta, query, theirs, offs)
    hidden, xn_two, keep, send = join(front_meta, att_mine, att_theirs, w_out, x, gain_two)

    offsets = np.array(
        [[plane.chip_offset(c, g) // 2 for g in range(plane.chips)] for c in range(2)], np.int32
    )
    chips = (index // 2) ^ by_core(offsets[0], offsets[1])
    expert_meta = jnp.concatenate([core[None], index[None], chips]).astype(jnp.int32)
    mine0 = jnp.stack([keep, sibling(send)])[None]
    theirs0 = jnp.stack([sibling(keep), send])[None]
    held = mine0
    for k in range(plane.steps):
        came = mix(held, k)
        if k == last - 1:
            came, dy_came = together(came, dy_came)
        if k == last:
            out_m0, out_t0, dx_m0, dx_t0, hid0, dhid0, gate0 = run_expert(
                plane, 0, expert_meta, after(mine0, held), theirs0, dy_m0, dy_t0, *weights
            )
            dy_m1 = jnp.concatenate([dy_held, dy_came])[1:]
            dy_t1 = sibling(dy_m1)
            came, hid0, dy_t1 = together(came, hid0, dy_t1)
        held = jnp.concatenate([held, came])
    mine1 = held[1:]
    theirs1 = sibling(mine1)
    out_m1, out_t1, dx_m1, dx_t1, hid1, dhid1, gate1 = run_expert(
        plane, 1, expert_meta, mine1, theirs1, dy_m1, dy_t1, *weights
    )

    def pick(terms, k):
        lo, hi = 2**k, 2 ** (k + 1)
        return total([a[lo - at : hi - at] for at, a in terms if at <= lo and hi - at <= a.shape[0]])

    def parts_of(terms, slot):
        return total([a[0, slot] for at, a in terms if at == 0])

    dx_r0, dx_r1 = sibling(dx_t0), sibling(dx_t1)
    grads = expert_grad(
        plane, expert_meta, (mine0, mine1, theirs0, theirs1), dhid0, dhid1, split
    )
    dx_r1, grads = together(dx_r1, grads)
    terms = [(0, dx_m0), (1, dx_m1), (0, dx_r0), (1, dx_r1)]
    for k in reversed(range(plane.steps)):
        send = pick(terms, k)
        arrived = mix(send, k)
        if k == last:
            grads = expert_grad(
                plane,
                expert_meta,
                (dy_m0, dy_m1, dy_t0, dy_t1),
                after(hid0, send),
                hid1,
                split,
                (gate0, gate1),
                grads,
            )
            arrived, grads = together(arrived, grads)
        terms.append((0, arrived))
    expert_grads = lax.psum_scatter(grads, ("context", "dp"), scatter_dimension=0, tiled=True)
    dx_keep = parts_of(terms, 0)
    dx_other = sibling(parts_of(terms, 1))

    marked = jnp.concatenate([dy, marks], axis=1)
    d_state, d_low, d_logits, d_gain_moe, d_attended = middle(
        front_meta,
        dx_keep,
        dx_other,
        hidden,
        xn_two,
        gain_two,
        marked,
        router_wide,
        w_out,
    )
    dq_theirs, d_theirs = attend_back(
        False, meta, query, d_attended, theirs, offs, *other_stats, cos, sin
    )
    d_sent = sibling(d_theirs)
    d_attended = after(d_attended, dq_theirs)
    dq_mine, d_mine = attend_back(
        True, meta, query, d_attended, mine, offs, *own_stats, cos, sin
    )

    custom = contexts == 2 and copies == 2 and (width // plane.chips) % LANES == 0
    kv_shape = (plane.chips, 2, contexts, rows, kv_width)
    terms = [(0, d_mine.reshape(kv_shape)), (0, d_sent.reshape(kv_shape))]
    if custom:
        place = lax.axis_index("context") * 2 + lax.axis_index("dp")
        dense_meta = jnp.concatenate([core[None], place[None], chips]).astype(jnp.int32)
        xn_other, low_other = sibling(xn_one), sibling(d_low)
        att_other, dq_other = sibling(att_theirs), sibling(dq_theirs)

    def step_sum(steps, came, k):
        return total([steps[k]] + [a[2**k : 2 ** (k + 1)] for a in came])

    def fold(values, axis, pairs):
        return lax.ppermute(total([a[1] for a in values]), axis, pairs)

    for k in reversed(range(plane.steps)):
        send = pick(terms, k)
        arrived = mix(send, k)
        if k == last and custom:
            *out_steps, out_own = dense_grad(
                plane, dense_meta, after(d_low, send), low_other, att_mine, att_other
            )
            *que_steps, que_own = dense_grad(
                plane, dense_meta, xn_one, xn_other, after(dq_mine, out_own), dq_other
            )
            arrived, out_steps, que_own = together(arrived, out_steps, que_own)
        if k == 0:
            dxq = times_transposed(front_meta, after(dq_mine, send), dq_theirs, w_query)
            arrived, dxq = together(arrived, dxq)
            if custom:
                out_steps[last], send = together(out_steps[last], send)
                out_came = [mix(out_steps[last], last)]
        terms.append((0, arrived))
    dkv_keep = parts_of(terms, 0)
    dkv_other = sibling(parts_of(terms, 1))
    dkv = jnp.stack([dkv_keep, dkv_other], axis=1)
    mix_t0, mix_t1, dkv = together(out_t0, out_t1, dkv)
    mix_terms = [(0, out_m0), (1, out_m1), (0, sibling(mix_t0)), (1, sibling(mix_t1))]
    mix_send = pick(mix_terms, last)
    if custom:
        que_steps[last], dkv = together(que_steps[last], dkv)
        que_came = [mix(que_steps[last], last)]
    if contexts > 1:
        dkv_came = lax.ppermute(dkv[1], "context", swap_context)
        dkv_came, mix_send = together(dkv_came, mix_send)
        if custom:
            for k in reversed(range(last)):
                send = step_sum(out_steps, out_came, k)
                dkv_came, send = together(dkv_came, send)
                out_came.append(mix(send, k))
        dkv = dkv[0].astype(f32) + dkv_came.astype(f32)
    else:
        dkv = dkv[0].astype(f32)

    d_in, d_kv, d_gain_attn = back(
        front_meta, dkv[0], dkv[1], dxq, x, gain_one, d_state, w_key, w_value, cos, sin
    )

    if custom:
        for k in reversed(range(last)):
            que_came[-1], d_kv = together(que_came[-1], d_kv)
            send = step_sum(que_steps, que_came, k)
            send, d_kv = together(send, d_kv)
            que_came.append(mix(send, k))
        d_own = by_core(d_kv[:, :kv_width], d_kv[:, kv_width:])
        d_sends = sibling(by_core(d_kv[:, kv_width:], d_kv[:, :kv_width]))
        *small_steps, small_own = dense_grad(
            plane,
            dense_meta,
            xn_one,
            xn_other,
            d_own,
            d_sends,
            (xn_two, d_logits, d_gain_attn, d_gain_moe),
        )
        outs = [out_own[0]] + [a[0] for a in out_came]
        small_steps[last], outs[-1] = together(small_steps[last], outs[-1])
        small_came = []
        for k in reversed(range(plane.steps)):
            send = step_sum(small_steps, small_came, k)
            if k == 0:
                send, que_came = together(send, que_came)
            small_came.append(mix(send, k))
        ques = [que_own[0]] + [a[0] for a in que_came]
        small = [small_own[0]] + [a[0] for a in small_came]
        values = (outs, ques, small)
        send = jnp.concatenate([total([a[1] for a in v]) for v in values], -1)
        mix_send, send = together(mix_send, send)
        arrived = lax.ppermute(send, "dp", swap_copies)
        mix_terms.append((0, mix(mix_send, last)))
        arrived, mix_came, expert_grads = together(arrived, mix_terms[-1][1], expert_grads)
        mix_terms[-1] = (0, mix_came)
        cuts = (slice(None, split), slice(split, width), slice(width, None))
        values = [[a[0] for a in v] + [arrived[..., cut]] for v, cut in zip(values, cuts)]
        send = jnp.concatenate([total([a[1] for a in v]) for v in values], -1)
        arrived = lax.ppermute(send, "context", swap_context)
        for k in reversed(range(last)):
            mix_send, send = together(pick(mix_terms, k), send)
            mix_terms.append((0, mix(mix_send, k)))
        mix_terms[-1] = (0, after(mix_terms[-1][1], send))
    else:
        for k in reversed(range(plane.steps)):
            mix_terms.append((0, mix(mix_send if k == last else pick(mix_terms, k), k)))

    def split_grads(grads):
        return (
            grads[:, :inner].astype(f32)[None],
            grads[:, inner : 2 * inner].astype(f32)[None],
            grads[:, 2 * inner :].astype(f32).T[None],
        )

    keep, other = parts_of(mix_terms, 0), sibling(parts_of(mix_terms, 1))
    mixture = jnp.concatenate([by_core(keep, other), by_core(other, keep)], axis=1)
    output = (hidden + mixture.astype(f32)).astype(bf16)[None]
    grad_gate, grad_up, grad_down = split_grads(expert_grads)
    if custom:
        arrived, output, grad_gate, grad_up, grad_down = together(
            arrived, output, grad_gate, grad_up, grad_down
        )
        values = [[a[0] for a in v] + [arrived[..., cut]] for v, cut in zip(values, cuts)]
        send = jnp.concatenate([total([a[1] for a in v]) for v in values], -1)
        own = jnp.concatenate([sum(a[0].astype(f32) for a in v) for v in values], -1)
        arrived = sibling(send)
        grad_query, grad_out, grad_key, grad_value, extra = finish(
            core_row, own, arrived, split, kv_width
        )
    else:
        in_order = lambda a, b: jnp.concatenate([by_core(a, b), by_core(b, a)], axis=1)
        scatter = lambda v: lax.psum_scatter(
            v.astype(bf16), ("expert", "context", "dp"), scatter_dimension=0, tiled=True
        ).astype(f32)
        grad_query = scatter(dot_tn(xn_one, in_order(dq_mine, dq_theirs)))
        grad_out = scatter(dot_tn(d_low, in_order(att_mine, att_theirs)))
        grad_kv = scatter(dot_tn(xn_one, d_kv))
        grad_key, grad_value = grad_kv[:, :kv_width], grad_kv[:, kv_width:]
        router = dot_tn(xn_two, d_logits)[:, : LANES - 2]
        extra = scatter(
            jnp.concatenate([router, d_gain_attn[:1].T, d_gain_moe[:1].T], axis=1)
        )
    return (
        output,
        d_in[None],
        extra[:, LANES - 2],
        grad_query,
        grad_key,
        grad_value,
        grad_out.T,
        extra[:, LANES - 1],
        extra[:, :experts],
        grad_gate,
        grad_up,
        grad_down,
    )


def solution(mesh):
    in_specs = (
        P("dp", ("expert", "context"), None),
        P(),
        P(),
        P(),
        P(),
        P(),
        P(),
        P(),
        P("expert", None, None),
        P("expert", None, None),
        P("expert", None, None),
        P("dp", ("expert", "context"), None),
        P("dp", ("expert", "context")),
        P("dp", ("expert", "context"), None),
    )
    out_specs = (
        P("dp", ("expert", "context"), None),
        P("dp", ("expert", "context"), None),
        P(("expert", "context", "dp")),
        P(("expert", "context", "dp"), None),
        P(("expert", "context", "dp"), None),
        P(("expert", "context", "dp"), None),
        P(None, ("expert", "context", "dp")),
        P(("expert", "context", "dp")),
        P(("expert", "context", "dp"), None),
        P("expert", ("context", "dp"), None),
        P("expert", ("context", "dp"), None),
        P("expert", None, ("context", "dp")),
    )
    return jax.shard_map(
        per_device, mesh=mesh, in_specs=in_specs, out_specs=out_specs, check_vma=False
    )
```

```python
import functools
import math

import jax
import jax.numpy as jnp
import numpy as np
from jax import lax
from jax.experimental import pallas as pl
from jax.experimental.pallas import tpu as pltpu
from jax.sharding import PartitionSpec as P

H = 12
KV = 2
HD = 128
TOP = 4

eps = 1e-06
rope_base = 1000000.0
negative = -1e30
LANES = 128
JOIN_TILES = 3
CHUNK_BLOCKS = 8
PAD_ROWS = 16
bf16 = jnp.bfloat16
f32 = jnp.float32
LOG2E = 1.4426950408889634


def dot(a, b):
    return lax.dot_general(a, b, (((1,), (0,)), ((), ())), preferred_element_type=f32)


def dot_nt(a, b):
    return lax.dot_general(a, b, (((1,), (1,)), ((), ())), preferred_element_type=f32)


def dot_tn(a, b):
    return lax.dot_general(a, b, (((0,), (0,)), ((), ())), preferred_element_type=f32)


def params(mebibytes):
    return pltpu.CompilerParams(
        dimension_semantics=("arbitrary",), vmem_limit_bytes=min(int(mebibytes), 60) * 1024 * 1024
    )


def after(value, *others):
    return lax.optimization_barrier((value,) + others)[0]


def cost(flops, moved, exps=0):
    return pl.CostEstimate(flops=int(flops), bytes_accessed=int(moved), transcendentals=int(exps))


def turn(values, cos, sin):
    return values * cos + pltpu.roll(values, HD // 2, 1) * sin


def norm_scale(values):
    return lax.rsqrt(jnp.mean(values * values, axis=-1, keepdims=True) + eps)


def rope_tables(count, half):
    freqs = rope_base ** (-np.arange(0, HD, 2) / HD)
    angles = np.concatenate([np.arange(count) * half, np.arange(half)])[:, None] * freqs[None, :]
    twice = np.concatenate([angles, angles], axis=1)
    return jnp.asarray(np.cos(twice), f32), jnp.asarray(np.sin(twice), f32)


def fixed(shape):
    zeros = (0,) * len(shape)
    return pl.BlockSpec(shape, lambda *_: zeros, pipeline_mode=pl.Buffered(1))


def front_kernel(
    core_ref,
    places_ref,
    x_ref,
    gain_ref,
    wk_ref,
    wv_ref,
    tcos_ref,
    tsin_ref,
    xn_ref,
    packed_ref,
    cos_ref,
    sin_ref,
):
    core = core_ref[0]
    rows = x_ref.shape[0]
    half = rows // 2
    bases = [lax.div(places_ref[part * half], half) for part in range(2)]
    count = tcos_ref.shape[0] - half
    sign = jnp.where(lax.broadcasted_iota(jnp.int32, (half, HD), 1) < HD // 2, -1.0, 1.0)
    for part in range(2):
        these = slice(part * half, (part + 1) * half)
        base = pl.ds(bases[part], 1)
        cos_base, sin_base = tcos_ref[base, :], tsin_ref[base, :]
        cos_off, sin_off = tcos_ref[count:, :], tsin_ref[count:, :]
        cos_ref[these, :] = cos_base * cos_off - sin_base * sin_off
        sin_ref[these, :] = (sin_base * cos_off + cos_base * sin_off) * sign
    values = x_ref[...].astype(f32)
    normed = (values * norm_scale(values) * gain_ref[...]).astype(bf16)
    xn_ref[...] = normed
    keys = dot(normed, wk_ref[...])
    vals = dot(normed, wv_ref[...]).astype(bf16)
    edge = lax.broadcasted_iota(jnp.int32, (PAD_ROWS, 2 * HD), 0) < PAD_ROWS // 2
    tail = jnp.where(edge, bases[0].astype(f32), bases[1].astype(f32)).astype(bf16)
    for head in range(KV):
        slot = jnp.where(core == head, 0, 1)
        span = slice(head * HD, (head + 1) * HD)
        turned = turn(keys[:, span], cos_ref[...], sin_ref[...]).astype(bf16)
        packed_ref[slot, :rows, :HD] = turned
        packed_ref[slot, :rows, HD:] = vals[:, span]
        packed_ref[slot, rows:, :] = tail


def front(core, places, x, gain, wk, wv, tcos, tsin):
    rows, width = x.shape
    return pl.pallas_call(
        front_kernel,
        grid_spec=pltpu.PrefetchScalarGridSpec(
            num_scalar_prefetch=2,
            grid=(1,),
            in_specs=[fixed(a.shape) for a in (x, gain, wk, wv, tcos, tsin)],
            out_specs=[
                fixed((rows, width)),
                fixed((2, rows + PAD_ROWS, 2 * HD)),
                fixed((rows, HD)),
                fixed((rows, HD)),
            ],
        ),
        out_shape=[
            jax.ShapeDtypeStruct((rows, width), bf16),
            jax.ShapeDtypeStruct((2, rows + PAD_ROWS, 2 * HD), bf16),
            jax.ShapeDtypeStruct((rows, HD), f32),
            jax.ShapeDtypeStruct((rows, HD), f32),
        ],
        compiler_params=params(60),
        cost_estimate=cost(4 * rows * width * KV * HD, 8 * rows * width),
        name="front",
    )(core, places, x, gain, wk, wv, tcos, tsin)


def query_kernel(x_ref, w_ref, cos_ref, sin_ref, out_ref):
    raw = dot(x_ref[...], w_ref[...])
    for head in range(raw.shape[1] // HD):
        span = slice(head * HD, (head + 1) * HD)
        out_ref[:, span] = turn(raw[:, span], cos_ref[...], sin_ref[...]).astype(bf16)


def make_query(x, w, cos, sin):
    rows, width = x.shape
    wide = w.shape[1]
    tile = 4 * HD
    return pl.pallas_call(
        query_kernel,
        grid=(wide // tile,),
        in_specs=[
            fixed((rows, width)),
            pl.BlockSpec((width, tile), lambda i: (0, i)),
            fixed((rows, HD)),
            fixed((rows, HD)),
        ],
        out_specs=pl.BlockSpec((rows, tile), lambda i: (0, i)),
        out_shape=jax.ShapeDtypeStruct((rows, wide), bf16),
        compiler_params=params(12),
        cost_estimate=cost(2 * rows * width * wide, 2 * width * wide),
        name="make_query",
    )(x, w, cos, sin)


def join_kernel(meta_ref, mine_ref, theirs_ref, w_ref, x_ref, gain_ref, hid_ref, xn_ref, keep_ref, send_ref):
    core = meta_ref[0]
    step = pl.program_id(0)
    width = hid_ref.shape[1]
    tile = width // JOIN_TILES
    span = pl.ds(pl.multiple_of(step * tile, LANES), tile)
    inner = mine_ref.shape[1]
    here = pl.ds(pl.multiple_of(core * inner, LANES), inner)
    there = pl.ds(pl.multiple_of((1 - core) * inner, LANES), inner)
    mixed = dot(mine_ref[...], w_ref[here, :]) + dot(theirs_ref[...], w_ref[there, :])
    hid_ref[:, span] = x_ref[:, span].astype(f32) + mixed

    @pl.when(step == pl.num_programs(0) - 1)
    def _():
        hidden = hid_ref[...]
        xn_ref[...] = (hidden * norm_scale(hidden) * gain_ref[...]).astype(bf16)
        half = width // 2
        keep_ref[...] = xn_ref[:, pl.ds(pl.multiple_of(core * half, LANES), half)]
        send_ref[...] = xn_ref[:, pl.ds(pl.multiple_of((1 - core) * half, LANES), half)]


def join(meta, mine, theirs, w, x, gain):
    rows, width = x.shape
    inner = w.shape[0]
    tile = width // JOIN_TILES
    return pl.pallas_call(
        join_kernel,
        grid_spec=pltpu.PrefetchScalarGridSpec(
            num_scalar_prefetch=1,
            grid=(width // tile,),
            in_specs=[
                fixed(mine.shape),
                fixed(theirs.shape),
                pl.BlockSpec((inner, tile), lambda i, m: (0, i)),
                fixed((rows, width)),
                fixed((width,)),
            ],
            out_specs=[
                fixed((rows, width)),
                fixed((rows, width)),
                fixed((rows, width // 2)),
                fixed((rows, width // 2)),
            ],
        ),
        out_shape=[
            jax.ShapeDtypeStruct((rows, width), f32),
            jax.ShapeDtypeStruct((rows, width), bf16),
            jax.ShapeDtypeStruct((rows, width // 2), bf16),
            jax.ShapeDtypeStruct((rows, width // 2), bf16),
        ],
        compiler_params=params(16),
        cost_estimate=cost(2 * rows * width * inner, 2 * width * inner),
        name="join",
    )(meta, mine, theirs, w, x, gain)


def middle_kernel(
    meta_ref,
    own_ref,
    other_ref,
    hid_ref,
    xn_ref,
    gain_ref,
    dy_ref,
    wr_ref,
    w_ref,
    dstate_ref,
    dlow_ref,
    dlog_ref,
    dgain_ref,
    datt_ref,
    dx_ref,
):
    core = meta_ref[0]
    step = pl.program_id(0)
    width = hid_ref.shape[1]
    half = width // 2

    @pl.when(step == 0)
    def _():
        dx_ref[:, pl.ds(pl.multiple_of(core * half, LANES), half)] = own_ref[:, :half].astype(f32)
        dx_ref[:, pl.ds(pl.multiple_of((1 - core) * half, LANES), half)] = other_ref[
            :, :half
        ].astype(f32)
        d_gate = own_ref[:, half:].astype(f32) + other_ref[:, half:].astype(f32)
        chosen = dy_ref[:, width:].astype(f32) > 0.5
        logits = dot(xn_ref[...], wr_ref[...])
        top = jnp.max(jnp.where(chosen, logits, negative), axis=-1, keepdims=True)
        shares = jnp.where(chosen, jnp.exp(logits - top), 0.0)
        gate = shares / jnp.sum(shares, axis=-1, keepdims=True)
        inner_sum = jnp.sum(gate * d_gate, axis=-1, keepdims=True)
        d_logits = (gate * (d_gate - inner_sum)).astype(bf16)
        dlog_ref[...] = d_logits
        d_xn = dx_ref[...] + dot_nt(d_logits, wr_ref[...])
        hidden = hid_ref[...]
        scale_row = norm_scale(hidden)
        normed = hidden * scale_row
        dgain_ref[...] = jnp.broadcast_to(
            jnp.sum(d_xn * normed, axis=0, keepdims=True), dgain_ref.shape
        )
        scaled = d_xn * gain_ref[...]
        inner_mean = jnp.mean(scaled * normed, axis=-1, keepdims=True)
        d_state = dy_ref[:, :width].astype(f32) + scale_row * (scaled - normed * inner_mean)
        dstate_ref[...] = d_state
        dlow_ref[...] = d_state.astype(bf16)

    datt_ref[...] = dot_nt(dlow_ref[...], w_ref[...]).astype(bf16)


def middle(meta, own, other, hidden, xn, gain, dy, wr, w):
    rows, width = hidden.shape
    inner = w.shape[0]
    tile = inner // JOIN_TILES
    return pl.pallas_call(
        middle_kernel,
        grid_spec=pltpu.PrefetchScalarGridSpec(
            num_scalar_prefetch=1,
            grid=(inner // tile,),
            in_specs=[fixed(a.shape) for a in (own, other, hidden, xn, gain, dy, wr)]
            + [pl.BlockSpec((tile, width), lambda i, m: (i, 0))],
            out_specs=[
                fixed((rows, width)),
                fixed((rows, width)),
                fixed((rows, LANES)),
                fixed((8, width)),
                pl.BlockSpec((rows, tile), lambda i, m: (0, i)),
            ],
            scratch_shapes=[pltpu.VMEM((rows, width), f32)],
        ),
        out_shape=[
            jax.ShapeDtypeStruct((rows, width), f32),
            jax.ShapeDtypeStruct((rows, width), bf16),
            jax.ShapeDtypeStruct((rows, LANES), bf16),
            jax.ShapeDtypeStruct((8, width), f32),
            jax.ShapeDtypeStruct((rows, inner), bf16),
        ],
        compiler_params=params(20),
        cost_estimate=cost(2 * rows * width * inner, 2 * width * inner),
        name="middle",
    )(meta, own, other, hidden, xn, gain, dy, wr, w)


def times_kernel(meta_ref, mine_ref, theirs_ref, w_ref, out_ref):
    core = meta_ref[0]
    inner = mine_ref.shape[1]
    here = pl.ds(pl.multiple_of(core * inner, LANES), inner)
    there = pl.ds(pl.multiple_of((1 - core) * inner, LANES), inner)
    out_ref[...] = dot_nt(mine_ref[...], w_ref[:, here]) + dot_nt(theirs_ref[...], w_ref[:, there])


def times_transposed(meta, mine, theirs, w):
    rows = mine.shape[0]
    width, inner = w.shape
    tile = width // JOIN_TILES
    return pl.pallas_call(
        times_kernel,
        grid_spec=pltpu.PrefetchScalarGridSpec(
            num_scalar_prefetch=1,
            grid=(width // tile,),
            in_specs=[
                fixed(mine.shape),
                fixed(theirs.shape),
                pl.BlockSpec((tile, inner), lambda i, m: (i, 0)),
            ],
            out_specs=pl.BlockSpec((rows, tile), lambda i, m: (0, i)),
        ),
        out_shape=jax.ShapeDtypeStruct((rows, width), f32),
        compiler_params=params(12),
        cost_estimate=cost(2 * rows * width * inner, 2 * width * inner),
        name="times_transposed",
    )(meta, mine, theirs, w)


def back_kernel(
    meta_ref,
    own_ref,
    other_ref,
    dxq_ref,
    x_ref,
    gain_ref,
    dstate_ref,
    wk_ref,
    wv_ref,
    cos_ref,
    sin_ref,
    din_ref,
    dkv_ref,
    dgain_ref,
    pair_ref,
):
    core = meta_ref[0]
    pair_ref[core] = own_ref[...].astype(f32)
    pair_ref[1 - core] = other_ref[...].astype(f32)
    wide = KV * HD
    for head in range(KV):
        turned = turn(pair_ref[head, :, :HD], cos_ref[...], -sin_ref[...])
        dkv_ref[:, head * HD : (head + 1) * HD] = turned.astype(bf16)
        dkv_ref[:, wide + head * HD : wide + (head + 1) * HD] = pair_ref[head, :, HD:].astype(bf16)
    d_xn = (
        dxq_ref[...]
        + dot_nt(dkv_ref[:, :wide], wk_ref[...])
        + dot_nt(dkv_ref[:, wide:], wv_ref[...])
    )
    values = x_ref[...].astype(f32)
    scale_row = norm_scale(values)
    normed = values * scale_row
    dgain_ref[...] = jnp.broadcast_to(
        jnp.sum(d_xn * normed, axis=0, keepdims=True), dgain_ref.shape
    )
    scaled = d_xn * gain_ref[...]
    inner_mean = jnp.mean(scaled * normed, axis=-1, keepdims=True)
    din_ref[...] = (dstate_ref[...] + scale_row * (scaled - normed * inner_mean)).astype(bf16)


def back(meta, own, other, dxq, x, gain, dstate, wk, wv, cos, sin):
    rows, width = x.shape
    return pl.pallas_call(
        back_kernel,
        grid_spec=pltpu.PrefetchScalarGridSpec(
            num_scalar_prefetch=1,
            grid=(1,),
            in_specs=[
                fixed(a.shape) for a in (own, other, dxq, x, gain, dstate, wk, wv, cos, sin)
            ],
            out_specs=[
                fixed((rows, width)),
                fixed((rows, 2 * KV * HD)),
                fixed((8, width)),
            ],
            scratch_shapes=[pltpu.VMEM((KV, rows, 2 * HD), f32)],
        ),
        out_shape=[
            jax.ShapeDtypeStruct((rows, width), bf16),
            jax.ShapeDtypeStruct((rows, 2 * KV * HD), bf16),
            jax.ShapeDtypeStruct((8, width), f32),
        ],
        compiler_params=params(16),
        cost_estimate=cost(4 * rows * width * KV * HD, 16 * rows * width),
        name="back",
    )(meta, own, other, dxq, x, gain, dstate, wk, wv, cos, sin)


def dense_kernel(steps, extra, meta_ref, left_ref, left2_ref, right_ref, right2_ref, *refs):
    if extra:
        xn_ref, dlog_ref, gain1_ref, gain2_ref = refs[:4]
        refs = refs[4:]
        more_ref = refs[-1]
        refs = refs[:-1]
    outs, whole_ref = refs[:-1], refs[-1]
    core = meta_ref[0]
    place = meta_ref[1]
    group = pl.program_id(0)
    piece = outs[0].shape[4]
    wide = right_ref.shape[1]
    left = jnp.concatenate([left_ref[...], left2_ref[...]], axis=0)
    right = jnp.concatenate([right_ref[...], right2_ref[...]], axis=0)
    whole_ref[...] = dot_tn(left, right)
    if extra:
        router = dot_tn(xn_ref[...], dlog_ref[...])
        first = jnp.broadcast_to(gain1_ref[0:1, :], (LANES, router.shape[0])).T
        second = jnp.broadcast_to(gain2_ref[0:1, :], (LANES, router.shape[0])).T
        lane = lax.broadcasted_iota(jnp.int32, router.shape, 1)
        more_ref[...] = jnp.where(
            lane == LANES - 2, first, jnp.where(lane == LANES - 1, second, router)
        )

    def give(out_ref):
        for d in range(2):
            for c in range(2):
                for t in range(2):
                    at = ((core ^ t) * 4 + (place ^ (c * 2 + d))) * piece
                    rows = pl.ds(pl.multiple_of(at, 16), piece)
                    out_ref[0, d, c, t, :, :wide] = whole_ref[rows, :].astype(bf16)
                    if extra:
                        out_ref[0, d, c, t, :, wide:] = more_ref[rows, :].astype(bf16)

    for k in range(steps):

        @pl.when((group >= 2**k) & (group < 2 ** (k + 1)))
        def _():
            give(outs[k])

    @pl.when(group == 0)
    def _():
        give(outs[steps])


def dense_grad(plane, meta, left, left2, right, right2, extra=()):
    rows, width = left.shape
    wide = right.shape[1]
    part = width // plane.chips
    piece = part // 8
    held = wide + (LANES if extra else 0)
    columns = pl.BlockSpec((rows, part), lambda g, m: (0, m[2 + g]))
    gains = pl.BlockSpec((8, part), lambda g, m: (0, m[2 + g]))
    more = [columns, fixed((rows, LANES)), gains, gains]

    def out(first, size):
        where = lambda g, m: (jnp.clip(g - first, 0, size - 1), 0, 0, 0, 0, 0)
        return pl.BlockSpec((1, 2, 2, 2, piece, held), where)

    ranges = [(2**k, 2**k) for k in range(plane.steps)] + [(0, 1)]
    return pl.pallas_call(
        functools.partial(dense_kernel, plane.steps, bool(extra)),
        grid_spec=pltpu.PrefetchScalarGridSpec(
            num_scalar_prefetch=1,
            grid=(plane.chips,),
            in_specs=[columns, columns, fixed((rows, wide)), fixed((rows, wide))]
            + (more if extra else []),
            out_specs=[out(*r) for r in ranges],
            scratch_shapes=[pltpu.VMEM((part, wide), f32)]
            + ([pltpu.VMEM((part, LANES), f32)] if extra else []),
        ),
        out_shape=[
            jax.ShapeDtypeStruct((size, 2, 2, 2, piece, held), bf16) for _, size in ranges
        ],
        compiler_params=params(28),
        cost_estimate=cost(4 * rows * width * wide, 2 * width * wide),
        name="dense_grad",
    )(meta, left, left2, right, right2, *extra)


def finish_kernel(core_ref, own_ref, came_ref, que_ref, out_ref, key_ref, val_ref, more_ref):
    core = core_ref[0]
    split = que_ref.shape[1] // 2
    wide = key_ref.shape[1]

    def place(first, second):
        here = pl.ds(pl.multiple_of(core * split, LANES), split)
        there = pl.ds(pl.multiple_of((1 - core) * split, LANES), split)
        out_ref[:, here] = first[:, :split]
        out_ref[:, there] = second[:, :split]
        que_ref[:, here] = first[:, split : 2 * split]
        que_ref[:, there] = second[:, split : 2 * split]
        more_ref[...] = first[:, 2 * split + wide :] + second[:, 2 * split + wide :]

    own, came = own_ref[...], came_ref[...].astype(f32)
    place(own, came)
    small_own, small_came = own[:, 2 * split : 2 * split + wide], came[:, 2 * split : 2 * split + wide]
    key_ref[...] = jnp.where(core == 0, small_own, small_came)
    val_ref[...] = jnp.where(core == 0, small_came, small_own)


def finish(core, own, came, split, wide):
    rows = own.shape[0]
    shapes = [(rows, 2 * split), (rows, 2 * split), (rows, wide), (rows, wide), (rows, LANES)]
    return pl.pallas_call(
        finish_kernel,
        grid_spec=pltpu.PrefetchScalarGridSpec(
            num_scalar_prefetch=1,
            grid=(1,),
            in_specs=[fixed(own.shape), fixed(came.shape)],
            out_specs=[fixed(shape) for shape in shapes],
        ),
        out_shape=[jax.ShapeDtypeStruct(shape, f32) for shape in shapes],
        compiler_params=params(8),
        name="finish",
    )(core, own, came)


class Plane:
    def __init__(self, size):
        self.size = size
        bits = size.bit_length() - 1
        self.steps = bits - 1
        self.shift = self.steps // 2 if self.steps % 2 == 0 else 0
        first = list(range(1, bits))
        self.order = (first, first[self.shift :] + first[: self.shift])
        self.sibling = [(i, i ^ 1) for i in range(size)]
        self.mixed = [
            [(i, i ^ (1 << self.order[i & 1][k])) for i in range(size)] for k in range(self.steps)
        ]
        self.chips = size // 2

    def chip_offset(self, core, group):
        return sum(((group >> k) & 1) << self.order[core][k] for k in range(self.steps))

    def swapped(self, group):
        if not self.shift:
            return group
        low_mask = (1 << self.shift) - 1
        return ((group & low_mask) << (self.steps - self.shift)) | (group >> self.shift)


def total(values):
    summed = values[0].astype(f32)
    for value in values[1:]:
        summed = summed + value.astype(f32)
    return summed.astype(bf16)


def reduce_steps(plane, terms, hold=()):
    terms = list(terms)

    def pick(first, last):
        return [
            a[first - at : last - at] for at, a in terms if at <= first and last - at <= a.shape[0]
        ]

    for k in reversed(range(plane.steps)):
        send = total(pick(2**k, 2 ** (k + 1)))
        terms.append((0, lax.ppermute(send, "expert", plane.mixed[k])))
    return [a[0] for a in pick(0, 1)]


def to_sibling(plane, value):
    return lax.ppermute(value, "expert", plane.sibling)


def place_keys(bases_ref, at, buf_ref, keys_ref, vals_ref, half, blocks):
    for block in range(blocks):
        for part in range(2):
            rows = pl.ds(pl.multiple_of(bases_ref[at + block * 2 + part] * half, 16), half)
            keys_ref[rows, :] = buf_ref[block, part * half : (part + 1) * half, :HD]
            vals_ref[rows, :] = buf_ref[block, part * half : (part + 1) * half, HD:]


def stack_heads(ref, part, half, groups):
    return jnp.concatenate(
        [
            ref[part * half : (part + 1) * half, g * HD : (g + 1) * HD]
            for g in range(groups)
        ],
        axis=0,
    )


def for_steps(count, body):
    if count <= 8:
        for n in range(count):
            body(n)
    else:
        lax.fori_loop(0, count, lambda n, _: (body(n), 0)[1], 0)


def attend_kernel(at, meta_ref, q_ref, buf_ref, offs_ref, *refs):
    (
        att_ref,
        attt_ref,
        lse_ref,
        keys_ref,
        vals_ref,
        query_ref,
        top_ref,
        sum_ref,
        mix_ref,
    ) = refs
    blocks = buf_ref.shape[0]
    half = q_ref.shape[0] // 2
    groups = q_ref.shape[1] // HD
    chunk = CHUNK_BLOCKS * half
    factor = LOG2E / math.sqrt(HD)
    count = 2 * blocks // CHUNK_BLOCKS - 1
    place_keys(meta_ref, at, buf_ref, keys_ref, vals_ref, half, blocks)
    for part in range(2):
        query_ref[part] = stack_heads(q_ref, part, half, groups)
    full = [lax.div(meta_ref[1 + part], CHUNK_BLOCKS) for part in range(2)]

    def step(n, part, j, edge):
        rows = pl.ds(pl.multiple_of(j * chunk, 16), chunk)
        scores = dot_nt(keys_ref[rows, :], query_ref[part])
        if edge is not None:
            row = lax.broadcasted_iota(jnp.int32, scores.shape, 0) + (j * chunk - edge * half)
            scores = jnp.where(row <= offs_ref[0:1, :], scores, negative)
        top = jnp.max(scores, axis=0, keepdims=True)
        weights = jnp.exp2((scores - top) * factor)
        top_ref[n, 0:1, :] = top
        sum_ref[n, 0:1, :] = jnp.sum(weights, axis=0, keepdims=True)
        mix_ref[n] = dot_tn(vals_ref[rows, :], weights.astype(bf16))

    def full_step(n):
        late = n >= full[0]
        part = jnp.where(late, 1, 0)
        step(n, part, n - jnp.where(late, full[0], 0), None)

    for_steps(count, full_step)
    for part in range(2):
        step(count + part, part, full[part], meta_ref[1 + part])
    for part in range(2):
        edge = count + part
        top = top_ref[edge, 0:1, :]

        def mine(n):
            return (n < full[0]) if part == 0 else (n >= full[0])

        def find(n, top):
            return jnp.where(mine(n), jnp.maximum(top, top_ref[n, 0:1, :]), top)

        def add(n, carry):
            summed, acc = carry
            share = jnp.exp2((top_ref[n, 0:1, :] - top) * factor)
            share = jnp.where(mine(n), jnp.minimum(share, 1.0), 0.0)
            return summed + share * sum_ref[n, 0:1, :], acc + share * mix_ref[n]

        top = fold_steps(count, find, top)
        share = jnp.exp2((top_ref[edge, 0:1, :] - top) * factor)
        summed, acc = fold_steps(
            count, add, (share * sum_ref[edge, 0:1, :], share * mix_ref[edge])
        )
        acc = acc / summed
        attt_ref[part] = acc
        lse_ref[part] = jnp.broadcast_to(top * factor + jnp.log2(summed), lse_ref.shape[1:])
        rowwise = acc.T.astype(bf16)
        for g in range(groups):
            att_ref[part * half : (part + 1) * half, g * HD : (g + 1) * HD] = rowwise[
                g * half : (g + 1) * half
            ]


def fold_steps(count, body, carry):
    if count <= 8:
        for n in range(count):
            carry = body(n, carry)
        return carry
    return lax.fori_loop(0, count, body, carry)


def attend(own, meta, query, buf, offs):
    rows = query.shape[0]
    groups = H // KV
    half = rows // 2
    blocks, padded, wide = buf.shape
    span = groups * HD
    width = groups * half
    keys = blocks * rows
    steps = 2 * blocks // CHUNK_BLOCKS + 1
    which = (lambda m: m[0]) if own else (lambda m: 1 - m[0])
    head = lambda i, m: (0, which(m))
    return pl.pallas_call(
        functools.partial(attend_kernel, 4 if own else 4 + 2 * blocks),
        grid_spec=pltpu.PrefetchScalarGridSpec(
            num_scalar_prefetch=1,
            grid=(1,),
            in_specs=[
                pl.BlockSpec((rows, span), head),
                fixed((blocks, padded, wide)),
                fixed((8, width)),
            ],
            out_specs=[
                fixed((rows, span)),
                fixed((2, HD, width)),
                fixed((2, 8, width)),
            ],
            scratch_shapes=[
                pltpu.VMEM((keys, HD), bf16),
                pltpu.VMEM((keys, HD), bf16),
                pltpu.VMEM((2, width, HD), bf16),
                pltpu.VMEM((steps, 8, width), f32),
                pltpu.VMEM((steps, 8, width), f32),
                pltpu.VMEM((steps, HD, width), f32),
            ],
        ),
        out_shape=[
            jax.ShapeDtypeStruct((rows, span), bf16),
            jax.ShapeDtypeStruct((2, HD, width), f32),
            jax.ShapeDtypeStruct((2, 8, width), f32),
        ],
        compiler_params=params(20 + blocks * rows * HD // 2**16),
        cost_estimate=cost(
            rows * keys * H * HD, blocks * padded * wide * 2, rows * keys * H // 4
        ),
        name="attend",
    )(meta, query, buf, offs)


def attend_back_kernel(
    at,
    meta_ref,
    q_ref,
    do_ref,
    buf_ref,
    offs_ref,
    attt_ref,
    lse_ref,
    cos_ref,
    sin_ref,
    *refs,
):
    (
        dq_ref,
        dbuf_ref,
        keys_ref,
        vals_ref,
        dkeys_ref,
        dvals_ref,
        query_ref,
        grad_ref,
        delta_ref,
        dquery_ref,
    ) = refs
    blocks = buf_ref.shape[0]
    half = q_ref.shape[0] // 2
    groups = q_ref.shape[1] // HD
    chunk = CHUNK_BLOCKS * half
    scale = 1.0 / math.sqrt(HD)
    factor = LOG2E * scale
    count = 2 * blocks // CHUNK_BLOCKS - 1
    place_keys(meta_ref, at, buf_ref, keys_ref, vals_ref, half, blocks)
    dkeys_ref[...] = jnp.zeros_like(dkeys_ref)
    dvals_ref[...] = jnp.zeros_like(dvals_ref)
    dquery_ref[...] = jnp.zeros_like(dquery_ref)
    for part in range(2):
        query_ref[part] = stack_heads(q_ref, part, half, groups)
        grad = stack_heads(do_ref, part, half, groups)
        grad_ref[part] = grad
        delta = jnp.sum(grad.astype(f32).T * attt_ref[part], axis=0, keepdims=True)
        delta_ref[part] = jnp.broadcast_to(delta, delta_ref.shape[1:])
    full = [lax.div(meta_ref[1 + part], CHUNK_BLOCKS) for part in range(2)]

    def step(part, j, edge):
        rows = pl.ds(pl.multiple_of(j * chunk, 16), chunk)
        keys = keys_ref[rows, :]
        query, grad = query_ref[part], grad_ref[part]
        scores = dot_nt(keys, query)
        weights = jnp.exp2(scores * factor - lse_ref[part, 0:1, :])
        if edge is not None:
            row = lax.broadcasted_iota(jnp.int32, scores.shape, 0) + (j * chunk - edge * half)
            weights = jnp.where(row <= offs_ref[0:1, :], weights, 0.0)
        dweights = dot_nt(vals_ref[rows, :], grad)
        dscores = (weights * (dweights - delta_ref[part, 0:1, :])).astype(bf16)
        dvals_ref[rows, :] += dot(weights.astype(bf16), grad)
        dkeys_ref[rows, :] += dot(dscores, query)
        dquery_ref[part] += dot_tn(keys, dscores)

    def full_step(n):
        late = n >= full[0]
        step(jnp.where(late, 1, 0), n - jnp.where(late, full[0], 0), None)

    for_steps(count, full_step)
    for part in range(2):
        step(part, full[part], meta_ref[1 + part])
    for part in range(2):
        rowwise = dquery_ref[part].T * scale
        these = slice(part * half, (part + 1) * half)
        for g in range(groups):
            turned = turn(rowwise[g * half : (g + 1) * half], cos_ref[these], -sin_ref[these])
            dq_ref[these, g * HD : (g + 1) * HD] = turned.astype(bf16)

    for block in range(blocks):
        for part in range(2):
            rows = pl.ds(pl.multiple_of(meta_ref[at + block * 2 + part] * half, 16), half)
            here = slice(part * half, (part + 1) * half)
            dbuf_ref[block, here, :HD] = (dkeys_ref[rows, :] * scale).astype(bf16)
            dbuf_ref[block, here, HD:] = dvals_ref[rows, :].astype(bf16)


def attend_back(own, meta, query, grad, buf, offs, attt, lse, cos, sin):
    rows = query.shape[0]
    groups = H // KV
    half = rows // 2
    blocks, padded, wide = buf.shape
    span = groups * HD
    width = groups * half
    keys = blocks * rows
    which = (lambda m: m[0]) if own else (lambda m: 1 - m[0])
    head = lambda i, m: (0, which(m))
    need = blocks * rows * (2 * HD * 2 + 2 * HD * 4 + 3 * wide * 2)
    return pl.pallas_call(
        functools.partial(attend_back_kernel, 4 if own else 4 + 2 * blocks),
        grid_spec=pltpu.PrefetchScalarGridSpec(
            num_scalar_prefetch=1,
            grid=(1,),
            in_specs=[
                pl.BlockSpec((rows, span), head),
                pl.BlockSpec((rows, span), head),
                fixed((blocks, padded, wide)),
                fixed((8, width)),
                fixed((2, HD, width)),
                fixed((2, 8, width)),
                fixed((rows, HD)),
                fixed((rows, HD)),
            ],
            out_specs=[fixed((rows, span)), fixed((blocks, rows, wide))],
            scratch_shapes=[
                pltpu.VMEM((keys, HD), bf16),
                pltpu.VMEM((keys, HD), bf16),
                pltpu.VMEM((keys, HD), f32),
                pltpu.VMEM((keys, HD), f32),
                pltpu.VMEM((2, width, HD), bf16),
                pltpu.VMEM((2, width, HD), bf16),
                pltpu.VMEM((2, 8, width), f32),
                pltpu.VMEM((2, HD, width), f32),
            ],
        ),
        out_shape=[
            jax.ShapeDtypeStruct((rows, span), bf16),
            jax.ShapeDtypeStruct((blocks, rows, wide), bf16),
        ],
        compiler_params=params(24 + need // 2**20),
        cost_estimate=cost(
            2.5 * rows * keys * H * HD, blocks * padded * wide * 4, rows * keys * H // 4
        ),
        name="attend_back",
    )(meta, query, grad, buf, offs, attt, lse, cos, sin)


def expert_kernel(
    plane,
    meta_ref,
    mine_ref,
    theirs_ref,
    dy_mine_ref,
    dy_theirs_ref,
    wg_ref,
    wu_ref,
    wd_ref,
    wr_ref,
    out_mine_ref,
    out_theirs_ref,
    dx_mine_ref,
    dx_theirs_ref,
    hidden_ref,
    dhid_ref,
    gate_ref,
):
    core = meta_ref[0]
    expert = meta_ref[1]
    rows, half = mine_ref.shape[2], mine_ref.shape[3]
    here = pl.ds(pl.multiple_of(core * half, LANES), half)
    there = pl.ds(pl.multiple_of((1 - core) * half, LANES), half)
    x_mine = mine_ref[0].reshape(2 * rows, half)
    x_theirs = jnp.concatenate([theirs_ref[0, 1], theirs_ref[0, 0]], axis=0)
    gate_pre = dot(x_mine, wg_ref[here, :]) + dot(x_theirs, wg_ref[there, :])
    up_pre = dot(x_mine, wu_ref[here, :]) + dot(x_theirs, wu_ref[there, :])
    logits = dot(x_mine, wr_ref[here, :]) + dot(x_theirs, wr_ref[there, :])
    marked = dy_mine_ref[0].reshape(2 * rows, half + LANES)
    dy_here = marked[:, :half].astype(f32)
    dy_there = jnp.concatenate(
        [dy_theirs_ref[0, 1, :, :half], dy_theirs_ref[0, 0, :, :half]], axis=0
    ).astype(f32)
    chosen = marked[:, half:].astype(f32) > 0.5
    top = jnp.max(jnp.where(chosen, logits, negative), axis=-1, keepdims=True)
    shares = jnp.where(chosen, jnp.exp(logits - top), 0.0)
    lane = lax.broadcasted_iota(jnp.int32, logits.shape, 1)
    own = jnp.sum(jnp.where(lane == expert, shares, 0.0), axis=-1, keepdims=True)
    gate = own / jnp.sum(shares, axis=-1, keepdims=True)
    routed = jnp.sum(jnp.where((lane == expert) & chosen, 1.0, 0.0), axis=-1, keepdims=True)
    gate_ref[...] = jnp.broadcast_to(gate, gate_ref.shape)

    sig = jax.nn.sigmoid(gate_pre)
    silu = gate_pre * sig
    hidden = (silu * up_pre).astype(bf16)
    hidden_ref[...] = hidden
    result_here = dot(hidden, wd_ref[:, here]).astype(bf16).astype(f32)
    result_there = dot(hidden, wd_ref[:, there]).astype(bf16).astype(f32)
    d_gate = routed * (
        jnp.sum(dy_here * result_here, axis=-1, keepdims=True)
        + jnp.sum(dy_there * result_there, axis=-1, keepdims=True)
    )
    out_here = (gate * result_here).astype(bf16)
    out_there = (gate * result_there).astype(bf16)
    d_hidden = dot_nt((gate * dy_here).astype(bf16), wd_ref[:, here]) + dot_nt(
        (gate * dy_there).astype(bf16), wd_ref[:, there]
    )
    d_up = (d_hidden * silu).astype(bf16)
    d_gp = (d_hidden * up_pre * (sig * (1.0 + gate_pre * (1.0 - sig)))).astype(bf16)
    inner = d_gp.shape[1]
    dhid_ref[:, :inner] = d_gp
    dhid_ref[:, inner:] = d_up
    high = d_gate.astype(bf16).astype(f32)
    low = d_gate - high
    spot = jnp.where(lane == expert, 1.0, 0.0)
    dx_here = (dot_nt(d_gp, wg_ref[here, :]) + dot_nt(d_up, wu_ref[here, :])).astype(bf16)
    dx_there = (dot_nt(d_gp, wg_ref[there, :]) + dot_nt(d_up, wu_ref[there, :])).astype(bf16)
    col_here = (spot * jnp.where(core == 0, high, low)).astype(bf16)
    col_there = (spot * jnp.where(core == 0, low, high)).astype(bf16)
    for t in range(2):
        these = slice(t * rows, (t + 1) * rows)
        dx_mine_ref[0, t, :, :half] = dx_here[these]
        dx_mine_ref[0, t, :, half:] = col_here[these]
        dx_theirs_ref[0, 1 - t, :, :half] = dx_there[these]
        dx_theirs_ref[0, 1 - t, :, half:] = col_there[these]
        out_mine_ref[0, t] = out_here[these]
        out_theirs_ref[0, 1 - t] = out_there[these]


def run_expert(plane, first, meta, mine, theirs, dy_mine, dy_theirs, wg, wu, wd, wr):
    chips, _, rows, half = mine.shape
    width, inner = wg.shape
    swap = lambda g: plane.swapped(g + first) - first
    pair = lambda w: pl.BlockSpec((1, 2, rows, w), lambda g, m: (g, 0, 0, 0))
    swapped = lambda w: pl.BlockSpec((1, 2, rows, w), lambda g, m: (swap(g), 0, 0, 0))
    flat = lambda w: pl.BlockSpec((2 * rows, w), lambda g, m: (g, 0))
    total_rows = chips * 2 * rows
    return pl.pallas_call(
        functools.partial(expert_kernel, plane),
        grid_spec=pltpu.PrefetchScalarGridSpec(
            num_scalar_prefetch=1,
            grid=(chips,),
            in_specs=[
                pair(half),
                swapped(half),
                pair(half + LANES),
                swapped(half + LANES),
                fixed((width, inner)),
                fixed((width, inner)),
                fixed((inner, width)),
                fixed((width, wr.shape[1])),
            ],
            out_specs=[
                pair(half),
                swapped(half),
                pair(half + LANES),
                swapped(half + LANES),
                flat(inner),
                flat(2 * inner),
                flat(LANES),
            ],
        ),
        out_shape=[
            jax.ShapeDtypeStruct((chips, 2, rows, half), bf16),
            jax.ShapeDtypeStruct((chips, 2, rows, half), bf16),
            jax.ShapeDtypeStruct((chips, 2, rows, half + LANES), bf16),
            jax.ShapeDtypeStruct((chips, 2, rows, half + LANES), bf16),
            jax.ShapeDtypeStruct((total_rows, inner), bf16),
            jax.ShapeDtypeStruct((total_rows, 2 * inner), bf16),
            jax.ShapeDtypeStruct((total_rows, LANES), f32),
        ],
        compiler_params=params(36),
        cost_estimate=cost(
            12 * total_rows * width * inner, 20 * total_rows * width, total_rows * inner
        ),
        name="expert",
    )(meta, mine, theirs, dy_mine, dy_theirs, wg, wu, wd, wr)


def rows_in_order(plane, own0, own, other0, other, mine):
    if mine:
        return [ref[g, t] for ref in (own0, own) for g in range(ref.shape[0]) for t in range(2)]
    parts = [other0[0, 1], other0[0, 0]]
    for g in range(1, plane.chips):
        at = plane.swapped(g) - 1
        parts += [other[at, 1], other[at, 0]]
    return parts


def expert_grad_kernel(plane, weigh, meta_ref, *refs):
    lefts, refs = refs[:4], refs[4:]
    if weigh:
        gate0_ref, gate_ref, right0_ref, right_ref, _, out_ref = refs
    else:
        right0_ref, right_ref, out_ref = refs
    step = pl.program_id(0)
    halves = pl.num_programs(0) // 2
    first = right0_ref.shape[0]

    def give(parts):
        if weigh:
            rows = parts[0].shape[0]
            gates = [gate0_ref[t * rows : (t + 1) * rows, 0:1] for t in range(2)]
            gates += [
                gate_ref[n * rows : (n + 1) * rows, 0:1] for n in range(len(parts) - 2)
            ]
            parts = [(g * p.astype(f32)).astype(bf16) for g, p in zip(gates, parts)]
        near = jnp.concatenate(parts[:2], axis=0)
        far = jnp.concatenate(parts[2:], axis=0)
        out_ref[...] = (dot_tn(near, right0_ref[...]) + dot_tn(far, right_ref[...])).astype(bf16)

    @pl.when(step < halves)
    def _():
        give(rows_in_order(plane, *lefts, True))

    @pl.when(step >= halves)
    def _():
        give(rows_in_order(plane, *lefts, False))


def expert_grad(plane, meta, lefts, right0, right, half, gates=None, grads=None):
    tile = half // 2
    rows = lefts[0].shape[2]
    inner = right.shape[1]
    own = lambda a: pl.BlockSpec(
        a.shape[:3] + (tile,), lambda i, m: (0, 0, 0, jnp.minimum(i, 1))
    )
    other = lambda a: pl.BlockSpec(
        a.shape[:3] + (tile,), lambda i, m: (0, 0, 0, jnp.maximum(i - 2, 0))
    )
    count = right0.shape[0] + right.shape[0]
    need = count * (8 * tile * 2 + inner * 2) + 3 * tile * inner * 4
    specs = [own(lefts[0]), own(lefts[1]), other(lefts[2]), other(lefts[3])]
    args = list(lefts)
    if gates:
        specs += [fixed(g.shape) for g in gates]
        args += list(gates)
    specs += [fixed(right0.shape), fixed(right.shape)]
    args += [right0, right]
    if gates:
        specs.append(pl.BlockSpec(memory_space=pl.ANY))
        args.append(grads)
        need += count * LANES * 4
        out_shape, place = grads.shape, 2
    else:
        out_shape, place = (2 * half, inner + inner // 2), 0
    return pl.pallas_call(
        functools.partial(expert_grad_kernel, plane, bool(gates)),
        grid_spec=pltpu.PrefetchScalarGridSpec(
            num_scalar_prefetch=1,
            grid=(4,),
            in_specs=specs,
            out_specs=pl.BlockSpec(
                (tile, inner), lambda i, m: ((m[0] ^ (i // 2)) * 2 + i % 2, place)
            ),
        ),
        out_shape=jax.ShapeDtypeStruct(out_shape, bf16),
        input_output_aliases={len(args): 0} if gates else {},
        compiler_params=params(2 + need // 2**20),
        cost_estimate=cost(4 * count * half * inner, 6 * count * half),
        name="down_grad" if gates else "up_grad",
    )(meta, *args)


def together(*values):
    return lax.optimization_barrier(values)


def per_device(
    tokens,
    gain_attn,
    w_query,
    w_key,
    w_value,
    w_out,
    gain_moe,
    w_router,
    w_gate,
    w_up,
    w_down,
    routes,
    positions,
    cotangent,
):
    rows = tokens.shape[1]
    width = tokens.shape[2]
    half = rows // 2
    split = width // 2
    groups = H // KV
    kv_width = KV * HD
    experts = w_router.shape[1]
    inner = w_gate.shape[2]
    plane = Plane(w_gate.shape[0] * lax.axis_size("expert"))
    last = plane.steps - 1
    contexts = lax.axis_size("context")
    copies = lax.axis_size("dp")
    blocks = plane.size * contexts
    index = lax.axis_index("expert")
    core = index % 2
    places = positions[0]
    x = tokens[0]
    gain_one, gain_two = gain_attn, gain_moe
    swap_context = [(i, i ^ 1) for i in range(contexts)]
    swap_copies = [(i, i ^ 1) for i in range(copies)]

    def by_core(zero, one):
        return jnp.where(core == 0, zero, one)

    def mix(value, k):
        return lax.ppermute(value, "expert", plane.mixed[k])

    def sibling(value):
        return lax.ppermute(value, "expert", plane.sibling)

    tcos, tsin = rope_tables(2 * blocks, half)
    own_bases = jnp.stack([places[0], places[half]]) // half
    front_meta = jnp.concatenate([core[None], own_bases]).astype(jnp.int32)
    core_row = jnp.reshape(core, (1,)).astype(jnp.int32)
    xn_one, packed, cos, sin = front(
        core_row, places, x, gain_one, w_key, w_value, tcos, tsin
    )

    lanes = jnp.arange(LANES, dtype=jnp.int32)
    marks = jnp.any(routes[0][:, :, None] == lanes[None, None, :], axis=1).astype(bf16)
    dy, marks = after(cotangent[0], packed), after(marks, packed)
    dy_keep = jnp.concatenate([by_core(dy[:, :split], dy[:, split:]), marks], axis=1)
    dy_send = jnp.concatenate([by_core(dy[:, split:], dy[:, :split]), marks], axis=1)

    router_wide = jnp.pad(w_router, ((0, 0), (0, LANES - experts)))
    weights = (w_gate[0], w_up[0], w_down[0], router_wide)
    dy_m0 = jnp.stack([dy_keep, sibling(dy_send)])[None]
    dy_t0 = jnp.stack([sibling(dy_keep), dy_send])[None]
    if contexts > 1:
        arrived = lax.ppermute(packed, "context", swap_context)
        arrived, dy_m0, dy_t0, front_meta = together(arrived, dy_m0, dy_t0, front_meta)
        packed = jnp.stack([packed, arrived], axis=1)
    else:
        packed = packed[:, None]
    held = jnp.stack([packed[0], sibling(packed[1])])[None]
    query = make_query(xn_one, w_query, cos, sin)
    for k in range(plane.steps):
        if k == last:
            held, query = together(held, query)
        held = jnp.concatenate([held, mix(held, k)])
    mine = held.reshape(blocks, rows + PAD_ROWS, kv_width)
    theirs = sibling(held).reshape(blocks, rows + PAD_ROWS, kv_width)
    own_order = mine[:, rows :: PAD_ROWS // 2, 0].astype(f32).astype(jnp.int32).reshape(-1)
    spots = [
        ((plane.swapped(g) * 2 + 1 - t) * contexts + c) * 2 + part
        for g in range(plane.chips)
        for t in range(2)
        for c in range(contexts)
        for part in range(2)
    ]
    other_order = jnp.stack([own_order[spot] for spot in spots])
    meta = jnp.concatenate([front_meta, front_meta[:1], own_order, other_order])
    offs = jnp.asarray(np.tile(np.arange(groups * half, dtype=np.int32) % half, (8, 1)))

    dy_held, meta = together(dy_m0, meta)
    dy_came = mix(dy_held, 0)
    att_mine, *own_stats = attend(True, meta, query, mine, offs)
    dy_came, theirs, att_mine = together(dy_came, theirs, att_mine)
    dy_held = jnp.concatenate([dy_held, dy_came])
    for k in range(1, last):
        dy_held = jnp.concatenate([dy_held, mix(dy_held, k)])
    dy_held, theirs = together(dy_held, theirs)
    dy_came = mix(dy_held, last)
    att_theirs, *other_stats = attend(False, meta, query, theirs, offs)
    hidden, xn_two, keep, send = join(front_meta, att_mine, att_theirs, w_out, x, gain_two)

    offsets = np.array(
        [[plane.chip_offset(c, g) // 2 for g in range(plane.chips)] for c in range(2)], np.int32
    )
    chips = (index // 2) ^ by_core(offsets[0], offsets[1])
    expert_meta = jnp.concatenate([core[None], index[None], chips]).astype(jnp.int32)
    mine0 = jnp.stack([keep, sibling(send)])[None]
    theirs0 = jnp.stack([sibling(keep), send])[None]
    held = mine0
    for k in range(plane.steps):
        came = mix(held, k)
        if k == last - 1:
            came, dy_came = together(came, dy_came)
        if k == last:
            out_m0, out_t0, dx_m0, dx_t0, hid0, dhid0, gate0 = run_expert(
                plane, 0, expert_meta, after(mine0, held), theirs0, dy_m0, dy_t0, *weights
            )
            dy_m1 = jnp.concatenate([dy_held, dy_came])[1:]
            dy_t1 = sibling(dy_m1)
            came, hid0, dy_t1 = together(came, hid0, dy_t1)
        held = jnp.concatenate([held, came])
    mine1 = held[1:]
    theirs1 = sibling(mine1)
    out_m1, out_t1, dx_m1, dx_t1, hid1, dhid1, gate1 = run_expert(
        plane, 1, expert_meta, mine1, theirs1, dy_m1, dy_t1, *weights
    )

    def pick(terms, k):
        lo, hi = 2**k, 2 ** (k + 1)
        return total([a[lo - at : hi - at] for at, a in terms if at <= lo and hi - at <= a.shape[0]])

    def parts_of(terms, slot):
        return total([a[0, slot] for at, a in terms if at == 0])

    dx_r0, dx_r1 = sibling(dx_t0), sibling(dx_t1)
    grads = expert_grad(
        plane, expert_meta, (mine0, mine1, theirs0, theirs1), dhid0, dhid1, split
    )
    dx_r1, grads = together(dx_r1, grads)
    terms = [(0, dx_m0), (1, dx_m1), (0, dx_r0), (1, dx_r1)]
    for k in reversed(range(plane.steps)):
        send = pick(terms, k)
        arrived = mix(send, k)
        if k == last:
            grads = expert_grad(
                plane,
                expert_meta,
                (dy_m0, dy_m1, dy_t0, dy_t1),
                after(hid0, send),
                hid1,
                split,
                (gate0, gate1),
                grads,
            )
            arrived, grads = together(arrived, grads)
        terms.append((0, arrived))
    expert_grads = lax.psum_scatter(grads, ("context", "dp"), scatter_dimension=0, tiled=True)
    dx_keep = parts_of(terms, 0)
    dx_other = sibling(parts_of(terms, 1))

    marked = jnp.concatenate([dy, marks], axis=1)
    d_state, d_low, d_logits, d_gain_moe, d_attended = middle(
        front_meta,
        dx_keep,
        dx_other,
        hidden,
        xn_two,
        gain_two,
        marked,
        router_wide,
        w_out,
    )
    dq_theirs, d_theirs = attend_back(
        False, meta, query, d_attended, theirs, offs, *other_stats, cos, sin
    )
    d_sent = sibling(d_theirs)
    d_attended = after(d_attended, dq_theirs)
    dq_mine, d_mine = attend_back(
        True, meta, query, d_attended, mine, offs, *own_stats, cos, sin
    )

    custom = contexts == 2 and copies == 2 and (width // plane.chips) % LANES == 0
    kv_shape = (plane.chips, 2, contexts, rows, kv_width)
    terms = [(0, d_mine.reshape(kv_shape)), (0, d_sent.reshape(kv_shape))]
    if custom:
        place = lax.axis_index("context") * 2 + lax.axis_index("dp")
        dense_meta = jnp.concatenate([core[None], place[None], chips]).astype(jnp.int32)
        xn_other, low_other = sibling(xn_one), sibling(d_low)
        att_other, dq_other = sibling(att_theirs), sibling(dq_theirs)

    def step_sum(steps, came, k):
        return total([steps[k]] + [a[2**k : 2 ** (k + 1)] for a in came])

    def fold(values, axis, pairs):
        return lax.ppermute(total([a[1] for a in values]), axis, pairs)

    for k in reversed(range(plane.steps)):
        send = pick(terms, k)
        arrived = mix(send, k)
        if k == last and custom:
            *out_steps, out_own = dense_grad(
                plane, dense_meta, after(d_low, send), low_other, att_mine, att_other
            )
            *que_steps, que_own = dense_grad(
                plane, dense_meta, xn_one, xn_other, after(dq_mine, out_own), dq_other
            )
            arrived, out_steps, que_own = together(arrived, out_steps, que_own)
        if k == 0:
            dxq = times_transposed(front_meta, after(dq_mine, send), dq_theirs, w_query)
            arrived, dxq = together(arrived, dxq)
            if custom:
                out_steps[last], send = together(out_steps[last], send)
                out_came = [mix(out_steps[last], last)]
        terms.append((0, arrived))
    dkv_keep = parts_of(terms, 0)
    dkv_other = sibling(parts_of(terms, 1))
    dkv = jnp.stack([dkv_keep, dkv_other], axis=1)
    mix_t0, mix_t1, dkv = together(out_t0, out_t1, dkv)
    mix_terms = [(0, out_m0), (1, out_m1), (0, sibling(mix_t0)), (1, sibling(mix_t1))]
    mix_send = pick(mix_terms, last)
    if custom:
        que_steps[last], dkv = together(que_steps[last], dkv)
        que_came = [mix(que_steps[last], last)]
    if contexts > 1:
        dkv_came = lax.ppermute(dkv[1], "context", swap_context)
        dkv_came, mix_send = together(dkv_came, mix_send)
        if custom:
            for k in reversed(range(last)):
                send = step_sum(out_steps, out_came, k)
                dkv_came, send = together(dkv_came, send)
                out_came.append(mix(send, k))
        dkv = dkv[0].astype(f32) + dkv_came.astype(f32)
    else:
        dkv = dkv[0].astype(f32)

    d_in, d_kv, d_gain_attn = back(
        front_meta, dkv[0], dkv[1], dxq, x, gain_one, d_state, w_key, w_value, cos, sin
    )

    if custom:
        for k in reversed(range(last)):
            que_came[-1], d_kv = together(que_came[-1], d_kv)
            send = step_sum(que_steps, que_came, k)
            send, d_kv = together(send, d_kv)
            que_came.append(mix(send, k))
        d_own = by_core(d_kv[:, :kv_width], d_kv[:, kv_width:])
        d_sends = sibling(by_core(d_kv[:, kv_width:], d_kv[:, :kv_width]))
        *small_steps, small_own = dense_grad(
            plane,
            dense_meta,
            xn_one,
            xn_other,
            d_own,
            d_sends,
            (xn_two, d_logits, d_gain_attn, d_gain_moe),
        )
        outs = [out_own[0]] + [a[0] for a in out_came]
        small_steps[last], outs[-1] = together(small_steps[last], outs[-1])
        small_came = []
        for k in reversed(range(plane.steps)):
            send = step_sum(small_steps, small_came, k)
            if k == 0:
                send, que_came = together(send, que_came)
            small_came.append(mix(send, k))
        ques = [que_own[0]] + [a[0] for a in que_came]
        small = [small_own[0]] + [a[0] for a in small_came]
        values = (outs, ques, small)
        send = jnp.concatenate([total([a[1] for a in v]) for v in values], -1)
        mix_send, send = together(mix_send, send)
        arrived = lax.ppermute(send, "dp", swap_copies)
        mix_terms.append((0, mix(mix_send, last)))
        arrived, mix_came, expert_grads = together(arrived, mix_terms[-1][1], expert_grads)
        mix_terms[-1] = (0, mix_came)
        cuts = (slice(None, split), slice(split, width), slice(width, None))
        values = [[a[0] for a in v] + [arrived[..., cut]] for v, cut in zip(values, cuts)]
        send = jnp.concatenate([total([a[1] for a in v]) for v in values], -1)
        arrived = lax.ppermute(send, "context", swap_context)
        for k in reversed(range(last)):
            mix_send, send = together(pick(mix_terms, k), send)
            mix_terms.append((0, mix(mix_send, k)))
        mix_terms[-1] = (0, after(mix_terms[-1][1], send))
    else:
        for k in reversed(range(plane.steps)):
            mix_terms.append((0, mix(mix_send if k == last else pick(mix_terms, k), k)))

    def split_grads(grads):
        return (
            grads[:, :inner].astype(f32)[None],
            grads[:, inner : 2 * inner].astype(f32)[None],
            grads[:, 2 * inner :].astype(f32).T[None],
        )

    keep, other = parts_of(mix_terms, 0), sibling(parts_of(mix_terms, 1))
    mixture = jnp.concatenate([by_core(keep, other), by_core(other, keep)], axis=1)
    output = (hidden + mixture.astype(f32)).astype(bf16)[None]
    grad_gate, grad_up, grad_down = split_grads(expert_grads)
    if custom:
        arrived, output, grad_gate, grad_up, grad_down = together(
            arrived, output, grad_gate, grad_up, grad_down
        )
        values = [[a[0] for a in v] + [arrived[..., cut]] for v, cut in zip(values, cuts)]
        send = jnp.concatenate([total([a[1] for a in v]) for v in values], -1)
        own = jnp.concatenate([sum(a[0].astype(f32) for a in v) for v in values], -1)
        arrived = sibling(send)
        grad_query, grad_out, grad_key, grad_value, extra = finish(
            core_row, own, arrived, split, kv_width
        )
    else:
        in_order = lambda a, b: jnp.concatenate([by_core(a, b), by_core(b, a)], axis=1)
        scatter = lambda v: lax.psum_scatter(
            v.astype(bf16), ("expert", "context", "dp"), scatter_dimension=0, tiled=True
        ).astype(f32)
        grad_query = scatter(dot_tn(xn_one, in_order(dq_mine, dq_theirs)))
        grad_out = scatter(dot_tn(d_low, in_order(att_mine, att_theirs)))
        grad_kv = scatter(dot_tn(xn_one, d_kv))
        grad_key, grad_value = grad_kv[:, :kv_width], grad_kv[:, kv_width:]
        router = dot_tn(xn_two, d_logits)[:, : LANES - 2]
        extra = scatter(
            jnp.concatenate([router, d_gain_attn[:1].T, d_gain_moe[:1].T], axis=1)
        )
    return (
        output,
        d_in[None],
        extra[:, LANES - 2],
        grad_query,
        grad_key,
        grad_value,
        grad_out.T,
        extra[:, LANES - 1],
        extra[:, :experts],
        grad_gate,
        grad_up,
        grad_down,
    )


def solution(mesh):
    in_specs = (
        P("dp", ("expert", "context"), None),
        P(),
        P(),
        P(),
        P(),
        P(),
        P(),
        P(),
        P("expert", None, None),
        P("expert", None, None),
        P("expert", None, None),
        P("dp", ("expert", "context"), None),
        P("dp", ("expert", "context")),
        P("dp", ("expert", "context"), None),
    )
    out_specs = (
        P("dp", ("expert", "context"), None),
        P("dp", ("expert", "context"), None),
        P(("expert", "context", "dp")),
        P(("expert", "context", "dp"), None),
        P(("expert", "context", "dp"), None),
        P(("expert", "context", "dp"), None),
        P(None, ("expert", "context", "dp")),
        P(("expert", "context", "dp")),
        P(("expert", "context", "dp"), None),
        P("expert", ("context", "dp"), None),
        P("expert", ("context", "dp"), None),
        P("expert", None, ("context", "dp")),
    )
    return jax.shard_map(
        per_device, mesh=mesh, in_specs=in_specs, out_specs=out_specs, check_vma=False
    )
```
